32 devices in a mesh: dp: 8 (over z, x), row: 2 (over y), col: 2 (over core).
Axes of the slice: x: 2, y: 2, z: 4, core: 2. Of those that a mesh axis runs over, the one named last changes fastest.
Arguments:
- block_in: float32 [8192, 768], P(('dp', 'row'), 'col'), may hold values from -6 to 6
- upstream: float32 [8192, 768], P(('dp', 'row'), 'col'), may hold values from -6 to 6
- norm_params: float32 [4, 768], P(None, 'col'), may hold values from -0.5 to 1.5
- w_qkv: float32 [3, 12, 64, 768], P(None, 'row', 'dp', 'col'), may hold values from -1.4433757 to 1.4433757
- w_attn: float32 [12, 64, 768], P('row', 'dp', 'col'), may hold values from -0.875 to 0.875
- w_up: float32 [3072, 768], P(('dp', 'row'), 'col'), may hold values from -0.21875 to 0.21875
- w_down: float32 [3072, 768], P(('dp', 'row'), 'col'), may hold values from -0.109375 to 0.109375
- mom_norm: float32 [2, 4, 768], P(None, None, 'col'), may hold values from -0.224 to 0.224, as said below
- mom_qkv: float32 [2, 3, 12, 64, 768], P(None, None, 'row', 'dp', 'col'), may hold values from -0.16 to 0.16, as said below
- mom_attn: float32 [2, 12, 64, 768], P(None, 'row', 'dp', 'col'), may hold values from -0.048 to 0.048, as said below
- mom_up: float32 [2, 3072, 768], P(None, ('dp', 'row'), 'col'), may hold values from -0.128 to 0.128, as said below
- mom_down: float32 [2, 3072, 768], P(None, ('dp', 'row'), 'col'), may hold values from -0.208 to 0.208, as said below
Outputs:
- block_out: float32 [8192, 768], P(('dp', 'row'), 'col')
- input_grad: float32 [8192, 768], P(('dp', 'row'), 'col')
- grad_norm: float32 [4, 768], P(None, 'col')
- grad_qkv: float32 [3, 12, 64, 768], P(None, 'row', 'dp', 'col')
- grad_attn: float32 [12, 64, 768], P('row', 'dp', 'col')
- grad_up: float32 [3072, 768], P(('dp', 'row'), 'col')
- grad_down: float32 [3072, 768], P(('dp', 'row'), 'col')
- new_norm: float32 [4, 768], P(None, 'col')
- new_qkv: float32 [3, 12, 64, 768], P(None, 'row', 'dp', 'col')
- new_attn: float32 [12, 64, 768], P('row', 'dp', 'col')
- new_up: float32 [3072, 768], P(('dp', 'row'), 'col')
- new_down: float32 [3072, 768], P(('dp', 'row'), 'col')
- new_mom_norm: float32 [2, 4, 768], P(None, None, 'col')
- new_mom_qkv: float32 [2, 3, 12, 64, 768], P(None, None, 'row', 'dp', 'col')
- new_mom_attn: float32 [2, 12, 64, 768], P(None, 'row', 'dp', 'col')
- new_mom_up: float32 [2, 3072, 768], P(None, ('dp', 'row'), 'col')
- new_mom_down: float32 [2, 3072, 768], P(None, ('dp', 'row'), 'col')
The draws below stay inside these ranges and needn't reach their ends.
Inputs may be any that keep to these rules, and one draw needn't show every extreme that they name: `mom_norm`: second moments are positive. `mom_qkv`: second moments are positive. `mom_attn`: second moments are positive. `mom_up`: second moments are positive. `mom_down`: second moments are positive.
All inputs are finite; a program needn't handle non-finite values.
Results may differ from the reference program's by a relative error of at most 0.012.
The reference program's roundings to bfloat16 on the way count: a program that leaves them out, or rounds other values in their place, can miss the bound.
Values may be sent and summed in bfloat16 or wider, within the bound.
A program may use at most 128 MiB of HBM per device.

```python
import math
import jax
import jax.numpy as jnp
from jax import lax

D = 768
H = 12
HD = 64
FF = 3072
SEQ = 512
STEP = 4
TOKENS = 8192


def draw_norm_params(key, part):
    gain_rows = jax.random.uniform(jax.random.fold_in(key, 1), (2, D), jnp.float32, 0.7, 1.3)
    shifts = jax.random.uniform(jax.random.fold_in(key, 2), (2, D), jnp.float32, -0.3, 0.3)
    return jnp.stack([gain_rows[0], shifts[0], gain_rows[1], shifts[1]])


def draw_w_qkv(key, part):
    base_draw = jnp.clip(jax.random.normal(jax.random.fold_in(key, 3), (3, H, HD, D), jnp.float32), -5.0, 5.0)
    base_draw = base_draw / math.sqrt(D)
    query_lift = jnp.array([1.5, 1.0, 1.0], jnp.float32)
    drawn_draw = base_draw * query_lift[:, None, None, None]
    return drawn_draw


def moment_pair(key, shape, grad_size):
    log_low = math.log(0.005)
    log_high = math.log(0.05)
    first_moment = grad_size * 0.08 * jnp.clip(jax.random.normal(jax.random.fold_in(key, 21), shape, jnp.float32), -4.0, 4.0)
    second_moment = grad_size * grad_size * jnp.exp(jax.random.uniform(jax.random.fold_in(key, 22), shape, jnp.float32, log_low, log_high))
    return jnp.stack([first_moment, second_moment])


def draw_mom_norm(key, part):
    return moment_pair(key, (4, D), 0.7)


def draw_mom_qkv(key, part):
    return moment_pair(key, (3, H, HD, D), 0.5)


def draw_mom_attn(key, part):
    return moment_pair(key, (H, HD, D), 0.15)


def draw_mom_up(key, part):
    return moment_pair(key, (FF, D), 0.4)


def draw_mom_down(key, part):
    return moment_pair(key, (FF, D), 0.65)


def shard_levels(rng, dims, shards, smallest, high):
    def one(position, blocks):
        heights = jax.random.uniform(jax.random.fold_in(jax.random.fold_in(rng, 6), position), (blocks,), jnp.float32, smallest / len(shards), high / len(shards))
        return jnp.repeat(jnp.exp(heights), dims[position] // blocks).reshape((-1,) + (1,) * (len(dims) - position - 1))

    gain = one(*shards[0])
    for cut in shards[1:]:
        gain = gain * one(*cut)
    return gain


def normal_values(rng, dims, scale, reach, split=(), kind=jnp.bfloat16):
    result = scale * jax.random.normal(rng, dims, jnp.float32)
    if split:
        result = result * shard_levels(rng, dims, split, -0.22, 0.18)
    return jnp.clip(result, -reach, reach).astype(kind)


def setup_inputs(seed: int = 0) -> dict:
    key_of = jax.random.split(jax.random.key(seed), 13)
    block_in = normal_values(key_of[0], (TOKENS, D), 1.0, 6.0, ((0, 16), (1, 2)), jnp.float32)
    upstream = normal_values(key_of[1], (TOKENS, D), 1.0, 6.0, ((0, 16), (1, 2)), jnp.float32)
    norm_params = draw_norm_params(jax.random.fold_in(key_of[12], 71), 0)
    w_qkv = draw_w_qkv(jax.random.fold_in(key_of[12], 71), 0)
    w_attn = normal_values(key_of[4], (H, HD, D), (D // 16) ** -0.5, 0.875, ((0, 2), (1, 8), (2, 2)), jnp.float32)
    w_up = normal_values(key_of[5], (FF, D), D ** -0.5, 0.21875, ((0, 16), (1, 2)), jnp.float32)
    w_down = normal_values(key_of[6], (FF, D), FF ** -0.5, 0.109375, ((0, 16), (1, 2)), jnp.float32)
    mom_norm = draw_mom_norm(jax.random.fold_in(key_of[12], 71), 0)
    mom_qkv = draw_mom_qkv(jax.random.fold_in(key_of[12], 71), 0)
    mom_attn = draw_mom_attn(jax.random.fold_in(key_of[12], 71), 0)
    mom_up = draw_mom_up(jax.random.fold_in(key_of[12], 71), 0)
    mom_down = draw_mom_down(jax.random.fold_in(key_of[12], 71), 0)
    return {"block_in": block_in, "upstream": upstream, "norm_params": norm_params, "w_qkv": w_qkv, "w_attn": w_attn, "w_up": w_up, "w_down": w_down, "mom_norm": mom_norm, "mom_qkv": mom_qkv, "mom_attn": mom_attn, "mom_up": mom_up, "mom_down": mom_down}


norm_eps = 1e-05
adam_eps = 1e-08
beta_one = 0.9
beta_two = 0.95
learn_rate = 0.02
decay_rate = 0.1
gelu_coef = math.sqrt(2.0 / math.pi)
cubic_coef = 0.044715
masked_score = -1e+30

def layer_norm(rows_in, gain_row, shift_row):
    center = rows_in - lax.optimization_barrier(jnp.mean(rows_in, axis=1, keepdims=True))
    spread = lax.optimization_barrier(jnp.mean(center * center, axis=1, keepdims=True))
    inverse = lax.rsqrt(spread + norm_eps)
    normal = center * inverse
    return (normal, inverse, (normal * gain_row + shift_row).astype(jnp.bfloat16))

def norm_back(grad_normed, normal, inverse, gain_row):
    scaled = grad_normed * gain_row
    first_mean = lax.optimization_barrier(jnp.mean(scaled, axis=1, keepdims=True))
    second_mean = lax.optimization_barrier(jnp.mean(scaled * normal, axis=1, keepdims=True))
    return inverse * (scaled - first_mean - normal * second_mean)

def smooth_pair(values):
    squared = values * values
    bent = jnp.tanh(gelu_coef * (values + cubic_coef * squared * values))
    smooth = 0.5 * values * (1.0 + bent)
    slope = 0.5 * (1.0 + bent) + 0.5 * values * (1.0 - bent * bent) * gelu_coef * (1.0 + 3.0 * cubic_coef * squared)
    return (smooth, slope)

def causal_mask(length):
    return lax.broadcasted_iota(jnp.int32, (length, length), 0) >= lax.broadcasted_iota(jnp.int32, (length, length), 1)

def seq_scores(qkv_seq):
    score_scale = 1.0 / math.sqrt(qkv_seq.shape[3])
    q_rows = qkv_seq[:, 0].astype(jnp.float32)
    k_rows = qkv_seq[:, 1].astype(jnp.float32)
    scores = jnp.einsum('qhd,khd->hqk', q_rows, k_rows) * score_scale
    return (jnp.where(causal_mask(qkv_seq.shape[0])[None], scores, masked_score), score_scale)

def attend(qkv_seq):
    scores, score_scale = seq_scores(qkv_seq)
    highest = lax.optimization_barrier(jnp.max(scores, axis=2, keepdims=True))
    log_total = highest + jnp.log(lax.optimization_barrier(jnp.sum(jnp.exp(scores - highest), axis=2, keepdims=True)))
    attn_probs = jnp.exp(scores - log_total).astype(jnp.bfloat16)
    mixed = jnp.einsum('hqk,khd->qhd', attn_probs.astype(jnp.float32), qkv_seq[:, 2].astype(jnp.float32))
    return (mixed.astype(jnp.bfloat16).reshape(qkv_seq.shape[0], -1), log_total)

def attend_back(qkv_seq, grad_mixed, log_total):
    grad_mixed = grad_mixed.reshape(qkv_seq.shape[0], qkv_seq.shape[2], qkv_seq.shape[3]).astype(jnp.float32)
    scores, score_scale = seq_scores(qkv_seq)
    attn_probs = jnp.exp(scores - log_total)
    probs_b = attn_probs.astype(jnp.bfloat16).astype(jnp.float32)
    q_rows = qkv_seq[:, 0].astype(jnp.float32)
    k_rows = qkv_seq[:, 1].astype(jnp.float32)
    v_rows = qkv_seq[:, 2].astype(jnp.float32)
    grad_values = jnp.einsum('hqk,qhd->khd', probs_b, grad_mixed)
    grad_probs = jnp.einsum('qhd,khd->hqk', grad_mixed, v_rows)
    delta_rows = lax.optimization_barrier(jnp.sum(attn_probs * grad_probs, axis=2, keepdims=True))
    grad_scores = (attn_probs * (grad_probs - delta_rows) * score_scale).astype(jnp.bfloat16).astype(jnp.float32)
    grad_queries = jnp.einsum('hqk,khd->qhd', grad_scores, k_rows)
    grad_keys = jnp.einsum('hqk,qhd->khd', grad_scores, q_rows)
    return jnp.stack([grad_queries, grad_keys, grad_values], axis=1).astype(jnp.bfloat16)

def adam_step(weight, grad, moments, decay):
    first_moment = beta_one * moments[0] + (1.0 - beta_one) * grad
    second_moment = beta_two * moments[1] + (1.0 - beta_two) * grad * grad
    step_size = first_moment / (1.0 - beta_one ** STEP) / (jnp.sqrt(second_moment / (1.0 - beta_two ** STEP)) + adam_eps)
    return (weight - learn_rate * (step_size + decay * weight), jnp.stack([first_moment, second_moment]))

def reference(block_in, upstream, norm_params, w_qkv, w_attn, w_up, w_down, mom_norm, mom_qkv, mom_attn, mom_up, mom_down):
    qkv_mat = w_qkv.reshape(3 * D, D).astype(jnp.bfloat16)
    attn_mat = w_attn.reshape(D, D).astype(jnp.bfloat16)
    up_mat = w_up.astype(jnp.bfloat16)
    down_mat = w_down.astype(jnp.bfloat16)
    seq_total = TOKENS // SEQ
    per_block = math.gcd(seq_total, 8)
    block_rows = per_block * SEQ

    def one_block(carry, block_index):
        first_row = (block_index * block_rows).astype(jnp.int32)
        rows_in = lax.dynamic_slice_in_dim(block_in, first_row, block_rows, 0)
        rows_up = lax.dynamic_slice_in_dim(upstream, first_row, block_rows, 0)
        normal_one, inverse_one, normed_one = layer_norm(rows_in, norm_params[0], norm_params[1])
        triples = jnp.dot(normed_one, qkv_mat.T, preferred_element_type=jnp.float32).astype(jnp.bfloat16)
        triples = triples.reshape(per_block, SEQ, 3, H, HD)
        mixed, log_total = jax.vmap(attend)(triples)
        mixed_rows = mixed.reshape(block_rows, D)
        middle = rows_in + jnp.dot(mixed_rows, attn_mat, preferred_element_type=jnp.float32)
        normal_two, inverse_two, normed_two = layer_norm(middle, norm_params[2], norm_params[3])
        hidden_pre = jnp.dot(normed_two, up_mat.T, preferred_element_type=jnp.float32)
        activated, slope = smooth_pair(hidden_pre)
        activated = activated.astype(jnp.bfloat16)
        block_out = middle + jnp.dot(activated, down_mat, preferred_element_type=jnp.float32)
        upstream_b = rows_up.astype(jnp.bfloat16)
        grad_hidden = jnp.dot(upstream_b, down_mat.T, preferred_element_type=jnp.float32)
        grad_pre = (grad_hidden * slope).astype(jnp.bfloat16)
        grad_normed_two = jnp.dot(grad_pre, up_mat, preferred_element_type=jnp.float32)
        middle_grad = rows_up + norm_back(grad_normed_two, normal_two, inverse_two, norm_params[2])
        middle_b = middle_grad.astype(jnp.bfloat16)
        grad_mixed = jnp.dot(middle_b, attn_mat.T, preferred_element_type=jnp.float32).astype(jnp.bfloat16)
        grad_mixed = grad_mixed.reshape(per_block, SEQ, D)
        grad_triples = jax.vmap(attend_back)(triples, grad_mixed, log_total).reshape(block_rows, 3 * D)
        grad_normed_one = jnp.dot(grad_triples, qkv_mat, preferred_element_type=jnp.float32)
        input_grad = middle_grad + norm_back(grad_normed_one, normal_one, inverse_one, norm_params[0])
        norm_terms = jnp.stack([lax.optimization_barrier(jnp.sum(grad_normed_one * normal_one, axis=0)), lax.optimization_barrier(jnp.sum(grad_normed_one, axis=0)), lax.optimization_barrier(jnp.sum(grad_normed_two * normal_two, axis=0)), lax.optimization_barrier(jnp.sum(grad_normed_two, axis=0))])
        totals = (carry[0] + jnp.dot(grad_triples.T, normed_one, preferred_element_type=jnp.float32), carry[1] + jnp.dot(mixed_rows.T, middle_b, preferred_element_type=jnp.float32), carry[2] + jnp.dot(grad_pre.T, normed_two, preferred_element_type=jnp.float32), carry[3] + jnp.dot(activated.T, upstream_b, preferred_element_type=jnp.float32), carry[4] + norm_terms)
        return (totals, (block_out, input_grad))
    start_totals = (jnp.zeros((3 * D, D), jnp.float32), jnp.zeros((D, D), jnp.float32), jnp.zeros((FF, D), jnp.float32), jnp.zeros((FF, D), jnp.float32), jnp.zeros((4, D), jnp.float32))
    totals, (outs_all, grads_all) = lax.scan(one_block, start_totals, jnp.arange(seq_total // per_block, dtype=jnp.int32))
    factor = 1.0 / math.sqrt(TOKENS)
    grad_qkv = (totals[0] * factor).reshape(3, H, HD, D)
    grad_attn = (totals[1] * factor).reshape(H, HD, D)
    grad_up = totals[2] * factor
    grad_down = totals[3] * factor
    grad_norm = totals[4] * factor
    new_norm, new_mom_norm = adam_step(norm_params, grad_norm, mom_norm, 0.0)
    new_qkv, new_mom_qkv = adam_step(w_qkv, grad_qkv, mom_qkv, decay_rate)
    new_attn, new_mom_attn = adam_step(w_attn, grad_attn, mom_attn, decay_rate)
    new_up, new_mom_up = adam_step(w_up, grad_up, mom_up, decay_rate)
    new_down, new_mom_down = adam_step(w_down, grad_down, mom_down, decay_rate)
    block_out = outs_all.reshape(TOKENS, D)
    input_grad = grads_all.reshape(TOKENS, D)
    return (block_out, input_grad, grad_norm, grad_qkv, grad_attn, grad_up, grad_down, new_norm, new_qkv, new_attn, new_up, new_down, new_mom_norm, new_mom_qkv, new_mom_attn, new_mom_up, new_mom_down)
```

```python
import functools
import math

import jax
import jax.numpy as jnp
from jax import lax
from jax.experimental import pallas as pl
from jax.experimental.pallas import tpu as pltpu
from jax.sharding import PartitionSpec as P

SEQ = 512
STEP = 4
LOW = 2


norm_eps = 1e-05
adam_eps = 1e-08
beta_one = 0.9
beta_two = 0.95
learn_rate = 0.02
decay_rate = 0.1
gelu_coef = math.sqrt(2.0 / math.pi)
cubic_coef = 0.044715
masked_score = -1e30

group = ("row", "col")
swap_pair = [(0, 1), (1, 0)]
spread_first = [(1, 2), (2, 1)]
spread_second = [(0, 2), (3, 1), (1, 0), (2, 3)]
collect_second = [(dst, src) for src, dst in spread_second]


def smooth_pair(values):
    squared = values * values
    bent = jnp.tanh(gelu_coef * (values + cubic_coef * squared * values))
    smooth = 0.5 * values * (1.0 + bent)
    slope = 0.5 * (1.0 + bent) + 0.5 * values * (1.0 - bent * bent) * gelu_coef * (
        1.0 + 3.0 * cubic_coef * squared
    )
    return (smooth, slope)


def wide(left, right, dims):
    return lax.dot_general(left, right, (dims, ((), ())), preferred_element_type=jnp.float32)


def normalize(rows_in, gain_row, shift_row):
    count = rows_in.shape[1]
    mean_here = jnp.mean(rows_in, axis=1, keepdims=True)
    offset = rows_in - mean_here
    square_here = jnp.sum(offset * offset, axis=1, keepdims=True)
    there = lax.ppermute(jnp.concatenate([mean_here, square_here], axis=1), "col", swap_pair)
    gap = mean_here - there[:, :1]
    spread = (square_here + there[:, 1:] + gap * gap * (0.5 * count)) / (2.0 * count)
    inverse = lax.rsqrt(spread + norm_eps)
    normal = (rows_in - (mean_here - 0.5 * gap)) * inverse
    return (normal, inverse, (normal * gain_row + shift_row).astype(jnp.bfloat16))


def norm_back(grad_normed, normal, inverse, gain_row):
    count = 2.0 * grad_normed.shape[1]
    scaled = grad_normed * gain_row
    here = jnp.concatenate(
        [
            jnp.sum(scaled, axis=1, keepdims=True),
            jnp.sum(scaled * normal, axis=1, keepdims=True),
        ],
        axis=1,
    )
    total = (here + lax.ppermute(here, "col", swap_pair)) / count
    return inverse * (scaled - total[:, :1] - normal * total[:, 1:])


def pick(flag, one, other):
    return jnp.where(flag, one, other), jnp.where(flag, other, one)


def spread_rows(block):
    row, col = lax.axis_index("row"), lax.axis_index("col")
    first = lax.ppermute(block, group, spread_first)
    second = lax.ppermute(block, group, spread_second)
    first = jnp.where(row == col, block, first)
    low, high = pick(row == 0, first, second)
    return low, high


def collect_rows(low, high):
    row, col = lax.axis_index("row"), lax.axis_index("col")
    first, second = pick(row == 0, low, high)
    first_in = lax.ppermute(first.astype(jnp.bfloat16), group, spread_first)
    second_in = lax.ppermute(second.astype(jnp.bfloat16), group, collect_second)
    return jnp.where(row == col, first, first_in.astype(jnp.float32)) + second_in.astype(
        jnp.float32
    )


def out_project(rows, weight):
    half = weight.shape[1] // 2
    return collect_rows(
        wide(rows, weight[:, :half], ((1,), (0,))), wide(rows, weight[:, half:], ((1,), (0,)))
    )


def small_ring():
    size = lax.axis_size("dp")
    return size % LOW == 0 and size <= 8


def high_steps(sign):
    size = lax.axis_size("dp")
    high = size // LOW
    return [
        [(i, ((i // LOW + sign * step) % high) * LOW + i % LOW) for i in range(size)]
        for step in range(1, high)
    ]


def low_step():
    return [(i, i ^ 1) for i in range(lax.axis_size("dp"))]


def gather_weight(shard, axis):
    shard = shard.astype(jnp.bfloat16)
    if small_ring():
        near = jnp.concatenate(
            [shard] + [lax.ppermute(shard, "dp", perm) for perm in high_steps(1)], axis=axis
        )
        block = jnp.concatenate([near, lax.ppermute(near, "dp", low_step())], axis=axis)
    else:
        block = lax.all_gather(shard, "dp", axis=axis, tiled=True)
    there = lax.ppermute(block, "col", swap_pair)
    low, high = pick(lax.axis_index("col") == 0, block, there)
    return jnp.concatenate([low, high], axis=-1)


def reduce_weight(make, axis):
    away = make(False).astype(jnp.bfloat16)
    total = make(True) + lax.ppermute(away, "col", swap_pair).astype(jnp.float32)
    if not small_ring():
        return lax.psum_scatter(total, "dp", scatter_dimension=axis, tiled=True)
    near, far = jnp.split(total, 2, axis=axis)
    near = near + lax.ppermute(far.astype(jnp.bfloat16), "dp", low_step()).astype(jnp.float32)
    own, *rest = jnp.split(near, lax.axis_size("dp") // LOW, axis=axis)
    for piece, perm in zip(rest, high_steps(-1)):
        own = own + lax.ppermute(piece.astype(jnp.bfloat16), "dp", perm).astype(jnp.float32)
    return own


def sum_everywhere(terms):
    if not small_ring():
        return lax.psum(terms, ("dp", "row"))
    terms = terms + lax.ppermute(terms, "row", swap_pair)
    terms = terms + lax.ppermute(terms, "dp", low_step())
    moved = [lax.ppermute(terms, "dp", perm) for perm in high_steps(1)]
    for piece in moved:
        terms = terms + piece
    return terms


def head_scores(triples_ref, heads, size, head):
    width = heads * size
    query = triples_ref[:, head * size : (head + 1) * size]
    key = triples_ref[:, width + head * size : width + (head + 1) * size]
    value = triples_ref[:, 2 * width + head * size : 2 * width + (head + 1) * size]
    scores = wide(query, key, ((1,), (1,))) * (1.0 / math.sqrt(size))
    length = scores.shape[0]
    allowed = lax.broadcasted_iota(jnp.int32, (length, length), 0) >= lax.broadcasted_iota(
        jnp.int32, (length, length), 1
    )
    return query, key, value, jnp.where(allowed, scores, masked_score)


def attend_kernel(heads, size, triples_ref, mixed_ref, total_ref):
    for head in range(heads):
        _, _, value, scores = head_scores(triples_ref, heads, size, head)
        highest = jnp.max(scores, axis=1, keepdims=True)
        log_total = highest + jnp.log(jnp.sum(jnp.exp(scores - highest), axis=1, keepdims=True))
        probs = jnp.exp(scores - log_total).astype(jnp.bfloat16)
        mixed_ref[:, head * size : (head + 1) * size] = wide(probs, value, ((1,), (0,))).astype(
            jnp.bfloat16
        )
        total_ref[:, head : head + 1] = log_total


def attend_back_kernel(heads, size, triples_ref, grad_ref, total_ref, out_ref):
    width = heads * size
    scale = 1.0 / math.sqrt(size)
    for head in range(heads):
        query, key, value, scores = head_scores(triples_ref, heads, size, head)
        grad_mixed = grad_ref[:, head * size : (head + 1) * size]
        probs = jnp.exp(scores - total_ref[:, head : head + 1])
        grad_values = wide(probs.astype(jnp.bfloat16), grad_mixed, ((0,), (0,)))
        grad_probs = wide(grad_mixed, value, ((1,), (1,)))
        delta = jnp.sum(probs * grad_probs, axis=1, keepdims=True)
        grad_scores = (probs * (grad_probs - delta) * scale).astype(jnp.bfloat16)
        for part, piece in enumerate(
            (
                wide(grad_scores, key, ((1,), (0,))),
                wide(grad_scores, query, ((0,), (0,))),
                grad_values,
            )
        ):
            start = part * width + head * size
            out_ref[:, start : start + size] = piece.astype(jnp.bfloat16)


def by_sequence(kernel, operands, outs):
    rows = operands[0].shape[0]

    def spec(shape):
        return pl.BlockSpec((SEQ, shape[1]), lambda step: (step, 0))

    return pl.pallas_call(
        kernel,
        grid=(rows // SEQ,),
        in_specs=[spec(item.shape) for item in operands],
        out_specs=[spec(item.shape) for item in outs],
        out_shape=outs,
        compiler_params=pltpu.CompilerParams(vmem_limit_bytes=40 * 1024 * 1024),
        cost_estimate=pl.CostEstimate(
            flops=rows * SEQ * 2048, bytes_accessed=rows * 8192, transcendentals=rows * SEQ * 6
        ),
    )(*operands)


def adam_step(weight, grad, moments, decay):
    first_moment = beta_one * moments[0] + (1.0 - beta_one) * grad
    second_moment = beta_two * moments[1] + (1.0 - beta_two) * grad * grad
    step_size = (
        first_moment
        / (1.0 - beta_one**STEP)
        / (jnp.sqrt(second_moment / (1.0 - beta_two**STEP)) + adam_eps)
    )
    return (
        weight - learn_rate * (step_size + decay * weight),
        jnp.stack([first_moment, second_moment]),
    )


def on_device(
    block_in,
    upstream,
    norm_params,
    w_qkv,
    w_attn,
    w_up,
    w_down,
    mom_norm,
    mom_qkv,
    mom_attn,
    mom_up,
    mom_down,
):
    heads = w_qkv.shape[1]
    size = w_qkv.shape[2] * lax.axis_size("dp")
    width = heads * size
    at_low = lax.axis_index("col") == 0

    normal_one, inverse_one, normed_one = normalize(block_in, norm_params[0], norm_params[1])
    qkv_mat = gather_weight(w_qkv, 2).reshape(3 * width, -1)
    one_low, one_high = spread_rows(normed_one)
    attn_mat = gather_weight(w_attn, 1).reshape(width, -1)
    up_mat = gather_weight(w_up, 0)
    up_low, up_high = spread_rows(upstream.astype(jnp.bfloat16))
    down_mat = gather_weight(w_down, 0)

    triples = wide(
        jnp.concatenate([one_low, one_high], axis=1), qkv_mat, ((1,), (1,))
    ).astype(jnp.bfloat16)
    mixed, log_total = by_sequence(
        functools.partial(attend_kernel, heads, size),
        (triples,),
        (
            jax.ShapeDtypeStruct((triples.shape[0], width), jnp.bfloat16),
            jax.ShapeDtypeStruct((triples.shape[0], heads), jnp.float32),
        ),
    )
    middle = block_in + out_project(mixed, attn_mat)
    normal_two, inverse_two, normed_two = normalize(middle, norm_params[2], norm_params[3])
    two_low, two_high = spread_rows(normed_two)
    grad_hidden = wide(jnp.concatenate([up_low, up_high], axis=1), down_mat, ((1,), (1,)))
    hidden_pre = wide(jnp.concatenate([two_low, two_high], axis=1), up_mat, ((1,), (1,)))
    activated, slope = smooth_pair(hidden_pre)
    activated = activated.astype(jnp.bfloat16)
    grad_pre = (grad_hidden * slope).astype(jnp.bfloat16)
    grad_normed_two = out_project(grad_pre, up_mat)
    block_out = middle + out_project(activated, down_mat)

    def products(left, low, high):
        own, away = pick(at_low, low, high)
        return lambda mine: wide(left, own if mine else away, ((0,), (0,)))

    grad_down = reduce_weight(products(activated, up_low, up_high), 0)
    grad_up = reduce_weight(products(grad_pre, two_low, two_high), 0)
    middle_grad = upstream + norm_back(grad_normed_two, normal_two, inverse_two, norm_params[2])
    mid_low, mid_high = spread_rows(middle_grad.astype(jnp.bfloat16))
    grad_mixed = wide(
        jnp.concatenate([mid_low, mid_high], axis=1), attn_mat, ((1,), (1,))
    ).astype(jnp.bfloat16)

    def by_head(make, parts):
        return lambda mine: make(mine).reshape(*parts, heads, size, -1)

    grad_attn = reduce_weight(by_head(products(mixed, mid_low, mid_high), ()), 1)
    (grad_triples,) = by_sequence(
        functools.partial(attend_back_kernel, heads, size),
        (triples, grad_mixed, log_total),
        (jax.ShapeDtypeStruct(triples.shape, jnp.bfloat16),),
    )
    grad_qkv = reduce_weight(by_head(products(grad_triples, one_low, one_high), (3,)), 2)
    grad_normed_one = out_project(grad_triples, qkv_mat)
    input_grad = middle_grad + norm_back(grad_normed_one, normal_one, inverse_one, norm_params[0])
    norm_terms = jnp.stack(
        [
            jnp.sum(grad_normed_one * normal_one, axis=0),
            jnp.sum(grad_normed_one, axis=0),
            jnp.sum(grad_normed_two * normal_two, axis=0),
            jnp.sum(grad_normed_two, axis=0),
        ]
    )
    grad_norm = sum_everywhere(norm_terms)
    token_count = block_in.shape[0] * lax.axis_size("dp") * lax.axis_size("row")
    factor = 1.0 / math.sqrt(token_count)
    grad_norm = grad_norm * factor
    grad_qkv = grad_qkv * factor
    grad_attn = grad_attn * factor
    grad_up = grad_up * factor
    grad_down = grad_down * factor
    new_norm, new_mom_norm = adam_step(norm_params, grad_norm, mom_norm, 0.0)
    new_qkv, new_mom_qkv = adam_step(w_qkv, grad_qkv, mom_qkv, decay_rate)
    new_attn, new_mom_attn = adam_step(w_attn, grad_attn, mom_attn, decay_rate)
    new_up, new_mom_up = adam_step(w_up, grad_up, mom_up, decay_rate)
    new_down, new_mom_down = adam_step(w_down, grad_down, mom_down, decay_rate)
    return (
        block_out,
        input_grad,
        grad_norm,
        grad_qkv,
        grad_attn,
        grad_up,
        grad_down,
        new_norm,
        new_qkv,
        new_attn,
        new_up,
        new_down,
        new_mom_norm,
        new_mom_qkv,
        new_mom_attn,
        new_mom_up,
        new_mom_down,
    )


MESH = pl.DeviceIdType.MESH
VMEM_BYTES = 67043328
HIDDEN_TILE = 256


def causal(rows, cols, first):
    return (
        lax.broadcasted_iota(jnp.int32, (rows, cols), 0) + first
        >= lax.broadcasted_iota(jnp.int32, (rows, cols), 1)
    )


def head_masks(per, width):
    lane = lax.broadcasted_iota(jnp.int32, (1, width), 1)
    return [
        jnp.where((lane // per) % 2 == part, 1.0, 0.0).astype(jnp.bfloat16) for part in range(2)
    ]


def row_stats(first, second, width=128):
    lane = lax.broadcasted_iota(jnp.int32, (first.shape[0], width), 1)
    return jnp.where(lane == 0, first, second)


def step_kernel(
    nz,
    low,
    factor,
    block_ref,
    up_ref,
    norm_ref,
    wqkv_ref,
    wattn_ref,
    wup_ref,
    wdown_ref,
    out_ref,
    back_ref,
    sum_a_ref,
    sum_u_ref,
    sum_d_ref,
    norm_sum_ref,
    shard_a,
    shard_u,
    shard_d,
    wa,
    wu,
    wd,
    stat_s,
    stat_r,
    spread_s,
    full,
    col_s,
    col_r,
    keep,
    tmp,
    trip,
    mixed,
    lse,
    act,
    gpre,
    middle,
    normal_one,
    normal_two,
    inverse,
    gmix,
    gtrip,
    mgrad,
    ga,
    gu,
    gd,
    gsa,
    gsu,
    gsd,
    gra,
    gru,
    grd,
    xra,
    xru,
    xrd,
    zra,
    zru,
    zrd,
    ns,
    nr,
    send,
    recv,
    local,
):
    dp, r, c = lax.axis_index("dp"), lax.axis_index("row"), lax.axis_index("col")
    z, x = dp // low, dp % low
    same = r == c
    tokens, half = block_ref.shape
    per = wqkv_ref.shape[2]
    pairs = wqkv_ref.shape[1] // 2
    width = 2 * per * nz * low
    groups = wa.shape[0]
    ndp = nz * low
    hidden_rows = wup_ref.shape[0]
    hidden = hidden_rows * ndp
    tiles = hidden // HIDDEN_TILE
    qkv_groups = 3 * pairs

    STAT, SPR = 0, 4
    COL = SPR + 8
    GZ = COL + 8
    GX = GZ + 3 * nz
    GC = GX + 3 * nz
    RC = GC + 3 * ndp
    RX = RC + 3 * tiles
    RZ = RX + 3 * nz
    NS = RZ + 3 * nz

    def at_z(zz):
        return {"dp": zz * low + x}

    x_peer = {"dp": z * low + 1 - x}
    partner = {"col": 1 - c}

    def far(other):
        return {"row": 1 - r, "col": other}

    def feat(f):
        return pl.ds(pl.multiple_of(f * half, half), half)

    mine, other = feat(c), feat(1 - c)
    pending = []

    def describe(src, dst, s, q, where):
        return pltpu.make_async_remote_copy(
            src_ref=src,
            dst_ref=dst,
            send_sem=send.at[s],
            recv_sem=recv.at[q],
            device_id=where,
            device_id_type=MESH,
        )

    def push(src, dst, s, q, where):
        copy = describe(src, dst, s, q, where)
        copy.start()
        return copy

    def arrived(dst, q):
        describe(dst, dst, q, q, partner).wait_recv()

    weights = (wa, wu, wd)

    def slot(p, owner, f):
        if p == 0:
            return wa.at[:, owner, :, feat(f)]
        rows = pl.ds(pl.multiple_of(owner * hidden_rows, hidden_rows), hidden_rows)
        return weights[p].at[rows, feat(f)]

    shards = (shard_a, shard_u, shard_d)

    shard_a[0:qkv_groups] = (
        wqkv_ref[...].reshape(qkv_groups, 2 * per, half).astype(jnp.bfloat16)
    )
    shard_a[qkv_groups:groups] = (
        wattn_ref[...].reshape(pairs, 2 * per, half).astype(jnp.bfloat16)
    )
    shard_u[...] = wup_ref[...].astype(jnp.bfloat16)
    shard_d[...] = wdown_ref[...].astype(jnp.bfloat16)

    def local_stats(rows_in, k):
        mean_here = jnp.mean(rows_in, axis=1, keepdims=True)
        offset = rows_in - mean_here
        square_here = jnp.sum(offset * offset, axis=1, keepdims=True)
        stat_s[k] = row_stats(mean_here, square_here)

    def swap_stats(k):
        pending.append(push(stat_s.at[k], stat_r.at[k], STAT + k, STAT + k, partner))

    def finish_norm(rows_in, k, gain, shift, normal_ref, inverse_index, out):
        arrived(stat_r.at[k], STAT + k)
        here, there = stat_s[k], stat_r[k]
        mean_here, square_here = here[:, 0:1], here[:, 1:2]
        gap = mean_here - there[:, 0:1]
        spread = (square_here + there[:, 1:2] + gap * gap * (0.5 * half)) / (2.0 * half)
        inv = lax.rsqrt(spread + norm_eps)
        normal = (rows_in - (mean_here - 0.5 * gap)) * inv
        normal_ref[...] = normal
        inverse[inverse_index] = inv
        out[...] = (normal * gain + shift).astype(jnp.bfloat16)

    def back_stats(grad, normal, gain, k):
        scaled = grad * gain
        stat_s[k] = row_stats(
            jnp.sum(scaled, axis=1, keepdims=True),
            jnp.sum(scaled * normal, axis=1, keepdims=True),
        )

    def finish_back(grad, normal, inv, gain, k):
        arrived(stat_r.at[k], STAT + k)
        total = (stat_s[k] + stat_r[k]) / (2.0 * half)
        return inv * (grad * gain - total[:, 0:1] - normal * total[:, 1:2])

    def spread_start(k):
        src = spread_s.at[k]
        dst = full.at[k, :, mine]
        pending.append(push(src, dst, SPR + 2 * k, SPR + 2 * k + c, far(r)))

        @pl.when(same)
        def _():
            pltpu.make_async_copy(src, dst, local.at[3 + k]).start()

        @pl.when(jnp.logical_not(same))
        def _():
            push(src, dst, SPR + 2 * k + 1, SPR + 2 * k + c, partner)

    def spread_wait(k):
        src = spread_s.at[k]
        arrived(full.at[k, :, other], SPR + 2 * k + 1 - c)

        @pl.when(same)
        def _():
            pltpu.make_async_copy(src, full.at[k, :, mine], local.at[3 + k]).wait()

        @pl.when(jnp.logical_not(same))
        def _():
            arrived(full.at[k, :, mine], SPR + 2 * k + c)
            describe(src, full.at[k, :, mine], SPR + 2 * k + 1, SPR + 2 * k + c, partner).wait_send()

    def collect_start(k):
        col_s[k, 0] = tmp[:, other].astype(jnp.bfloat16)
        col_s[k, 1] = tmp[:, mine].astype(jnp.bfloat16)

        @pl.when(same)
        def _():
            keep[k % 2] = tmp[:, mine]
            push(col_s.at[k, 0], col_r.at[k, 0], COL + 2 * k, COL + 2 * k, partner)

        @pl.when(jnp.logical_not(same))
        def _():
            push(col_s.at[k, 0], col_r.at[k, 1], COL + 2 * k, COL + 2 * k + 1, far(1 - c))
            push(col_s.at[k, 1], col_r.at[k, 1], COL + 2 * k + 1, COL + 2 * k + 1, far(c))

    def collect_wait(k):
        arrived(col_r.at[k, 1], COL + 2 * k + 1)

        @pl.when(same)
        def _():
            describe(col_s.at[k, 0], col_r.at[k, 0], COL + 2 * k, COL + 2 * k, partner).wait_send()

        @pl.when(jnp.logical_not(same))
        def _():
            arrived(col_r.at[k, 0], COL + 2 * k)
            keep[k % 2] = col_r[k, 0].astype(jnp.float32)
            for part in range(2):
                describe(
                    col_s.at[k, part], col_r.at[k, 1], COL + 2 * k + part, COL + 2 * k + 1, partner
                ).wait_send()

        return keep[k % 2] + col_r[k, 1].astype(jnp.float32)

    def gather_own_z(p):
        for step in range(1, nz):
            pending.append(
                push(
                    shards[p],
                    slot(p, dp, c),
                    GZ + p * nz + step,
                    GZ + p * nz + z,
                    at_z((z + step) % nz),
                )
            )

    def gather_own_x(p):
        pending.append(
            push(shards[p], slot(p, dp, c), GX + p * nz + z, GX + p * nz + z, x_peer)
        )

    def to_partner(p, owner):
        pending.append(
            push(
                slot(p, owner, c),
                slot(p, owner, c),
                GC + p * ndp + owner,
                GC + p * ndp + owner,
                partner,
            )
        )

    def gather_own_c(p):
        pltpu.make_async_copy(shards[p], slot(p, dp, c), local.at[p]).start()
        pending.append(
            push(shards[p], slot(p, dp, c), GC + p * ndp + dp, GC + p * ndp + dp, partner)
        )

    def gather_z(p):
        for step in range(1, nz):
            zz = (z + step) % nz
            owner = zz * low + x
            arrived(slot(p, owner, c), GZ + p * nz + zz)
            pending.append(
                push(
                    slot(p, owner, c), slot(p, owner, c), GX + p * nz + zz, GX + p * nz + zz, x_peer
                )
            )
            to_partner(p, owner)

    def gather_x(p):
        for step in range(nz):
            zz = (z + step) % nz
            owner = zz * low + 1 - x
            arrived(slot(p, owner, c), GX + p * nz + zz)
            to_partner(p, owner)

    def gather_c(p):
        pltpu.make_async_copy(shards[p], slot(p, dp, c), local.at[p]).wait()
        for owner in range(ndp):
            arrived(slot(p, owner, 1 - c), GC + p * ndp + owner)

    sums = (ga, gu, gd)
    away = (gsa, gsu, gsd)
    near = (gra, gru, grd)
    from_x = (xra, xru, xrd)
    from_z = (zra, zru, zrd)

    def index(p, owner):
        if p == 0:
            return (slice(None), owner)
        return (pl.ds(pl.multiple_of(owner * hidden_rows, hidden_rows), hidden_rows),)

    def rows_of(p, i):
        if p == 0:
            return pl.ds(i * pairs, pairs)
        return pl.ds(pl.multiple_of(i * HIDDEN_TILE, HIDDEN_TILE), HIDDEN_TILE)

    def chunk_count(p):
        return groups // pairs if p == 0 else tiles

    def swap_chunk(p, i):
        rows = rows_of(p, i)
        return describe(
            away[p].at[rows], near[p].at[rows], RC + p * tiles + i, RC + p * tiles + i, partner
        )

    def product(p, i, left, right):
        tmp_rows = left.shape[1]
        tmp[0:tmp_rows] = wide(left, right, ((0,), (0,)))
        rows = rows_of(p, i)
        own, gone = tmp[0:tmp_rows, mine], tmp[0:tmp_rows, other].astype(jnp.bfloat16)
        if p == 0:
            own = own.reshape(pairs, ndp, 2 * per, half)
            gone = gone.reshape(pairs, ndp, 2 * per, half)
        sums[p][rows] = own
        away[p][rows] = gone
        swap_chunk(p, i).start()

    def reduce_x(p):
        @pl.loop(0, chunk_count(p))
        def _(i):
            swap_chunk(p, i).wait()

        for step in list(range(1, nz)) + [0]:
            zz = (z + step) % nz
            at = index(p, zz * low + 1 - x)
            total = sums[p][at] + near[p][at].astype(jnp.float32)
            away[p][at] = total.astype(jnp.bfloat16)
            pending.append(
                push(
                    away[p].at[at],
                    from_x[p].at[zz],
                    RX + p * nz + step,
                    RX + p * nz + zz,
                    x_peer,
                )
            )

    def reduce_z(p):
        for step in list(range(1, nz)) + [0]:
            zz = (z + step) % nz
            at = index(p, zz * low + x)
            arrived(from_x[p].at[zz], RX + p * nz + zz)
            total = (
                sums[p][at] + near[p][at].astype(jnp.float32) + from_x[p][zz].astype(jnp.float32)
            )
            if step == 0:
                sums[p][at] = total
                continue
            away[p][at] = total.astype(jnp.bfloat16)
            pending.append(
                push(
                    away[p].at[at],
                    from_z[p].at[z],
                    RZ + p * nz + step,
                    RZ + p * nz + z,
                    at_z(zz),
                )
            )

    def reduce_end(p, result):
        total = sums[p][index(p, dp)]
        for step in range(1, nz):
            zz = (z + step) % nz
            arrived(from_z[p].at[zz], RZ + p * nz + zz)
            total = total + from_z[p][zz].astype(jnp.float32)
        result[...] = total * factor

    gain_one, shift_one = norm_ref[0:1], norm_ref[1:2]
    gain_two, shift_two = norm_ref[2:3], norm_ref[3:4]

    barrier = pltpu.get_barrier_semaphore()
    peers = [at_z((z + step) % nz) for step in range(1, nz)] + [
        x_peer,
        partner,
        far(c),
        far(1 - c),
    ]
    for peer in peers:
        pl.semaphore_signal(barrier, inc=1, device_id=peer, device_id_type=MESH)
    local_stats(block_ref[...], 0)
    pl.semaphore_wait(barrier, len(peers))

    gather_own_z(0)
    gather_own_x(0)
    swap_stats(0)
    gather_own_c(0)
    gather_own_z(1)
    gather_own_z(2)
    finish_norm(block_ref[...], 0, gain_one, shift_one, normal_one, 0, spread_s.at[0])
    spread_start(0)
    spread_s[1] = up_ref[...].astype(jnp.bfloat16)
    spread_start(1)
    gather_z(0)
    gather_own_x(1)
    gather_own_c(1)
    gather_x(0)
    gather_c(0)
    spread_wait(0)

    trip[...] = wide(
        full[0], wa[0:qkv_groups].reshape(qkv_groups * width, 2 * half), ((1,), (1,))
    ).astype(jnp.bfloat16)

    scale = 1.0 / math.sqrt(width // 2)
    block = tokens // 2
    masks = head_masks(per, width)

    def part_of(ref, part, hp):
        return ref[:, pl.ds(pl.multiple_of((part * pairs + hp) * width, width), width)]

    @pl.loop(0, pairs)
    def _(hp):
        query, key, value = (part_of(trip, part, hp) for part in range(3))
        rows = [None, None]
        for head in range(2):
            query_m, value_m = query * masks[head], value * masks[head]
            for b in range(2):
                n = (b + 1) * block
                scores = wide(query_m[b * block : n], key[:n], ((1,), (1,))) * scale
                scores = jnp.where(causal(block, n, b * block), scores, masked_score)
                highest = jnp.max(scores, axis=1, keepdims=True)
                raised = jnp.exp(scores - highest)
                total = jnp.sum(raised, axis=1, keepdims=True)
                lse[hp * 2 + head, b * block : n] = highest + jnp.log(total)
                probs = (raised * (1.0 / total)).astype(jnp.bfloat16)
                got = wide(probs, value_m[:n], ((1,), (0,)))
                rows[b] = got if rows[b] is None else rows[b] + got
        for b in range(2):
            mixed[b * block : (b + 1) * block, pl.ds(pl.multiple_of(hp * width, width), width)] = (
                rows[b].astype(jnp.bfloat16)
            )

    def attn_weight():
        return wa[qkv_groups:groups].reshape(pairs * width, 2 * half)

    tmp[...] = wide(mixed[...], attn_weight(), ((1,), (0,)))
    collect_start(0)
    gather_z(1)
    gather_own_x(2)
    gather_own_c(2)
    middle[...] = block_ref[...] + collect_wait(0)
    local_stats(middle[...], 1)
    swap_stats(1)
    finish_norm(middle[...], 1, gain_two, shift_two, normal_two, 1, spread_s.at[2])
    spread_start(2)
    gather_x(1)
    gather_z(2)
    gather_x(2)
    gather_c(1)
    gather_c(2)
    spread_wait(1)
    spread_wait(2)

    def tile(i):
        return pl.ds(pl.multiple_of(i * HIDDEN_TILE, HIDDEN_TILE), HIDDEN_TILE)

    @pl.loop(0, tiles)
    def _(i):
        pre = wide(full[2], wu[tile(i)], ((1,), (1,)))
        grad = wide(full[1], wd[tile(i)], ((1,), (1,)))
        smooth, slope = smooth_pair(pre)
        act[:, tile(i)] = smooth.astype(jnp.bfloat16)
        gpre[:, tile(i)] = (grad * slope).astype(jnp.bfloat16)

    tmp[...] = wide(gpre[...], wu[...], ((1,), (0,)))
    collect_start(1)
    tmp[...] = wide(act[...], wd[...], ((1,), (0,)))
    collect_start(2)

    @pl.loop(0, tiles)
    def _(i):
        product(2, i, act[:, tile(i)], full[1])

    @pl.loop(0, tiles)
    def _(i):
        product(1, i, gpre[:, tile(i)], full[2])

    reduce_x(2)

    grad_two = collect_wait(1)
    back_stats(grad_two, normal_two[...], gain_two, 2)
    swap_stats(2)
    ns[0, 2:3] = jnp.sum(grad_two * normal_two[...], axis=0, keepdims=True)
    ns[0, 3:4] = jnp.sum(grad_two, axis=0, keepdims=True)
    ns[0, 4:8] = jnp.zeros((4, half), jnp.float32)
    grad = up_ref[...] + finish_back(grad_two, normal_two[...], inverse[1], gain_two, 2)
    mgrad[...] = grad
    spread_s[3] = grad.astype(jnp.bfloat16)
    spread_start(3)
    reduce_x(1)
    out_ref[...] = middle[...] + collect_wait(2)
    reduce_z(2)
    spread_wait(3)

    gmix[...] = wide(full[3], attn_weight(), ((1,), (1,))).astype(jnp.bfloat16)
    product(0, 3, mixed[...], full[3])

    @pl.loop(0, pairs)
    def _(hp):
        query, key, value = (part_of(trip, part, hp) for part in range(3))
        upper = gmix[:, pl.ds(pl.multiple_of(hp * width, width), width)]
        grad_query = [None, None]
        grad_key = [None, None]
        grad_value = [None, None]

        def add(total, spot, term):
            total[spot] = term if total[spot] is None else total[spot] + term

        for head in range(2):
            query_m, key_m = query * masks[head], key * masks[head]
            upper_m = upper * masks[head]
            for b in range(2):
                n = (b + 1) * block
                here = slice(b * block, n)
                scores = wide(query_m[here], key[:n], ((1,), (1,))) * scale
                scores = jnp.where(causal(block, n, b * block), scores, masked_score)
                probs = jnp.exp(scores - lse[hp * 2 + head, b * block : n])
                rounded = probs.astype(jnp.bfloat16)
                grad_probs = wide(upper_m[here], value[:n], ((1,), (1,)))
                delta = jnp.sum(probs * grad_probs, axis=1, keepdims=True)
                grad_scores = (probs * (grad_probs - delta) * scale).astype(jnp.bfloat16)
                add(grad_query, b, wide(grad_scores, key_m[:n], ((1,), (0,))))
                for spot in range(b + 1):
                    cols = slice(spot * block, (spot + 1) * block)
                    add(grad_key, spot, wide(grad_scores[:, cols], query_m[here], ((0,), (0,))))
                    add(grad_value, spot, wide(rounded[:, cols], upper_m[here], ((0,), (0,))))
        for part, pieces in enumerate((grad_query, grad_key, grad_value)):
            for b in range(2):
                gtrip[
                    b * block : (b + 1) * block,
                    pl.ds(pl.multiple_of((part * pairs + hp) * width, width), width),
                ] = pieces[b].astype(jnp.bfloat16)

    tmp[...] = wide(
        gtrip[...], wa[0:qkv_groups].reshape(qkv_groups * width, 2 * half), ((1,), (0,))
    )
    collect_start(3)

    @pl.loop(0, 3)
    def _(i):
        product(
            0,
            i,
            gtrip[:, pl.ds(pl.multiple_of(i * pairs * width, pairs * width), pairs * width)],
            full[0],
        )

    reduce_x(0)
    reduce_z(1)
    grad_one = collect_wait(3)
    back_stats(grad_one, normal_one[...], gain_one, 3)
    swap_stats(3)
    ns[0, 0:1] = jnp.sum(grad_one * normal_one[...], axis=0, keepdims=True)
    ns[0, 1:2] = jnp.sum(grad_one, axis=0, keepdims=True)
    pending.append(push(ns.at[0], nr.at[0], NS, NS, far(c)))
    back_ref[...] = mgrad[...] + finish_back(
        grad_one, normal_one[...], inverse[0], gain_one, 3
    )
    arrived(nr.at[0], NS)
    ns[1] = ns[0] + nr[0]
    pending.append(push(ns.at[1], nr.at[1], NS + 1, NS + 1, x_peer))
    reduce_z(0)
    arrived(nr.at[1], NS + 1)
    ns[2] = ns[1] + nr[1]
    for step in range(1, nz):
        pending.append(
            push(ns.at[2], nr.at[2 + z], NS + 2 + step, NS + 2 + z, at_z((z + step) % nz))
        )
    nr[2 + z] = ns[2]
    reduce_end(2, sum_d_ref)
    reduce_end(1, sum_u_ref)
    reduce_end(0, sum_a_ref)
    for step in range(1, nz):
        zz = (z + step) % nz
        arrived(nr.at[2 + zz], NS + 2 + zz)
    total = nr[2]
    for zz in range(1, nz):
        total = total + nr[2 + zz]
    norm_sum_ref[...] = total * factor

    for copy in pending:
        copy.wait_send()


def adam_values(weight, grad, first, second, decay):
    first_moment = beta_one * first + (1.0 - beta_one) * grad
    second_moment = beta_two * second + (1.0 - beta_two) * grad * grad
    step_size = (
        first_moment
        / (1.0 - beta_one**STEP)
        / (jnp.sqrt(second_moment / (1.0 - beta_two**STEP)) + adam_eps)
    )
    return weight - learn_rate * (step_size + decay * weight), first_moment, second_moment


def adam_kernel(pairs, *refs):
    sum_a, sum_u, sum_d, norm_sum = refs[:4]
    params, moments = refs[4:9], refs[9:14]
    grads, news, new_moments = refs[14:19], refs[19:24], refs[24:29]
    cut = 3 * pairs
    values = (
        norm_sum[0 : params[0].shape[0]],
        sum_a[0:cut].reshape(params[1].shape),
        sum_a[cut:].reshape(params[2].shape),
        sum_u[...],
        sum_d[...],
    )
    for i in range(5):
        grads[i][...] = values[i]
        new, first, second = adam_values(
            params[i][...], values[i], moments[i][0], moments[i][1], decay_rate if i else 0.0
        )
        news[i][...] = new
        new_moments[i][0] = first
        new_moments[i][1] = second


def on_device_fused(
    block_in,
    upstream,
    norm_params,
    w_qkv,
    w_attn,
    w_up,
    w_down,
    mom_norm,
    mom_qkv,
    mom_attn,
    mom_up,
    mom_down,
):
    low = LOW
    ndp = lax.axis_size("dp")
    nz = ndp // low
    tokens, half = block_in.shape
    pairs = w_qkv.shape[1] // 2
    per = w_qkv.shape[2]
    groups = 4 * pairs
    width = 2 * per * ndp
    hidden_rows = w_up.shape[0]
    hidden = hidden_rows * ndp
    tiles = hidden // HIDDEN_TILE
    token_count = tokens * ndp * lax.axis_size("row")
    bf, f32 = jnp.bfloat16, jnp.float32

    def both(kind_of):
        return [kind_of(0), kind_of(1), kind_of(1)]

    def piece(p):
        return (groups, 2 * per, half) if p == 0 else (hidden_rows, half)

    def whole(p, cols):
        return (groups, ndp, 2 * per, cols) if p == 0 else (hidden, cols)

    scratch = (
        both(lambda p: pltpu.VMEM(piece(p), bf))
        + both(lambda p: pltpu.VMEM(whole(p, 2 * half), bf))
        + [
            pltpu.VMEM((4, tokens, 128), f32),
            pltpu.VMEM((4, tokens, 128), f32),
            pltpu.VMEM((4, tokens, half), bf),
            pltpu.VMEM((4, tokens, 2 * half), bf),
            pltpu.VMEM((4, 2, tokens, half), bf),
            pltpu.VMEM((4, 2, tokens, half), bf),
            pltpu.VMEM((2, tokens, half), f32),
            pltpu.VMEM((tokens, 2 * half), f32),
            pltpu.VMEM((tokens, 3 * pairs * width), bf),
            pltpu.VMEM((tokens, pairs * width), bf),
            pltpu.VMEM((2 * pairs, tokens, 1), f32),
            pltpu.VMEM((tokens, hidden), bf),
            pltpu.VMEM((tokens, hidden), bf),
            pltpu.VMEM((tokens, half), f32),
            pltpu.VMEM((tokens, half), f32),
            pltpu.VMEM((tokens, half), f32),
            pltpu.VMEM((2, tokens, 1), f32),
            pltpu.VMEM((tokens, pairs * width), bf),
            pltpu.VMEM((tokens, 3 * pairs * width), bf),
            pltpu.VMEM((tokens, half), f32),
        ]
        + both(lambda p: pltpu.VMEM(whole(p, half), f32))
        + both(lambda p: pltpu.VMEM(whole(p, half), bf))
        + both(lambda p: pltpu.VMEM(whole(p, half), bf))
        + both(lambda p: pltpu.VMEM((nz,) + piece(p), bf))
        + both(lambda p: pltpu.VMEM((nz,) + piece(p), bf))
        + [
            pltpu.VMEM((3, 8, half), f32),
            pltpu.VMEM((2 + nz, 8, half), f32),
            pltpu.SemaphoreType.DMA((22 + 15 * nz + 6 * low * nz + 3 * tiles,)),
            pltpu.SemaphoreType.DMA((22 + 15 * nz + 6 * low * nz + 3 * tiles,)),
            pltpu.SemaphoreType.DMA((7,)),
        ]
    )
    vmem = pl.BlockSpec(memory_space=pltpu.VMEM)
    outs = (
        jax.ShapeDtypeStruct(block_in.shape, f32),
        jax.ShapeDtypeStruct(block_in.shape, f32),
        jax.ShapeDtypeStruct(piece(0), f32),
        jax.ShapeDtypeStruct(piece(1), f32),
        jax.ShapeDtypeStruct(piece(1), f32),
        jax.ShapeDtypeStruct((8, half), f32),
    )
    block_out, input_grad, *totals = pl.pallas_call(
        functools.partial(step_kernel, nz, low, 1.0 / math.sqrt(token_count)),
        out_shape=outs,
        in_specs=[vmem] * 7,
        out_specs=[vmem] * len(outs),
        scratch_shapes=scratch,
        compiler_params=pltpu.CompilerParams(
            collective_id=0, has_side_effects=True, vmem_limit_bytes=VMEM_BYTES
        ),
    )(block_in, upstream, norm_params, w_qkv, w_attn, w_up, w_down)
    params = (norm_params, w_qkv, w_attn, w_up, w_down)
    moments = (mom_norm, mom_qkv, mom_attn, mom_up, mom_down)
    shapes = [jax.ShapeDtypeStruct(item.shape, f32) for item in params * 2 + moments]
    updated = pl.pallas_call(
        functools.partial(adam_kernel, pairs),
        out_shape=shapes,
        in_specs=[vmem] * 14,
        out_specs=[vmem] * 15,
        compiler_params=pltpu.CompilerParams(vmem_limit_bytes=40 * 1024 * 1024),
    )(*totals, *params, *moments)
    return (block_out, input_grad, *updated)


def fits(block_in, w_qkv, w_up, ndp, nrow, ncol):
    return (
        nrow == 2
        and ncol == 2
        and ndp % LOW == 0
        and ndp <= 8
        and block_in.shape[0] == SEQ
        and w_qkv.shape[1] % 2 == 0
        and w_qkv.shape[2] == 8
        and (w_up.shape[0] * ndp) % HIDDEN_TILE == 0
        and w_up.shape[0] % 16 == 0
    )


def run_step(*args):
    sizes = [lax.axis_size(name) for name in ("dp", "row", "col")]
    if fits(args[0], args[3], args[5], *sizes):
        return on_device_fused(*args)
    return on_device(*args)


def solution(mesh):
    in_specs = (
        P(("dp", "row"), "col"),
        P(("dp", "row"), "col"),
        P(None, "col"),
        P(None, "row", "dp", "col"),
        P("row", "dp", "col"),
        P(("dp", "row"), "col"),
        P(("dp", "row"), "col"),
        P(None, None, "col"),
        P(None, None, "row", "dp", "col"),
        P(None, "row", "dp", "col"),
        P(None, ("dp", "row"), "col"),
        P(None, ("dp", "row"), "col"),
    )
    out_specs = (
        P(("dp", "row"), "col"),
        P(("dp", "row"), "col"),
        P(None, "col"),
        P(None, "row", "dp", "col"),
        P("row", "dp", "col"),
        P(("dp", "row"), "col"),
        P(("dp", "row"), "col"),
        P(None, "col"),
        P(None, "row", "dp", "col"),
        P("row", "dp", "col"),
        P(("dp", "row"), "col"),
        P(("dp", "row"), "col"),
        P(None, None, "col"),
        P(None, None, "row", "dp", "col"),
        P(None, "row", "dp", "col"),
        P(None, ("dp", "row"), "col"),
        P(None, ("dp", "row"), "col"),
    )
    return jax.shard_map(
        run_step, mesh=mesh, in_specs=in_specs, out_specs=out_specs, check_vma=False
    )
```

```python
import functools
import math

import jax
import jax.numpy as jnp
from jax import lax
from jax.experimental import pallas as pl
from jax.experimental.pallas import tpu as pltpu
from jax.sharding import PartitionSpec as P

SEQ = 512
STEP = 4
LOW = 2


norm_eps = 1e-05
adam_eps = 1e-08
beta_one = 0.9
beta_two = 0.95
learn_rate = 0.02
decay_rate = 0.1
gelu_coef = math.sqrt(2.0 / math.pi)
cubic_coef = 0.044715
masked_score = -1e30

group = ("row", "col")
swap_pair = [(0, 1), (1, 0)]
spread_first = [(1, 2), (2, 1)]
spread_second = [(0, 2), (3, 1), (1, 0), (2, 3)]
collect_second = [(dst, src) for src, dst in spread_second]


def smooth_pair(values):
    squared = values * values
    bent = jnp.tanh(gelu_coef * (values + cubic_coef * squared * values))
    smooth = 0.5 * values * (1.0 + bent)
    slope = 0.5 * (1.0 + bent) + 0.5 * values * (1.0 - bent * bent) * gelu_coef * (
        1.0 + 3.0 * cubic_coef * squared
    )
    return (smooth, slope)


def wide(left, right, dims):
    return lax.dot_general(left, right, (dims, ((), ())), preferred_element_type=jnp.float32)


def normalize(rows_in, gain_row, shift_row):
    count = rows_in.shape[1]
    mean_here = jnp.mean(rows_in, axis=1, keepdims=True)
    offset = rows_in - mean_here
    square_here = jnp.sum(offset * offset, axis=1, keepdims=True)
    there = lax.ppermute(jnp.concatenate([mean_here, square_here], axis=1), "col", swap_pair)
    gap = mean_here - there[:, :1]
    spread = (square_here + there[:, 1:] + gap * gap * (0.5 * count)) / (2.0 * count)
    inverse = lax.rsqrt(spread + norm_eps)
    normal = (rows_in - (mean_here - 0.5 * gap)) * inverse
    return (normal, inverse, (normal * gain_row + shift_row).astype(jnp.bfloat16))


def norm_back(grad_normed, normal, inverse, gain_row):
    count = 2.0 * grad_normed.shape[1]
    scaled = grad_normed * gain_row
    here = jnp.concatenate(
        [
            jnp.sum(scaled, axis=1, keepdims=True),
            jnp.sum(scaled * normal, axis=1, keepdims=True),
        ],
        axis=1,
    )
    total = (here + lax.ppermute(here, "col", swap_pair)) / count
    return inverse * (scaled - total[:, :1] - normal * total[:, 1:])


def pick(flag, one, other):
    return jnp.where(flag, one, other), jnp.where(flag, other, one)


def spread_rows(block):
    row, col = lax.axis_index("row"), lax.axis_index("col")
    first = lax.ppermute(block, group, spread_first)
    second = lax.ppermute(block, group, spread_second)
    first = jnp.where(row == col, block, first)
    low, high = pick(row == 0, first, second)
    return low, high


def collect_rows(low, high):
    row, col = lax.axis_index("row"), lax.axis_index("col")
    first, second = pick(row == 0, low, high)
    first_in = lax.ppermute(first.astype(jnp.bfloat16), group, spread_first)
    second_in = lax.ppermute(second.astype(jnp.bfloat16), group, collect_second)
    return jnp.where(row == col, first, first_in.astype(jnp.float32)) + second_in.astype(
        jnp.float32
    )


def out_project(rows, weight):
    half = weight.shape[1] // 2
    return collect_rows(
        wide(rows, weight[:, :half], ((1,), (0,))), wide(rows, weight[:, half:], ((1,), (0,)))
    )


def small_ring():
    size = lax.axis_size("dp")
    return size % LOW == 0 and size <= 8


def high_steps(sign):
    size = lax.axis_size("dp")
    high = size // LOW
    return [
        [(i, ((i // LOW + sign * step) % high) * LOW + i % LOW) for i in range(size)]
        for step in range(1, high)
    ]


def low_step():
    return [(i, i ^ 1) for i in range(lax.axis_size("dp"))]


def gather_weight(shard, axis):
    shard = shard.astype(jnp.bfloat16)
    if small_ring():
        near = jnp.concatenate(
            [shard] + [lax.ppermute(shard, "dp", perm) for perm in high_steps(1)], axis=axis
        )
        block = jnp.concatenate([near, lax.ppermute(near, "dp", low_step())], axis=axis)
    else:
        block = lax.all_gather(shard, "dp", axis=axis, tiled=True)
    there = lax.ppermute(block, "col", swap_pair)
    low, high = pick(lax.axis_index("col") == 0, block, there)
    return jnp.concatenate([low, high], axis=-1)


def reduce_weight(make, axis):
    away = make(False).astype(jnp.bfloat16)
    total = make(True) + lax.ppermute(away, "col", swap_pair).astype(jnp.float32)
    if not small_ring():
        return lax.psum_scatter(total, "dp", scatter_dimension=axis, tiled=True)
    near, far = jnp.split(total, 2, axis=axis)
    near = near + lax.ppermute(far.astype(jnp.bfloat16), "dp", low_step()).astype(jnp.float32)
    own, *rest = jnp.split(near, lax.axis_size("dp") // LOW, axis=axis)
    for piece, perm in zip(rest, high_steps(-1)):
        own = own + lax.ppermute(piece.astype(jnp.bfloat16), "dp", perm).astype(jnp.float32)
    return own


def sum_everywhere(terms):
    if not small_ring():
        return lax.psum(terms, ("dp", "row"))
    terms = terms + lax.ppermute(terms, "row", swap_pair)
    terms = terms + lax.ppermute(terms, "dp", low_step())
    moved = [lax.ppermute(terms, "dp", perm) for perm in high_steps(1)]
    for piece in moved:
        terms = terms + piece
    return terms


def head_scores(triples_ref, heads, size, head):
    width = heads * size
    query = triples_ref[:, head * size : (head + 1) * size]
    key = triples_ref[:, width + head * size : width + (head + 1) * size]
    value = triples_ref[:, 2 * width + head * size : 2 * width + (head + 1) * size]
    scores = wide(query, key, ((1,), (1,))) * (1.0 / math.sqrt(size))
    length = scores.shape[0]
    allowed = lax.broadcasted_iota(jnp.int32, (length, length), 0) >= lax.broadcasted_iota(
        jnp.int32, (length, length), 1
    )
    return query, key, value, jnp.where(allowed, scores, masked_score)


def attend_kernel(heads, size, triples_ref, mixed_ref, total_ref):
    for head in range(heads):
        _, _, value, scores = head_scores(triples_ref, heads, size, head)
        highest = jnp.max(scores, axis=1, keepdims=True)
        log_total = highest + jnp.log(jnp.sum(jnp.exp(scores - highest), axis=1, keepdims=True))
        probs = jnp.exp(scores - log_total).astype(jnp.bfloat16)
        mixed_ref[:, head * size : (head + 1) * size] = wide(probs, value, ((1,), (0,))).astype(
            jnp.bfloat16
        )
        total_ref[:, head : head + 1] = log_total


def attend_back_kernel(heads, size, triples_ref, grad_ref, total_ref, out_ref):
    width = heads * size
    scale = 1.0 / math.sqrt(size)
    for head in range(heads):
        query, key, value, scores = head_scores(triples_ref, heads, size, head)
        grad_mixed = grad_ref[:, head * size : (head + 1) * size]
        probs = jnp.exp(scores - total_ref[:, head : head + 1])
        grad_values = wide(probs.astype(jnp.bfloat16), grad_mixed, ((0,), (0,)))
        grad_probs = wide(grad_mixed, value, ((1,), (1,)))
        delta = jnp.sum(probs * grad_probs, axis=1, keepdims=True)
        grad_scores = (probs * (grad_probs - delta) * scale).astype(jnp.bfloat16)
        for part, piece in enumerate(
            (
                wide(grad_scores, key, ((1,), (0,))),
                wide(grad_scores, query, ((0,), (0,))),
                grad_values,
            )
        ):
            start = part * width + head * size
            out_ref[:, start : start + size] = piece.astype(jnp.bfloat16)


def by_sequence(kernel, operands, outs):
    rows = operands[0].shape[0]

    def spec(shape):
        return pl.BlockSpec((SEQ, shape[1]), lambda step: (step, 0))

    return pl.pallas_call(
        kernel,
        grid=(rows // SEQ,),
        in_specs=[spec(item.shape) for item in operands],
        out_specs=[spec(item.shape) for item in outs],
        out_shape=outs,
        compiler_params=pltpu.CompilerParams(vmem_limit_bytes=40 * 1024 * 1024),
        cost_estimate=pl.CostEstimate(
            flops=rows * SEQ * 2048, bytes_accessed=rows * 8192, transcendentals=rows * SEQ * 6
        ),
    )(*operands)


def adam_step(weight, grad, moments, decay):
    first_moment = beta_one * moments[0] + (1.0 - beta_one) * grad
    second_moment = beta_two * moments[1] + (1.0 - beta_two) * grad * grad
    step_size = (
        first_moment
        / (1.0 - beta_one**STEP)
        / (jnp.sqrt(second_moment / (1.0 - beta_two**STEP)) + adam_eps)
    )
    return (
        weight - learn_rate * (step_size + decay * weight),
        jnp.stack([first_moment, second_moment]),
    )


def on_device(
    block_in,
    upstream,
    norm_params,
    w_qkv,
    w_attn,
    w_up,
    w_down,
    mom_norm,
    mom_qkv,
    mom_attn,
    mom_up,
    mom_down,
):
    heads = w_qkv.shape[1]
    size = w_qkv.shape[2] * lax.axis_size("dp")
    width = heads * size
    at_low = lax.axis_index("col") == 0

    normal_one, inverse_one, normed_one = normalize(block_in, norm_params[0], norm_params[1])
    qkv_mat = gather_weight(w_qkv, 2).reshape(3 * width, -1)
    one_low, one_high = spread_rows(normed_one)
    attn_mat = gather_weight(w_attn, 1).reshape(width, -1)
    up_mat = gather_weight(w_up, 0)
    up_low, up_high = spread_rows(upstream.astype(jnp.bfloat16))
    down_mat = gather_weight(w_down, 0)

    triples = wide(
        jnp.concatenate([one_low, one_high], axis=1), qkv_mat, ((1,), (1,))
    ).astype(jnp.bfloat16)
    mixed, log_total = by_sequence(
        functools.partial(attend_kernel, heads, size),
        (triples,),
        (
            jax.ShapeDtypeStruct((triples.shape[0], width), jnp.bfloat16),
            jax.ShapeDtypeStruct((triples.shape[0], heads), jnp.float32),
        ),
    )
    middle = block_in + out_project(mixed, attn_mat)
    normal_two, inverse_two, normed_two = normalize(middle, norm_params[2], norm_params[3])
    two_low, two_high = spread_rows(normed_two)
    grad_hidden = wide(jnp.concatenate([up_low, up_high], axis=1), down_mat, ((1,), (1,)))
    hidden_pre = wide(jnp.concatenate([two_low, two_high], axis=1), up_mat, ((1,), (1,)))
    activated, slope = smooth_pair(hidden_pre)
    activated = activated.astype(jnp.bfloat16)
    grad_pre = (grad_hidden * slope).astype(jnp.bfloat16)
    grad_normed_two = out_project(grad_pre, up_mat)
    block_out = middle + out_project(activated, down_mat)

    def products(left, low, high):
        own, away = pick(at_low, low, high)
        return lambda mine: wide(left, own if mine else away, ((0,), (0,)))

    grad_down = reduce_weight(products(activated, up_low, up_high), 0)
    grad_up = reduce_weight(products(grad_pre, two_low, two_high), 0)
    middle_grad = upstream + norm_back(grad_normed_two, normal_two, inverse_two, norm_params[2])
    mid_low, mid_high = spread_rows(middle_grad.astype(jnp.bfloat16))
    grad_mixed = wide(
        jnp.concatenate([mid_low, mid_high], axis=1), attn_mat, ((1,), (1,))
    ).astype(jnp.bfloat16)

    def by_head(make, parts):
        return lambda mine: make(mine).reshape(*parts, heads, size, -1)

    grad_attn = reduce_weight(by_head(products(mixed, mid_low, mid_high), ()), 1)
    (grad_triples,) = by_sequence(
        functools.partial(attend_back_kernel, heads, size),
        (triples, grad_mixed, log_total),
        (jax.ShapeDtypeStruct(triples.shape, jnp.bfloat16),),
    )
    grad_qkv = reduce_weight(by_head(products(grad_triples, one_low, one_high), (3,)), 2)
    grad_normed_one = out_project(grad_triples, qkv_mat)
    input_grad = middle_grad + norm_back(grad_normed_one, normal_one, inverse_one, norm_params[0])
    norm_terms = jnp.stack(
        [
            jnp.sum(grad_normed_one * normal_one, axis=0),
            jnp.sum(grad_normed_one, axis=0),
            jnp.sum(grad_normed_two * normal_two, axis=0),
            jnp.sum(grad_normed_two, axis=0),
        ]
    )
    grad_norm = sum_everywhere(norm_terms)
    token_count = block_in.shape[0] * lax.axis_size("dp") * lax.axis_size("row")
    factor = 1.0 / math.sqrt(token_count)
    grad_norm = grad_norm * factor
    grad_qkv = grad_qkv * factor
    grad_attn = grad_attn * factor
    grad_up = grad_up * factor
    grad_down = grad_down * factor
    new_norm, new_mom_norm = adam_step(norm_params, grad_norm, mom_norm, 0.0)
    new_qkv, new_mom_qkv = adam_step(w_qkv, grad_qkv, mom_qkv, decay_rate)
    new_attn, new_mom_attn = adam_step(w_attn, grad_attn, mom_attn, decay_rate)
    new_up, new_mom_up = adam_step(w_up, grad_up, mom_up, decay_rate)
    new_down, new_mom_down = adam_step(w_down, grad_down, mom_down, decay_rate)
    return (
        block_out,
        input_grad,
        grad_norm,
        grad_qkv,
        grad_attn,
        grad_up,
        grad_down,
        new_norm,
        new_qkv,
        new_attn,
        new_up,
        new_down,
        new_mom_norm,
        new_mom_qkv,
        new_mom_attn,
        new_mom_up,
        new_mom_down,
    )


MESH = pl.DeviceIdType.MESH
VMEM_BYTES = 67043328
HIDDEN_TILE = 256


def causal(rows, cols, first):
    return (
        lax.broadcasted_iota(jnp.int32, (rows, cols), 0) + first
        >= lax.broadcasted_iota(jnp.int32, (rows, cols), 1)
    )


def head_masks(per, width):
    lane = lax.broadcasted_iota(jnp.int32, (1, width), 1)
    return [
        jnp.where((lane // per) % 2 == part, 1.0, 0.0).astype(jnp.bfloat16) for part in range(2)
    ]


def row_stats(first, second, width=128):
    lane = lax.broadcasted_iota(jnp.int32, (first.shape[0], width), 1)
    return jnp.where(lane == 0, first, second)


def step_kernel(
    nz,
    low,
    factor,
    block_ref,
    up_ref,
    norm_ref,
    wqkv_ref,
    wattn_ref,
    wup_ref,
    wdown_ref,
    out_ref,
    back_ref,
    sum_q_ref,
    sum_o_ref,
    sum_u_ref,
    sum_d_ref,
    norm_sum_ref,
    shard_q,
    shard_o,
    shard_u,
    shard_d,
    wq,
    wo,
    wu,
    wd,
    stat_s,
    stat_r,
    spread_s,
    full,
    col_s,
    col_r,
    keep,
    tmp,
    trip,
    mixed,
    lse,
    act,
    gpre,
    middle,
    normal_one,
    normal_two,
    inverse,
    gmix,
    gtrip,
    mgrad,
    gq,
    go,
    gu,
    gd,
    gsq,
    gso,
    gsu,
    gsd,
    grq,
    gro,
    gru,
    grd,
    xrq,
    xro,
    xru,
    xrd,
    zrq,
    zro,
    zru,
    zrd,
    total_q,
    total_o,
    total_u,
    total_d,
    total_norm,
    ns,
    nr,
    send,
    recv,
    local,
):
    dp, r, c = lax.axis_index("dp"), lax.axis_index("row"), lax.axis_index("col")
    z, x = dp // low, dp % low
    same = r == c
    tokens, half = block_ref.shape
    per = wqkv_ref.shape[2]
    pairs = wqkv_ref.shape[1] // 2
    width = 2 * per * nz * low
    ndp = nz * low
    hidden_rows = wup_ref.shape[0]
    hidden = hidden_rows * ndp
    tiles = hidden // HIDDEN_TILE
    groups = 3 * pairs
    Q, O, U, D = range(4)

    STAT, SPR, COL, GZ = 0, 8, 24, 40
    GX = GZ + 4 * nz
    GC = GX + 4 * nz
    RC = GC + 4
    RX = RC + 4
    RZ = RX + 4 * nz
    NS = RZ + 4 * nz
    GD = NS + 2 + nz

    def at_z(zz):
        return {"dp": zz * low + x}

    x_peer = {"dp": z * low + 1 - x}
    partner = {"col": 1 - c}

    def far(other):
        return {"row": 1 - r, "col": other}

    def feat(f):
        return pl.ds(pl.multiple_of(f * half, half), half)

    mine, other = feat(c), feat(1 - c)
    pending = []
    writes = []
    guarded = []

    def describe(src, dst, s, q, where):
        return pltpu.make_async_remote_copy(
            src_ref=src,
            dst_ref=dst,
            send_sem=send.at[s],
            recv_sem=recv.at[q],
            device_id=where,
            device_id_type=MESH,
        )

    def push(src, dst, s, q, where):
        copy = describe(src, dst, s, q, where)
        copy.start()
        return copy

    def arrived(dst, q):
        describe(dst, dst, q, q, partner).wait_recv()

    weights = (wq, wo, wu, wd)

    def slot(p, owner, f):
        if p < 2:
            return weights[p].at[:, owner, :, feat(f)]
        rows = pl.ds(pl.multiple_of(owner * hidden_rows, hidden_rows), hidden_rows)
        return weights[p].at[rows, feat(f)]

    shards = (shard_q, shard_o, shard_u, shard_d)

    shard_q[...] = wqkv_ref[...].reshape(groups, 2 * per, half).astype(jnp.bfloat16)
    shard_o[...] = wattn_ref[...].reshape(pairs, 2 * per, half).astype(jnp.bfloat16)
    shard_u[...] = wup_ref[...].astype(jnp.bfloat16)
    shard_d[...] = wdown_ref[...].astype(jnp.bfloat16)

    block = tokens // 2
    parts = [slice(h * block, (h + 1) * block) for h in range(2)]

    def local_stats(rows_in, k, h):
        mean_here = jnp.mean(rows_in, axis=1, keepdims=True)
        offset = rows_in - mean_here
        square_here = jnp.sum(offset * offset, axis=1, keepdims=True)
        stat_s[k, parts[h]] = row_stats(mean_here, square_here)

    def swap_stats(k, h):
        spot = STAT + 2 * k + h
        pending.append(
            push(stat_s.at[k, parts[h]], stat_r.at[k, parts[h]], spot, spot, partner)
        )

    def finish_norm(rows_in, k, h, gain, shift, normal_ref, inverse_index, out):
        rows = parts[h]
        arrived(stat_r.at[k, rows], STAT + 2 * k + h)
        here, there = stat_s[k, rows], stat_r[k, rows]
        mean_here, square_here = here[:, 0:1], here[:, 1:2]
        gap = mean_here - there[:, 0:1]
        spread = (square_here + there[:, 1:2] + gap * gap * (0.5 * half)) / (2.0 * half)
        inv = lax.rsqrt(spread + norm_eps)
        normal = (rows_in - (mean_here - 0.5 * gap)) * inv
        normal_ref[rows] = normal
        inverse[inverse_index, rows] = inv
        out[rows] = (normal * gain + shift).astype(jnp.bfloat16)

    def back_stats(grad, normal, gain, k, h):
        scaled = grad * gain
        stat_s[k, parts[h]] = row_stats(
            jnp.sum(scaled, axis=1, keepdims=True),
            jnp.sum(scaled * normal, axis=1, keepdims=True),
        )

    def finish_back(grad, normal, inv, gain, k, h):
        rows = parts[h]
        arrived(stat_r.at[k, rows], STAT + 2 * k + h)
        total = (stat_s[k, rows] + stat_r[k, rows]) / (2.0 * half)
        return inv * (grad * gain - total[:, 0:1] - normal * total[:, 1:2])

    def spread_spot(k, f, h):
        return SPR + (2 * k + f) * 2 + h

    def spread_start(k, h):
        rows = parts[h]
        src = spread_s.at[k, rows]
        dst = full.at[k, rows, mine]
        pending.append(push(src, dst, spread_spot(k, 0, h), spread_spot(k, c, h), far(r)))

        @pl.when(same)
        def _():
            pltpu.make_async_copy(src, dst, local.at[4 + 2 * k + h]).start()

        @pl.when(jnp.logical_not(same))
        def _():
            push(src, dst, spread_spot(k, 1, h), spread_spot(k, c, h), partner)

    def spread_wait(k):
        for h in range(2):
            rows = parts[h]
            src = spread_s.at[k, rows]
            dst = full.at[k, rows, mine]
            arrived(full.at[k, rows, other], spread_spot(k, 1 - c, h))

            @pl.when(same)
            def _():
                pltpu.make_async_copy(src, dst, local.at[4 + 2 * k + h]).wait()

            @pl.when(jnp.logical_not(same))
            def _():
                arrived(dst, spread_spot(k, c, h))
                describe(
                    src, dst, spread_spot(k, 1, h), spread_spot(k, c, h), partner
                ).wait_send()

    def collect_spot(k, f, h):
        return COL + (2 * k + f) * 2 + h

    def collect_start(k, h):
        rows = parts[h]
        col_s[k, 0, rows] = tmp[rows, other].astype(jnp.bfloat16)
        col_s[k, 1, rows] = tmp[rows, mine].astype(jnp.bfloat16)

        @pl.when(same)
        def _():
            keep[k % 2, rows] = tmp[rows, mine]
            spot = collect_spot(k, 0, h)
            push(col_s.at[k, 0, rows], col_r.at[k, 0, rows], spot, spot, partner)

        @pl.when(jnp.logical_not(same))
        def _():
            for f, where in enumerate((far(1 - c), far(c))):
                push(
                    col_s.at[k, f, rows],
                    col_r.at[k, 1, rows],
                    collect_spot(k, f, h),
                    collect_spot(k, 1, h),
                    where,
                )

    def collect_wait(k, h):
        rows = parts[h]
        arrived(col_r.at[k, 1, rows], collect_spot(k, 1, h))

        def sent(f):
            spot = collect_spot(k, f, h)
            describe(
                col_s.at[k, f, rows], col_r.at[k, f, rows], spot, spot, partner
            ).wait_send()

        @pl.when(same)
        def _():
            sent(0)

        @pl.when(jnp.logical_not(same))
        def _():
            arrived(col_r.at[k, 0, rows], collect_spot(k, 0, h))
            keep[k % 2, rows] = col_r[k, 0, rows].astype(jnp.float32)
            sent(0)
            sent(1)

        return keep[k % 2, rows] + col_r[k, 1, rows].astype(jnp.float32)

    def relay(p, zz, up, src):
        dst = slot(p, zz * low + x, c)
        spot = (GZ if up else GD) + p * nz + zz
        to = at_z((z + 1) % nz) if up else at_z((z + nz - 1) % nz)
        return describe(dst if src is None else src, dst, spot, GZ + p * nz + zz, to)

    def guard(flag, copy):
        @pl.when(flag)
        def _():
            copy.start()

        guarded.append((flag, copy))

    def gather_own_z(p):
        guard(z < nz - 1, relay(p, z, True, shards[p]))
        guard(z > 0, relay(p, z, False, shards[p]))

    def x_copy(p, zz, src):
        dst = slot(p, zz * low + x, c)
        spot = GX + p * nz + zz
        return describe(dst if src is None else src, dst, spot, spot, x_peer)

    def gather_own_x(p):
        x_copy(p, z, shards[p]).start()
        for step in range(nz):
            pending.append(x_copy(p, (z + step) % nz, None))

    def band(p, cols):
        return weights[p].at[:, :, :, cols] if p < 2 else weights[p].at[:, cols]

    def to_partner(p, owner):
        push(slot(p, owner, c), slot(p, owner, c), GC + p, GC + p, partner)

    def gather_own_c(p):
        pltpu.make_async_copy(shards[p], slot(p, dp, c), local.at[p]).start()
        push(shards[p], slot(p, dp, c), GC + p, GC + p, partner)
        pending.append(describe(band(p, mine), band(p, mine), GC + p, GC + p, partner))

    steps = list(range(1, nz))
    def by_distance(far_z, serve):
        below, above = (z + nz - far_z) % nz, (z + far_z) % nz

        @pl.when(z >= far_z)
        def _():
            serve(below, True)

        @pl.when(z + far_z < nz)
        def _():
            serve(above, False)

    def gather_z(p, some):
        def serve(zz, up):
            owner = zz * low + x
            arrived(slot(p, owner, c), GZ + p * nz + zz)
            x_copy(p, zz, None).start()

            @pl.when((z < nz - 1) if up else (z > 0))
            def _():
                relay(p, zz, up, None).start()

            to_partner(p, owner)

        for far_z in some:
            by_distance(far_z, serve)
            for zz, up, flag in (
                ((z + nz - far_z) % nz, True, jnp.logical_and(z >= far_z, z < nz - 1)),
                ((z + far_z) % nz, False, jnp.logical_and(z + far_z < nz, z > 0)),
            ):
                guarded.append((flag, relay(p, zz, up, None)))

    def gather_x(p):
        def serve(zz, up):
            owner = zz * low + 1 - x
            arrived(slot(p, owner, c), GX + p * nz + zz)
            to_partner(p, owner)

        serve(z, True)
        for far_z in steps:
            by_distance(far_z, serve)

    def gather_c(p):
        pltpu.make_async_copy(shards[p], slot(p, dp, c), local.at[p]).wait()
        arrived(band(p, other), GC + p)

    sums = (gq, go, gu, gd)
    away = (gsq, gso, gsu, gsd)
    near = (grq, gro, gru, grd)
    from_x = (xrq, xro, xru, xrd)
    from_z = (zrq, zro, zru, zrd)
    totals = (total_q, total_o, total_u, total_d)
    results = (sum_q_ref, sum_o_ref, sum_u_ref, sum_d_ref)

    def index(p, owner):
        if p < 2:
            return (slice(None), owner)
        return (pl.ds(pl.multiple_of(owner * hidden_rows, hidden_rows), hidden_rows),)

    def rows_of(p, i):
        if p < 2:
            return pl.ds(i * pairs, pairs)
        return pl.ds(pl.multiple_of(i * HIDDEN_TILE, HIDDEN_TILE), HIDDEN_TILE)

    def swap_chunk(p, i):
        rows = rows_of(p, i)
        return describe(
            away[p].at[rows], near[p].at[rows], RC + p, RC + p, partner
        )

    def product(p, i, left, right):
        tmp_rows = left.shape[1]
        tmp[0:tmp_rows] = wide(left, right, ((0,), (0,)))
        rows = rows_of(p, i)
        own, gone = tmp[0:tmp_rows, mine], tmp[0:tmp_rows, other].astype(jnp.bfloat16)
        if p < 2:
            own = own.reshape(pairs, ndp, 2 * per, half)
            gone = gone.reshape(pairs, ndp, 2 * per, half)
        sums[p][rows] = own
        away[p][rows] = gone
        swap_chunk(p, i).start()

    def reduce_x(p):
        describe(away[p], near[p], RC + p, RC + p, partner).wait()
        for step in steps + [0]:
            zz = (z + step) % nz
            at = index(p, zz * low + 1 - x)
            total = sums[p][at] + near[p][at].astype(jnp.float32)
            away[p][at] = total.astype(jnp.bfloat16)
            pending.append(
                push(
                    away[p].at[at],
                    from_x[p].at[zz],
                    RX + p * nz + step,
                    RX + p * nz + zz,
                    x_peer,
                )
            )

    def reduce_z(p, some):
        for step in some:
            zz = (z + step) % nz
            at = index(p, zz * low + x)
            arrived(from_x[p].at[zz], RX + p * nz + zz)
            total = (
                sums[p][at] + near[p][at].astype(jnp.float32) + from_x[p][zz].astype(jnp.float32)
            )
            if step == 0:
                sums[p][at] = total
                continue
            away[p][at] = total.astype(jnp.bfloat16)
            pending.append(
                push(
                    away[p].at[at],
                    from_z[p].at[z],
                    RZ + p * nz + step,
                    RZ + p * nz + z,
                    at_z(zz),
                )
            )

    def reduce_end(p):
        total = sums[p][index(p, dp)]
        for step in range(1, nz):
            zz = (z + step) % nz
            arrived(from_z[p].at[zz], RZ + p * nz + zz)
            total = total + from_z[p][zz].astype(jnp.float32)
        totals[p][...] = total * factor
        to_hbm(totals[p], results[p], p)

    def to_hbm(src, dst, i):
        copy = pltpu.make_async_copy(src, dst, local.at[12 + i])
        copy.start()
        writes.append(copy)

    gain_one, shift_one = norm_ref[0:1], norm_ref[1:2]
    gain_two, shift_two = norm_ref[2:3], norm_ref[3:4]

    barrier = pltpu.get_barrier_semaphore()
    peers = [at_z((z + step) % nz) for step in range(1, nz)] + [
        x_peer,
        partner,
        far(c),
        far(1 - c),
    ]
    for peer in peers:
        pl.semaphore_signal(barrier, inc=1, device_id=peer, device_id_type=MESH)
    for h in range(2):
        local_stats(block_ref[parts[h]], 0, h)
    pl.semaphore_wait(barrier, len(peers))

    gather_own_z(Q)
    gather_own_x(Q)
    for h in range(2):
        swap_stats(0, h)
    gather_own_c(Q)
    gather_own_z(O)
    gather_own_x(O)
    for h in range(2):
        finish_norm(
            block_ref[parts[h]], 0, h, gain_one, shift_one, normal_one, 0, spread_s.at[0]
        )
        spread_start(0, h)
    spread_s[1] = up_ref[...].astype(jnp.bfloat16)
    for h in range(2):
        spread_start(1, h)
    gather_own_x(U)
    for far_z in steps[:-1]:
        gather_z(Q, [far_z])
        gather_z(O, [far_z])
    gather_own_z(U)
    gather_own_z(D)
    gather_z(Q, steps[-1:])
    gather_z(O, steps[-1:])
    gather_own_x(D)
    gather_own_c(O)
    gather_x(Q)
    gather_own_c(U)
    gather_own_c(D)
    gather_c(Q)
    spread_wait(0)
    gather_z(U, steps[:1])

    trip[...] = wide(
        full[0], wq[...].reshape(groups * width, 2 * half), ((1,), (1,))
    ).astype(jnp.bfloat16)

    gather_z(D, steps[:1])

    scale = 1.0 / math.sqrt(width // 2)
    masks = head_masks(per, width)

    def part_of(ref, part, hp):
        return ref[:, pl.ds(pl.multiple_of((part * pairs + hp) * width, width), width)]

    def attend_pair(hp):
        query, key, value = (part_of(trip, part, hp) for part in range(3))
        rows = [None, None]
        for head in range(2):
            query_m, value_m = query * masks[head], value * masks[head]
            for b in range(2):
                n = (b + 1) * block
                scores = wide(query_m[b * block : n], key[:n], ((1,), (1,))) * scale
                scores = jnp.where(causal(block, n, b * block), scores, masked_score)
                highest = jnp.max(scores, axis=1, keepdims=True)
                raised = jnp.exp(scores - highest)
                total = jnp.sum(raised, axis=1, keepdims=True)
                lse[hp * 2 + head, b * block : n] = highest + jnp.log(total)
                probs = (raised * (1.0 / total)).astype(jnp.bfloat16)
                got = wide(probs, value_m[:n], ((1,), (0,)))
                rows[b] = got if rows[b] is None else rows[b] + got
        for b in range(2):
            mixed[b * block : (b + 1) * block, pl.ds(pl.multiple_of(hp * width, width), width)] = (
                rows[b].astype(jnp.bfloat16)
            )

    def attn_weight():
        return wo[...].reshape(pairs * width, 2 * half)

    for hp in range(pairs):
        attend_pair(hp)
        if hp == pairs - 2:
            gather_z(U, steps[1:2])
    gather_z(D, steps[1:2])

    gather_x(O)
    gather_c(O)
    for h in range(2):
        tmp[parts[h]] = wide(mixed[parts[h]], attn_weight(), ((1,), (0,)))
        collect_start(0, h)
    gather_z(U, steps[2:])
    gather_z(D, steps[2:])
    for h in range(2):
        middle[parts[h]] = block_ref[parts[h]] + collect_wait(0, h)
        local_stats(middle[parts[h]], 1, h)
        swap_stats(1, h)
        finish_norm(
            middle[parts[h]], 1, h, gain_two, shift_two, normal_two, 1, spread_s.at[2]
        )
        spread_start(2, h)
    gather_x(U)
    gather_x(D)
    gather_c(U)
    gather_c(D)
    spread_wait(1)
    spread_wait(2)

    def tile(i):
        return pl.ds(pl.multiple_of(i * HIDDEN_TILE, HIDDEN_TILE), HIDDEN_TILE)

    @pl.loop(0, tiles)
    def _(i):
        pre = wide(full[2], wu[tile(i)], ((1,), (1,)))
        grad = wide(full[1], wd[tile(i)], ((1,), (1,)))
        smooth, slope = smooth_pair(pre)
        act[:, tile(i)] = smooth.astype(jnp.bfloat16)
        gpre[:, tile(i)] = (grad * slope).astype(jnp.bfloat16)

    for h in range(2):
        tmp[parts[h]] = wide(gpre[parts[h]], wu[...], ((1,), (0,)))
        collect_start(1, h)

    @pl.loop(0, tiles)
    def _(i):
        product(D, i, act[:, tile(i)], full[1])

    @pl.loop(0, tiles // 2)
    def _(i):
        product(U, i, gpre[:, tile(i)], full[2])

    reduce_x(D)

    @pl.loop(tiles // 2, tiles)
    def _(i):
        product(U, i, gpre[:, tile(i)], full[2])

    ns[0] = jnp.zeros((8, half), jnp.float32)
    for h in range(2):
        rows = parts[h]
        grad_two, normal = collect_wait(1, h), normal_two[rows]
        back_stats(grad_two, normal, gain_two, 2, h)
        swap_stats(2, h)
        ns[0, 2:3] += jnp.sum(grad_two * normal, axis=0, keepdims=True)
        ns[0, 3:4] += jnp.sum(grad_two, axis=0, keepdims=True)
        grad = up_ref[rows] + finish_back(grad_two, normal, inverse[1, rows], gain_two, 2, h)
        mgrad[rows] = grad
        spread_s[3, rows] = grad.astype(jnp.bfloat16)
        spread_start(3, h)
    reduce_x(U)
    reduce_z(D, steps[:-1])
    tmp[...] = wide(act[...], wd[...], ((1,), (0,)))
    for h in range(2):
        collect_start(2, h)
    reduce_z(D, steps[-1:])
    spread_wait(3)

    gmix[...] = wide(full[3], attn_weight(), ((1,), (1,))).astype(jnp.bfloat16)
    product(O, 0, mixed[...], full[3])

    def attend_back_pair(hp):
        query, key, value = (part_of(trip, part, hp) for part in range(3))
        upper = gmix[:, pl.ds(pl.multiple_of(hp * width, width), width)]
        grad_query = [None, None]
        grad_key = [None, None]
        grad_value = [None, None]

        def add(total, spot, term):
            total[spot] = term if total[spot] is None else total[spot] + term

        for head in range(2):
            query_m, key_m = query * masks[head], key * masks[head]
            upper_m = upper * masks[head]
            for b in range(2):
                n = (b + 1) * block
                here = slice(b * block, n)
                scores = wide(query_m[here], key[:n], ((1,), (1,))) * scale
                scores = jnp.where(causal(block, n, b * block), scores, masked_score)
                probs = jnp.exp(scores - lse[hp * 2 + head, b * block : n])
                rounded = probs.astype(jnp.bfloat16)
                grad_probs = wide(upper_m[here], value[:n], ((1,), (1,)))
                delta = jnp.sum(probs * grad_probs, axis=1, keepdims=True)
                grad_scores = (probs * (grad_probs - delta) * scale).astype(jnp.bfloat16)
                add(grad_query, b, wide(grad_scores, key_m[:n], ((1,), (0,))))
                for spot in range(b + 1):
                    cols = slice(spot * block, (spot + 1) * block)
                    add(grad_key, spot, wide(grad_scores[:, cols], query_m[here], ((0,), (0,))))
                    add(grad_value, spot, wide(rounded[:, cols], upper_m[here], ((0,), (0,))))
        for part, pieces in enumerate((grad_query, grad_key, grad_value)):
            for b in range(2):
                gtrip[
                    b * block : (b + 1) * block,
                    pl.ds(pl.multiple_of((part * pairs + hp) * width, width), width),
                ] = pieces[b].astype(jnp.bfloat16)

    for hp in range(pairs):
        attend_back_pair(hp)
        if hp == 0:
            reduce_z(D, [0])
        reduce_z(U, steps[hp - 1 : hp] if 0 < hp < nz - 1 else [])

    @pl.loop(0, 3)
    def _(i):
        product(
            Q,
            i,
            gtrip[:, pl.ds(pl.multiple_of(i * pairs * width, pairs * width), pairs * width)],
            full[0],
        )

    reduce_z(U, steps[pairs - 1 :])
    for h in range(2):
        tmp[parts[h]] = wide(
            gtrip[parts[h]], wq[...].reshape(groups * width, 2 * half), ((1,), (0,))
        )
        collect_start(3, h)
    reduce_x(O)
    reduce_x(Q)
    reduce_z(U, [0])
    for h in range(2):
        middle[parts[h]] = middle[parts[h]] + collect_wait(2, h)
    to_hbm(middle, out_ref, 4)
    reduce_z(O, steps + [0])
    reduce_z(Q, steps[:-1])
    for h in range(2):
        rows = parts[h]
        grad_one, normal = collect_wait(3, h), normal_one[rows]
        tmp[rows, 0:half] = grad_one
        ns[0, 0:1] += jnp.sum(grad_one * normal, axis=0, keepdims=True)
        ns[0, 1:2] += jnp.sum(grad_one, axis=0, keepdims=True)
        back_stats(grad_one, normal, gain_one, 3, h)
        swap_stats(3, h)
    pending.append(push(ns.at[0], nr.at[0], NS, NS, far(c)))
    reduce_z(Q, steps[-1:])
    arrived(nr.at[0], NS)
    ns[1] = ns[0] + nr[0]
    pending.append(push(ns.at[1], nr.at[1], NS + 1, NS + 1, x_peer))
    for h in range(2):
        rows = parts[h]
        mgrad[rows] += finish_back(
            tmp[rows, 0:half], normal_one[rows], inverse[0, rows], gain_one, 3, h
        )
    to_hbm(mgrad, back_ref, 5)
    arrived(nr.at[1], NS + 1)
    ns[2] = ns[1] + nr[1]
    for step in range(1, nz):
        pending.append(
            push(ns.at[2], nr.at[2 + z], NS + 2 + step, NS + 2 + z, at_z((z + step) % nz))
        )
    nr[2 + z] = ns[2]
    reduce_z(Q, [0])
    for p in (D, U, O, Q):
        reduce_end(p)
    for step in range(1, nz):
        zz = (z + step) % nz
        arrived(nr.at[2 + zz], NS + 2 + zz)
    total = nr[2]
    for zz in range(1, nz):
        total = total + nr[2 + zz]
    total_norm[...] = total * factor
    to_hbm(total_norm, norm_sum_ref, 6)

    for copy in pending:
        copy.wait_send()
    for flag, copy in guarded:

        @pl.when(flag)
        def _():
            copy.wait_send()

    for copy in writes:
        copy.wait()


def adam_values(weight, grad, first, second, decay):
    first_moment = beta_one * first + (1.0 - beta_one) * grad
    second_moment = beta_two * second + (1.0 - beta_two) * grad * grad
    step_size = (
        first_moment
        / (1.0 - beta_one**STEP)
        / (jnp.sqrt(second_moment / (1.0 - beta_two**STEP)) + adam_eps)
    )
    return weight - learn_rate * (step_size + decay * weight), first_moment, second_moment


def adam_kernel(*refs):
    ins, outs = refs[:17], refs[17:34]
    held, made, in_sem, out_sem = refs[34:51], refs[51:66], refs[66], refs[67]
    reads = [pltpu.make_async_copy(ins[i], held[i], in_sem.at[i]) for i in range(17)]
    order = (3, 4, 1, 2, 0)
    for i in order:
        for k in (i, 5 + i, 10 + i):
            reads[k].start()
    for k in (15, 16):
        reads[k].start()
    writes = []

    def write(src, dst, k):
        copy = pltpu.make_async_copy(src, outs[dst], out_sem.at[k])
        copy.start()
        writes.append(copy)

    for i in order:
        for k in (i, 5 + i, 10 + i):
            reads[k].wait()
        weight, moments = held[5 + i], held[10 + i]
        grad = held[i][...]
        if i == 0:
            grad = grad[0 : weight.shape[0]]
        grad = grad.reshape(weight.shape)
        made[i][...] = grad
        write(made[i], 2 + i, i)
        new, first, second = adam_values(
            weight[...], grad, moments[0], moments[1], decay_rate if i else 0.0
        )
        made[5 + i][...] = new
        write(made[5 + i], 7 + i, 5 + i)
        made[10 + i][0] = first
        made[10 + i][1] = second
        write(made[10 + i], 12 + i, 10 + i)
    for k in (15, 16):
        reads[k].wait()
        write(held[k], k - 15, k)
    for copy in writes:
        copy.wait()


def on_device_fused(
    block_in,
    upstream,
    norm_params,
    w_qkv,
    w_attn,
    w_up,
    w_down,
    mom_norm,
    mom_qkv,
    mom_attn,
    mom_up,
    mom_down,
):
    low = LOW
    ndp = lax.axis_size("dp")
    nz = ndp // low
    tokens, half = block_in.shape
    pairs = w_qkv.shape[1] // 2
    per = w_qkv.shape[2]
    groups = 3 * pairs
    width = 2 * per * ndp
    hidden_rows = w_up.shape[0]
    hidden = hidden_rows * ndp
    tiles = hidden // HIDDEN_TILE
    token_count = tokens * ndp * lax.axis_size("row")
    bf, f32 = jnp.bfloat16, jnp.float32

    def both(kind_of):
        return [kind_of(p) for p in range(4)]

    def piece(p):
        return ((groups, pairs)[p], 2 * per, half) if p < 2 else (hidden_rows, half)

    def whole(p, cols):
        return ((groups, pairs)[p], ndp, 2 * per, cols) if p < 2 else (hidden, cols)

    scratch = (
        both(lambda p: pltpu.VMEM(piece(p), bf))
        + both(lambda p: pltpu.VMEM(whole(p, 2 * half), bf))
        + [
            pltpu.VMEM((4, tokens, 128), f32),
            pltpu.VMEM((4, tokens, 128), f32),
            pltpu.VMEM((4, tokens, half), bf),
            pltpu.VMEM((4, tokens, 2 * half), bf),
            pltpu.VMEM((4, 2, tokens, half), bf),
            pltpu.VMEM((4, 2, tokens, half), bf),
            pltpu.VMEM((2, tokens, half), f32),
            pltpu.VMEM((tokens, 2 * half), f32),
            pltpu.VMEM((tokens, 3 * pairs * width), bf),
            pltpu.VMEM((tokens, pairs * width), bf),
            pltpu.VMEM((2 * pairs, tokens, 1), f32),
            pltpu.VMEM((tokens, hidden), bf),
            pltpu.VMEM((tokens, hidden), bf),
            pltpu.VMEM((tokens, half), f32),
            pltpu.VMEM((tokens, half), f32),
            pltpu.VMEM((tokens, half), f32),
            pltpu.VMEM((2, tokens, 1), f32),
            pltpu.VMEM((tokens, pairs * width), bf),
            pltpu.VMEM((tokens, 3 * pairs * width), bf),
            pltpu.VMEM((tokens, half), f32),
        ]
        + both(lambda p: pltpu.VMEM(whole(p, half), f32))
        + both(lambda p: pltpu.VMEM(whole(p, half), bf))
        + both(lambda p: pltpu.VMEM(whole(p, half), bf))
        + both(lambda p: pltpu.VMEM((nz,) + piece(p), bf))
        + both(lambda p: pltpu.VMEM((nz,) + piece(p), bf))
        + both(lambda p: pltpu.VMEM(piece(p), f32))
        + [
            pltpu.VMEM((8, half), f32),
            pltpu.VMEM((3, 8, half), f32),
            pltpu.VMEM((2 + nz, 8, half), f32),
            pltpu.SemaphoreType.DMA((50 + 21 * nz,)),
            pltpu.SemaphoreType.DMA((50 + 21 * nz,)),
            pltpu.SemaphoreType.DMA((19,)),
        ]
    )
    vmem = pl.BlockSpec(memory_space=pltpu.VMEM)
    hbm = pl.BlockSpec(memory_space=pltpu.HBM)
    outs = (
        jax.ShapeDtypeStruct(block_in.shape, f32),
        jax.ShapeDtypeStruct(block_in.shape, f32),
        *both(lambda p: jax.ShapeDtypeStruct(piece(p), f32)),
        jax.ShapeDtypeStruct((8, half), f32),
    )
    block_out, input_grad, *totals = pl.pallas_call(
        functools.partial(step_kernel, nz, low, 1.0 / math.sqrt(token_count)),
        out_shape=outs,
        in_specs=[vmem] * 7,
        out_specs=[hbm] * len(outs),
        scratch_shapes=scratch,
        compiler_params=pltpu.CompilerParams(
            collective_id=0, has_side_effects=True, vmem_limit_bytes=VMEM_BYTES
        ),
    )(block_in, upstream, norm_params, w_qkv, w_attn, w_up, w_down)
    params = (norm_params, w_qkv, w_attn, w_up, w_down)
    moments = (mom_norm, mom_qkv, mom_attn, mom_up, mom_down)
    norm_total = totals.pop()
    operands = (norm_total, *totals, *params, *moments, block_out, input_grad)
    shapes = [
        jax.ShapeDtypeStruct(item.shape, f32)
        for item in (block_out, input_grad) + params * 2 + moments
    ]
    return pl.pallas_call(
        adam_kernel,
        out_shape=shapes,
        in_specs=[hbm] * len(operands),
        out_specs=[hbm] * len(shapes),
        scratch_shapes=[pltpu.VMEM(item.shape, f32) for item in operands]
        + [pltpu.VMEM(item.shape, f32) for item in shapes[2:]]
        + [pltpu.SemaphoreType.DMA((17,)), pltpu.SemaphoreType.DMA((17,))],
        compiler_params=pltpu.CompilerParams(vmem_limit_bytes=VMEM_BYTES),
    )(*operands)


def fits(block_in, w_qkv, w_up, ndp, nrow, ncol):
    return (
        nrow == 2
        and ncol == 2
        and ndp % LOW == 0
        and ndp <= 8
        and block_in.shape[0] == SEQ
        and w_qkv.shape[1] % 2 == 0
        and w_qkv.shape[2] == 8
        and (w_up.shape[0] * ndp) % HIDDEN_TILE == 0
        and w_up.shape[0] % 16 == 0
    )


def run_step(*args):
    sizes = [lax.axis_size(name) for name in ("dp", "row", "col")]
    if fits(args[0], args[3], args[5], *sizes):
        return on_device_fused(*args)
    return on_device(*args)


def solution(mesh):
    in_specs = (
        P(("dp", "row"), "col"),
        P(("dp", "row"), "col"),
        P(None, "col"),
        P(None, "row", "dp", "col"),
        P("row", "dp", "col"),
        P(("dp", "row"), "col"),
        P(("dp", "row"), "col"),
        P(None, None, "col"),
        P(None, None, "row", "dp", "col"),
        P(None, "row", "dp", "col"),
        P(None, ("dp", "row"), "col"),
        P(None, ("dp", "row"), "col"),
    )
    out_specs = (
        P(("dp", "row"), "col"),
        P(("dp", "row"), "col"),
        P(None, "col"),
        P(None, "row", "dp", "col"),
        P("row", "dp", "col"),
        P(("dp", "row"), "col"),
        P(("dp", "row"), "col"),
        P(None, "col"),
        P(None, "row", "dp", "col"),
        P("row", "dp", "col"),
        P(("dp", "row"), "col"),
        P(("dp", "row"), "col"),
        P(None, None, "col"),
        P(None, None, "row", "dp", "col"),
        P(None, "row", "dp", "col"),
        P(None, ("dp", "row"), "col"),
        P(None, ("dp", "row"), "col"),
    )
    return jax.shard_map(
        run_step, mesh=mesh, in_specs=in_specs, out_specs=out_specs, check_vma=False
    )
```

```python
import functools
import math

import jax
import jax.numpy as jnp
from jax import lax
from jax.experimental import pallas as pl
from jax.experimental.pallas import tpu as pltpu
from jax.sharding import PartitionSpec as P

SEQ = 512
STEP = 4
LOW = 2


norm_eps = 1e-05
adam_eps = 1e-08
beta_one = 0.9
beta_two = 0.95
learn_rate = 0.02
decay_rate = 0.1
gelu_coef = math.sqrt(2.0 / math.pi)
cubic_coef = 0.044715
masked_score = -1e30

group = ("row", "col")
swap_pair = [(0, 1), (1, 0)]
spread_first = [(1, 2), (2, 1)]
spread_second = [(0, 2), (3, 1), (1, 0), (2, 3)]
collect_second = [(dst, src) for src, dst in spread_second]


def smooth_pair(values):
    squared = values * values
    bent = jnp.tanh(gelu_coef * (values + cubic_coef * squared * values))
    smooth = 0.5 * values * (1.0 + bent)
    slope = 0.5 * (1.0 + bent) + 0.5 * values * (1.0 - bent * bent) * gelu_coef * (
        1.0 + 3.0 * cubic_coef * squared
    )
    return (smooth, slope)


def wide(left, right, dims):
    return lax.dot_general(left, right, (dims, ((), ())), preferred_element_type=jnp.float32)


def normalize(rows_in, gain_row, shift_row):
    count = rows_in.shape[1]
    mean_here = jnp.mean(rows_in, axis=1, keepdims=True)
    offset = rows_in - mean_here
    square_here = jnp.sum(offset * offset, axis=1, keepdims=True)
    there = lax.ppermute(jnp.concatenate([mean_here, square_here], axis=1), "col", swap_pair)
    gap = mean_here - there[:, :1]
    spread = (square_here + there[:, 1:] + gap * gap * (0.5 * count)) / (2.0 * count)
    inverse = lax.rsqrt(spread + norm_eps)
    normal = (rows_in - (mean_here - 0.5 * gap)) * inverse
    return (normal, inverse, (normal * gain_row + shift_row).astype(jnp.bfloat16))


def norm_back(grad_normed, normal, inverse, gain_row):
    count = 2.0 * grad_normed.shape[1]
    scaled = grad_normed * gain_row
    here = jnp.concatenate(
        [
            jnp.sum(scaled, axis=1, keepdims=True),
            jnp.sum(scaled * normal, axis=1, keepdims=True),
        ],
        axis=1,
    )
    total = (here + lax.ppermute(here, "col", swap_pair)) / count
    return inverse * (scaled - total[:, :1] - normal * total[:, 1:])


def pick(flag, one, other):
    return jnp.where(flag, one, other), jnp.where(flag, other, one)


def spread_rows(block):
    row, col = lax.axis_index("row"), lax.axis_index("col")
    first = lax.ppermute(block, group, spread_first)
    second = lax.ppermute(block, group, spread_second)
    first = jnp.where(row == col, block, first)
    low, high = pick(row == 0, first, second)
    return low, high


def collect_rows(low, high):
    row, col = lax.axis_index("row"), lax.axis_index("col")
    first, second = pick(row == 0, low, high)
    first_in = lax.ppermute(first.astype(jnp.bfloat16), group, spread_first)
    second_in = lax.ppermute(second.astype(jnp.bfloat16), group, collect_second)
    return jnp.where(row == col, first, first_in.astype(jnp.float32)) + second_in.astype(
        jnp.float32
    )


def out_project(rows, weight):
    half = weight.shape[1] // 2
    return collect_rows(
        wide(rows, weight[:, :half], ((1,), (0,))), wide(rows, weight[:, half:], ((1,), (0,)))
    )


def small_ring():
    size = lax.axis_size("dp")
    return size % LOW == 0 and size <= 8


def high_steps(sign):
    size = lax.axis_size("dp")
    high = size // LOW
    return [
        [(i, ((i // LOW + sign * step) % high) * LOW + i % LOW) for i in range(size)]
        for step in range(1, high)
    ]


def low_step():
    return [(i, i ^ 1) for i in range(lax.axis_size("dp"))]


def gather_weight(shard, axis):
    shard = shard.astype(jnp.bfloat16)
    if small_ring():
        near = jnp.concatenate(
            [shard] + [lax.ppermute(shard, "dp", perm) for perm in high_steps(1)], axis=axis
        )
        block = jnp.concatenate([near, lax.ppermute(near, "dp", low_step())], axis=axis)
    else:
        block = lax.all_gather(shard, "dp", axis=axis, tiled=True)
    there = lax.ppermute(block, "col", swap_pair)
    low, high = pick(lax.axis_index("col") == 0, block, there)
    return jnp.concatenate([low, high], axis=-1)


def reduce_weight(make, axis):
    away = make(False).astype(jnp.bfloat16)
    total = make(True) + lax.ppermute(away, "col", swap_pair).astype(jnp.float32)
    if not small_ring():
        return lax.psum_scatter(total, "dp", scatter_dimension=axis, tiled=True)
    near, far = jnp.split(total, 2, axis=axis)
    near = near + lax.ppermute(far.astype(jnp.bfloat16), "dp", low_step()).astype(jnp.float32)
    own, *rest = jnp.split(near, lax.axis_size("dp") // LOW, axis=axis)
    for piece, perm in zip(rest, high_steps(-1)):
        own = own + lax.ppermute(piece.astype(jnp.bfloat16), "dp", perm).astype(jnp.float32)
    return own


def sum_everywhere(terms):
    if not small_ring():
        return lax.psum(terms, ("dp", "row"))
    terms = terms + lax.ppermute(terms, "row", swap_pair)
    terms = terms + lax.ppermute(terms, "dp", low_step())
    moved = [lax.ppermute(terms, "dp", perm) for perm in high_steps(1)]
    for piece in moved:
        terms = terms + piece
    return terms


def head_scores(triples_ref, heads, size, head):
    width = heads * size
    query = triples_ref[:, head * size : (head + 1) * size]
    key = triples_ref[:, width + head * size : width + (head + 1) * size]
    value = triples_ref[:, 2 * width + head * size : 2 * width + (head + 1) * size]
    scores = wide(query, key, ((1,), (1,))) * (1.0 / math.sqrt(size))
    length = scores.shape[0]
    allowed = lax.broadcasted_iota(jnp.int32, (length, length), 0) >= lax.broadcasted_iota(
        jnp.int32, (length, length), 1
    )
    return query, key, value, jnp.where(allowed, scores, masked_score)


def attend_kernel(heads, size, triples_ref, mixed_ref, total_ref):
    for head in range(heads):
        _, _, value, scores = head_scores(triples_ref, heads, size, head)
        highest = jnp.max(scores, axis=1, keepdims=True)
        log_total = highest + jnp.log(jnp.sum(jnp.exp(scores - highest), axis=1, keepdims=True))
        probs = jnp.exp(scores - log_total).astype(jnp.bfloat16)
        mixed_ref[:, head * size : (head + 1) * size] = wide(probs, value, ((1,), (0,))).astype(
            jnp.bfloat16
        )
        total_ref[:, head : head + 1] = log_total


def attend_back_kernel(heads, size, triples_ref, grad_ref, total_ref, out_ref):
    width = heads * size
    scale = 1.0 / math.sqrt(size)
    for head in range(heads):
        query, key, value, scores = head_scores(triples_ref, heads, size, head)
        grad_mixed = grad_ref[:, head * size : (head + 1) * size]
        probs = jnp.exp(scores - total_ref[:, head : head + 1])
        grad_values = wide(probs.astype(jnp.bfloat16), grad_mixed, ((0,), (0,)))
        grad_probs = wide(grad_mixed, value, ((1,), (1,)))
        delta = jnp.sum(probs * grad_probs, axis=1, keepdims=True)
        grad_scores = (probs * (grad_probs - delta) * scale).astype(jnp.bfloat16)
        for part, piece in enumerate(
            (
                wide(grad_scores, key, ((1,), (0,))),
                wide(grad_scores, query, ((0,), (0,))),
                grad_values,
            )
        ):
            start = part * width + head * size
            out_ref[:, start : start + size] = piece.astype(jnp.bfloat16)


def by_sequence(kernel, operands, outs):
    rows = operands[0].shape[0]

    def spec(shape):
        return pl.BlockSpec((SEQ, shape[1]), lambda step: (step, 0))

    return pl.pallas_call(
        kernel,
        grid=(rows // SEQ,),
        in_specs=[spec(item.shape) for item in operands],
        out_specs=[spec(item.shape) for item in outs],
        out_shape=outs,
        compiler_params=pltpu.CompilerParams(vmem_limit_bytes=40 * 1024 * 1024),
        cost_estimate=pl.CostEstimate(
            flops=rows * SEQ * 2048, bytes_accessed=rows * 8192, transcendentals=rows * SEQ * 6
        ),
    )(*operands)


def adam_step(weight, grad, moments, decay):
    first_moment = beta_one * moments[0] + (1.0 - beta_one) * grad
    second_moment = beta_two * moments[1] + (1.0 - beta_two) * grad * grad
    step_size = (
        first_moment
        / (1.0 - beta_one**STEP)
        / (jnp.sqrt(second_moment / (1.0 - beta_two**STEP)) + adam_eps)
    )
    return (
        weight - learn_rate * (step_size + decay * weight),
        jnp.stack([first_moment, second_moment]),
    )


def on_device(
    block_in,
    upstream,
    norm_params,
    w_qkv,
    w_attn,
    w_up,
    w_down,
    mom_norm,
    mom_qkv,
    mom_attn,
    mom_up,
    mom_down,
):
    heads = w_qkv.shape[1]
    size = w_qkv.shape[2] * lax.axis_size("dp")
    width = heads * size
    at_low = lax.axis_index("col") == 0

    normal_one, inverse_one, normed_one = normalize(block_in, norm_params[0], norm_params[1])
    qkv_mat = gather_weight(w_qkv, 2).reshape(3 * width, -1)
    one_low, one_high = spread_rows(normed_one)
    attn_mat = gather_weight(w_attn, 1).reshape(width, -1)
    up_mat = gather_weight(w_up, 0)
    up_low, up_high = spread_rows(upstream.astype(jnp.bfloat16))
    down_mat = gather_weight(w_down, 0)

    triples = wide(
        jnp.concatenate([one_low, one_high], axis=1), qkv_mat, ((1,), (1,))
    ).astype(jnp.bfloat16)
    mixed, log_total = by_sequence(
        functools.partial(attend_kernel, heads, size),
        (triples,),
        (
            jax.ShapeDtypeStruct((triples.shape[0], width), jnp.bfloat16),
            jax.ShapeDtypeStruct((triples.shape[0], heads), jnp.float32),
        ),
    )
    middle = block_in + out_project(mixed, attn_mat)
    normal_two, inverse_two, normed_two = normalize(middle, norm_params[2], norm_params[3])
    two_low, two_high = spread_rows(normed_two)
    grad_hidden = wide(jnp.concatenate([up_low, up_high], axis=1), down_mat, ((1,), (1,)))
    hidden_pre = wide(jnp.concatenate([two_low, two_high], axis=1), up_mat, ((1,), (1,)))
    activated, slope = smooth_pair(hidden_pre)
    activated = activated.astype(jnp.bfloat16)
    grad_pre = (grad_hidden * slope).astype(jnp.bfloat16)
    grad_normed_two = out_project(grad_pre, up_mat)
    block_out = middle + out_project(activated, down_mat)

    def products(left, low, high):
        own, away = pick(at_low, low, high)
        return lambda mine: wide(left, own if mine else away, ((0,), (0,)))

    grad_down = reduce_weight(products(activated, up_low, up_high), 0)
    grad_up = reduce_weight(products(grad_pre, two_low, two_high), 0)
    middle_grad = upstream + norm_back(grad_normed_two, normal_two, inverse_two, norm_params[2])
    mid_low, mid_high = spread_rows(middle_grad.astype(jnp.bfloat16))
    grad_mixed = wide(
        jnp.concatenate([mid_low, mid_high], axis=1), attn_mat, ((1,), (1,))
    ).astype(jnp.bfloat16)

    def by_head(make, parts):
        return lambda mine: make(mine).reshape(*parts, heads, size, -1)

    grad_attn = reduce_weight(by_head(products(mixed, mid_low, mid_high), ()), 1)
    (grad_triples,) = by_sequence(
        functools.partial(attend_back_kernel, heads, size),
        (triples, grad_mixed, log_total),
        (jax.ShapeDtypeStruct(triples.shape, jnp.bfloat16),),
    )
    grad_qkv = reduce_weight(by_head(products(grad_triples, one_low, one_high), (3,)), 2)
    grad_normed_one = out_project(grad_triples, qkv_mat)
    input_grad = middle_grad + norm_back(grad_normed_one, normal_one, inverse_one, norm_params[0])
    norm_terms = jnp.stack(
        [
            jnp.sum(grad_normed_one * normal_one, axis=0),
            jnp.sum(grad_normed_one, axis=0),
            jnp.sum(grad_normed_two * normal_two, axis=0),
            jnp.sum(grad_normed_two, axis=0),
        ]
    )
    grad_norm = sum_everywhere(norm_terms)
    token_count = block_in.shape[0] * lax.axis_size("dp") * lax.axis_size("row")
    factor = 1.0 / math.sqrt(token_count)
    grad_norm = grad_norm * factor
    grad_qkv = grad_qkv * factor
    grad_attn = grad_attn * factor
    grad_up = grad_up * factor
    grad_down = grad_down * factor
    new_norm, new_mom_norm = adam_step(norm_params, grad_norm, mom_norm, 0.0)
    new_qkv, new_mom_qkv = adam_step(w_qkv, grad_qkv, mom_qkv, decay_rate)
    new_attn, new_mom_attn = adam_step(w_attn, grad_attn, mom_attn, decay_rate)
    new_up, new_mom_up = adam_step(w_up, grad_up, mom_up, decay_rate)
    new_down, new_mom_down = adam_step(w_down, grad_down, mom_down, decay_rate)
    return (
        block_out,
        input_grad,
        grad_norm,
        grad_qkv,
        grad_attn,
        grad_up,
        grad_down,
        new_norm,
        new_qkv,
        new_attn,
        new_up,
        new_down,
        new_mom_norm,
        new_mom_qkv,
        new_mom_attn,
        new_mom_up,
        new_mom_down,
    )


MESH = pl.DeviceIdType.MESH
VMEM_BYTES = 67043328
HIDDEN_TILE = 256


def causal(rows, cols, first):
    return (
        lax.broadcasted_iota(jnp.int32, (rows, cols), 0) + first
        >= lax.broadcasted_iota(jnp.int32, (rows, cols), 1)
    )


def head_masks(per, width):
    lane = lax.broadcasted_iota(jnp.int32, (1, width), 1)
    return [
        jnp.where((lane // per) % 2 == part, 1.0, 0.0).astype(jnp.bfloat16) for part in range(2)
    ]


def row_stats(first, second, width=128):
    lane = lax.broadcasted_iota(jnp.int32, (first.shape[0], width), 1)
    return jnp.where(lane == 0, first, second)


def step_kernel(
    nz,
    low,
    factor,
    block_ref,
    up_ref,
    norm_ref,
    wqkv_ref,
    wattn_ref,
    wup_ref,
    wdown_ref,
    out_ref,
    back_ref,
    sum_q_ref,
    sum_o_ref,
    sum_u_ref,
    sum_d_ref,
    norm_sum_ref,
    shard_q,
    shard_o,
    shard_u,
    shard_d,
    wq,
    wo,
    wu,
    wd,
    stat_s,
    stat_r,
    spread_s,
    full,
    col_s,
    col_r,
    keep,
    tmp,
    trip,
    mixed,
    lse,
    act,
    gpre,
    middle,
    normal_one,
    normal_two,
    inverse,
    gmix,
    gtrip,
    mgrad,
    gq,
    go,
    gu,
    gd,
    gsq,
    gso,
    gsu,
    gsd,
    grq,
    gro,
    gru,
    grd,
    xrq,
    xro,
    xru,
    xrd,
    zrq,
    zro,
    zru,
    zrd,
    total_q,
    total_o,
    total_u,
    total_d,
    total_norm,
    ns,
    nr,
    send,
    recv,
    local,
):
    dp, r, c = lax.axis_index("dp"), lax.axis_index("row"), lax.axis_index("col")
    z, x = dp // low, dp % low
    same = r == c
    tokens, half = block_ref.shape
    per = wqkv_ref.shape[2]
    pairs = wqkv_ref.shape[1] // 2
    width = 2 * per * nz * low
    ndp = nz * low
    hidden_rows = wup_ref.shape[0]
    hidden = hidden_rows * ndp
    tiles = hidden // HIDDEN_TILE
    groups = 3 * pairs
    Q, O, U, D = range(4)

    STAT, SPR, COL, GZ = 0, 8, 24, 40
    GX = GZ + 4 * nz
    GC = GX + 4 * nz
    RC = GC + 4
    RX = RC + 4
    RZ = RX + 4 * nz
    NS = RZ + 4 * nz
    GD = NS + 2 + nz

    def at_z(zz):
        return {"dp": zz * low + x}

    x_peer = {"dp": z * low + 1 - x}
    partner = {"col": 1 - c}

    def far(other):
        return {"row": 1 - r, "col": other}

    def feat(f):
        return pl.ds(pl.multiple_of(f * half, half), half)

    mine, other = feat(c), feat(1 - c)
    pending = []
    writes = []
    guarded = []

    def describe(src, dst, s, q, where):
        return pltpu.make_async_remote_copy(
            src_ref=src,
            dst_ref=dst,
            send_sem=send.at[s],
            recv_sem=recv.at[q],
            device_id=where,
            device_id_type=MESH,
        )

    def push(src, dst, s, q, where):
        copy = describe(src, dst, s, q, where)
        copy.start()
        return copy

    def arrived(dst, q):
        describe(dst, dst, q, q, partner).wait_recv()

    weights = (wq, wo, wu, wd)

    def slot(p, owner, f):
        if p < 2:
            return weights[p].at[:, owner, :, feat(f)]
        rows = pl.ds(pl.multiple_of(owner * hidden_rows, hidden_rows), hidden_rows)
        return weights[p].at[rows, feat(f)]

    shards = (shard_q, shard_o, shard_u, shard_d)

    shard_q[...] = wqkv_ref[...].reshape(groups, 2 * per, half).astype(jnp.bfloat16)
    shard_o[...] = wattn_ref[...].reshape(pairs, 2 * per, half).astype(jnp.bfloat16)
    shard_u[...] = wup_ref[...].astype(jnp.bfloat16)
    shard_d[...] = wdown_ref[...].astype(jnp.bfloat16)

    block = tokens // 2
    parts = [slice(h * block, (h + 1) * block) for h in range(2)]

    def local_stats(rows_in, k, h):
        mean_here = jnp.mean(rows_in, axis=1, keepdims=True)
        offset = rows_in - mean_here
        square_here = jnp.sum(offset * offset, axis=1, keepdims=True)
        stat_s[k, parts[h]] = row_stats(mean_here, square_here)

    def swap_stats(k, h):
        spot = STAT + 2 * k + h
        pending.append(
            push(stat_s.at[k, parts[h]], stat_r.at[k, parts[h]], spot, spot, partner)
        )

    def finish_norm(rows_in, k, h, gain, shift, normal_ref, inverse_index, out):
        rows = parts[h]
        arrived(stat_r.at[k, rows], STAT + 2 * k + h)
        here, there = stat_s[k, rows], stat_r[k, rows]
        mean_here, square_here = here[:, 0:1], here[:, 1:2]
        gap = mean_here - there[:, 0:1]
        spread = (square_here + there[:, 1:2] + gap * gap * (0.5 * half)) / (2.0 * half)
        inv = lax.rsqrt(spread + norm_eps)
        normal = (rows_in - (mean_here - 0.5 * gap)) * inv
        normal_ref[rows] = normal
        inverse[inverse_index, rows] = inv
        out[rows] = (normal * gain + shift).astype(jnp.bfloat16)

    def back_stats(grad, normal, gain, k, h):
        scaled = grad * gain
        stat_s[k, parts[h]] = row_stats(
            jnp.sum(scaled, axis=1, keepdims=True),
            jnp.sum(scaled * normal, axis=1, keepdims=True),
        )

    def finish_back(grad, normal, inv, gain, k, h):
        rows = parts[h]
        arrived(stat_r.at[k, rows], STAT + 2 * k + h)
        total = (stat_s[k, rows] + stat_r[k, rows]) / (2.0 * half)
        return inv * (grad * gain - total[:, 0:1] - normal * total[:, 1:2])

    def spread_spot(k, f, h):
        return SPR + (2 * k + f) * 2 + h

    def spread_start(k, h):
        rows = parts[h]
        src = spread_s.at[k, rows]
        dst = full.at[k, rows, mine]
        pending.append(push(src, dst, spread_spot(k, 0, h), spread_spot(k, c, h), far(r)))

        @pl.when(same)
        def _():
            pltpu.make_async_copy(src, dst, local.at[4 + 2 * k + h]).start()

        @pl.when(jnp.logical_not(same))
        def _():
            push(src, dst, spread_spot(k, 1, h), spread_spot(k, c, h), partner)

    def spread_wait(k):
        for h in range(2):
            rows = parts[h]
            src = spread_s.at[k, rows]
            dst = full.at[k, rows, mine]
            arrived(full.at[k, rows, other], spread_spot(k, 1 - c, h))

            @pl.when(same)
            def _():
                pltpu.make_async_copy(src, dst, local.at[4 + 2 * k + h]).wait()

            @pl.when(jnp.logical_not(same))
            def _():
                arrived(dst, spread_spot(k, c, h))
                describe(
                    src, dst, spread_spot(k, 1, h), spread_spot(k, c, h), partner
                ).wait_send()

    def collect_spot(k, f, h):
        return COL + (2 * k + f) * 2 + h

    def collect_start(k, h):
        rows = parts[h]
        col_s[k, 0, rows] = tmp[rows, other].astype(jnp.bfloat16)
        col_s[k, 1, rows] = tmp[rows, mine].astype(jnp.bfloat16)

        @pl.when(same)
        def _():
            keep[k % 2, rows] = tmp[rows, mine]
            spot = collect_spot(k, 0, h)
            push(col_s.at[k, 0, rows], col_r.at[k, 0, rows], spot, spot, partner)

        @pl.when(jnp.logical_not(same))
        def _():
            for f, where in enumerate((far(1 - c), far(c))):
                push(
                    col_s.at[k, f, rows],
                    col_r.at[k, 1, rows],
                    collect_spot(k, f, h),
                    collect_spot(k, 1, h),
                    where,
                )

    def collect_wait(k, h):
        rows = parts[h]
        arrived(col_r.at[k, 1, rows], collect_spot(k, 1, h))

        def sent(f):
            spot = collect_spot(k, f, h)
            describe(
                col_s.at[k, f, rows], col_r.at[k, f, rows], spot, spot, partner
            ).wait_send()

        @pl.when(same)
        def _():
            sent(0)

        @pl.when(jnp.logical_not(same))
        def _():
            arrived(col_r.at[k, 0, rows], collect_spot(k, 0, h))
            keep[k % 2, rows] = col_r[k, 0, rows].astype(jnp.float32)
            sent(0)
            sent(1)

        return keep[k % 2, rows] + col_r[k, 1, rows].astype(jnp.float32)

    def relay(p, zz, up, src):
        dst = slot(p, zz * low + x, c)
        spot = (GZ if up else GD) + p * nz + zz
        to = at_z((z + 1) % nz) if up else at_z((z + nz - 1) % nz)
        return describe(dst if src is None else src, dst, spot, GZ + p * nz + zz, to)

    def guard(flag, copy):
        @pl.when(flag)
        def _():
            copy.start()

        guarded.append((flag, copy))

    def gather_own_z(p):
        guard(z < nz - 1, relay(p, z, True, shards[p]))
        guard(z > 0, relay(p, z, False, shards[p]))

    def x_copy(p, zz, src):
        dst = slot(p, zz * low + x, c)
        spot = GX + p * nz + zz
        return describe(dst if src is None else src, dst, spot, spot, x_peer)

    def gather_own_x(p):
        x_copy(p, z, shards[p]).start()
        for step in range(nz):
            pending.append(x_copy(p, (z + step) % nz, None))

    def band(p, cols):
        return weights[p].at[:, :, :, cols] if p < 2 else weights[p].at[:, cols]

    def to_partner(p, owner):
        push(slot(p, owner, c), slot(p, owner, c), GC + p, GC + p, partner)

    def gather_own_c(p):
        pltpu.make_async_copy(shards[p], slot(p, dp, c), local.at[p]).start()
        push(shards[p], slot(p, dp, c), GC + p, GC + p, partner)
        pending.append(describe(band(p, mine), band(p, mine), GC + p, GC + p, partner))

    steps = list(range(1, nz))
    def by_distance(far_z, serve):
        below, above = (z + nz - far_z) % nz, (z + far_z) % nz

        @pl.when(z >= far_z)
        def _():
            serve(below, True)

        @pl.when(z + far_z < nz)
        def _():
            serve(above, False)

    def gather_z(p, some):
        def serve(zz, up):
            owner = zz * low + x
            arrived(slot(p, owner, c), GZ + p * nz + zz)
            x_copy(p, zz, None).start()

            @pl.when((z < nz - 1) if up else (z > 0))
            def _():
                relay(p, zz, up, None).start()

            to_partner(p, owner)

        for far_z in some:
            by_distance(far_z, serve)
            for zz, up, flag in (
                ((z + nz - far_z) % nz, True, jnp.logical_and(z >= far_z, z < nz - 1)),
                ((z + far_z) % nz, False, jnp.logical_and(z + far_z < nz, z > 0)),
            ):
                guarded.append((flag, relay(p, zz, up, None)))

    def gather_x(p):
        def serve(zz, up):
            owner = zz * low + 1 - x
            arrived(slot(p, owner, c), GX + p * nz + zz)
            to_partner(p, owner)

        serve(z, True)
        for far_z in steps:
            by_distance(far_z, serve)

    def gather_c(p):
        pltpu.make_async_copy(shards[p], slot(p, dp, c), local.at[p]).wait()
        arrived(band(p, other), GC + p)

    sums = (gq, go, gu, gd)
    away = (gsq, gso, gsu, gsd)
    near = (grq, gro, gru, grd)
    from_x = (xrq, xro, xru, xrd)
    from_z = (zrq, zro, zru, zrd)
    totals = (total_q, total_o, total_u, total_d)
    results = (sum_q_ref, sum_o_ref, sum_u_ref, sum_d_ref)

    def index(p, owner):
        if p < 2:
            return (slice(None), owner)
        return (pl.ds(pl.multiple_of(owner * hidden_rows, hidden_rows), hidden_rows),)

    def rows_of(p, i):
        if p < 2:
            return pl.ds(i * pairs, pairs)
        return pl.ds(pl.multiple_of(i * HIDDEN_TILE, HIDDEN_TILE), HIDDEN_TILE)

    def swap_chunk(p, i):
        rows = rows_of(p, i)
        return describe(
            away[p].at[rows], near[p].at[rows], RC + p, RC + p, partner
        )

    def product(p, i, left, right):
        tmp_rows = left.shape[1]
        tmp[0:tmp_rows] = wide(left, right, ((0,), (0,)))
        rows = rows_of(p, i)
        own, gone = tmp[0:tmp_rows, mine], tmp[0:tmp_rows, other].astype(jnp.bfloat16)
        if p < 2:
            own = own.reshape(pairs, ndp, 2 * per, half)
            gone = gone.reshape(pairs, ndp, 2 * per, half)
        sums[p][rows] = own
        away[p][rows] = gone
        swap_chunk(p, i).start()

    inner, upper = z * (nz - 1 - z) // 2, z // 2

    def target(step):
        if step == 0:
            return z
        place = (1 - inner) * (nz - step) + inner * (2, 0, 3)[step - 1]
        return place + upper * (nz - 1 - 2 * place)

    def reduce_x(p):
        describe(away[p], near[p], RC + p, RC + p, partner).wait()
        for step in steps + [0]:
            zz = target(step)
            at = index(p, zz * low + 1 - x)
            total = sums[p][at] + near[p][at].astype(jnp.float32)
            away[p][at] = total.astype(jnp.bfloat16)
            pending.append(
                push(
                    away[p].at[at],
                    from_x[p].at[zz],
                    RX + p * nz + step,
                    RX + p * nz + zz,
                    x_peer,
                )
            )

    def reduce_z(p, some):
        for step in some:
            zz = target(step)
            at = index(p, zz * low + x)
            arrived(from_x[p].at[zz], RX + p * nz + zz)
            if step == nz - 1:

                @pl.when(inner == 1)
                def _():
                    arrived(from_z[p].at[z], RZ + p * nz + z)
                    sums[p][at] = sums[p][at] + from_z[p][z].astype(jnp.float32)

            total = (
                sums[p][at] + near[p][at].astype(jnp.float32) + from_x[p][zz].astype(jnp.float32)
            )
            if step == 0:
                sums[p][at] = total
                continue
            away[p][at] = total.astype(jnp.bfloat16)
            to, spot = zz, z
            if step == 1:
                to = inner * zz + (1 - inner) * (1 + upper)
                spot = inner * z + (1 - inner) * (1 + upper)
            pending.append(
                push(
                    away[p].at[at],
                    from_z[p].at[spot],
                    RZ + p * nz + step,
                    RZ + p * nz + spot,
                    at_z(to),
                )
            )

    def reduce_end(p):
        totals[p][...] = sums[p][index(p, dp)]
        for step in range(1, nz):
            zz = (z + step) % nz

            @pl.when((zz - z) * (zz - z) < (nz - 1) * (nz - 1))
            def _():
                arrived(from_z[p].at[zz], RZ + p * nz + zz)
                totals[p][...] = totals[p][...] + from_z[p][zz].astype(jnp.float32)

        totals[p][...] = totals[p][...] * factor
        to_hbm(totals[p], results[p], p)

    def to_hbm(src, dst, i):
        copy = pltpu.make_async_copy(src, dst, local.at[12 + i])
        copy.start()
        writes.append(copy)

    gain_one, shift_one = norm_ref[0:1], norm_ref[1:2]
    gain_two, shift_two = norm_ref[2:3], norm_ref[3:4]

    barrier = pltpu.get_barrier_semaphore()
    peers = [at_z((z + step) % nz) for step in range(1, nz)] + [
        x_peer,
        partner,
        far(c),
        far(1 - c),
    ]
    for peer in peers:
        pl.semaphore_signal(barrier, inc=1, device_id=peer, device_id_type=MESH)
    for h in range(2):
        local_stats(block_ref[parts[h]], 0, h)
    pl.semaphore_wait(barrier, len(peers))

    gather_own_z(Q)
    gather_own_x(Q)
    for h in range(2):
        swap_stats(0, h)
    gather_own_c(Q)
    gather_own_z(O)
    gather_own_x(O)
    for h in range(2):
        finish_norm(
            block_ref[parts[h]], 0, h, gain_one, shift_one, normal_one, 0, spread_s.at[0]
        )
        spread_start(0, h)
    spread_s[1] = up_ref[...].astype(jnp.bfloat16)
    for h in range(2):
        spread_start(1, h)
    for far_z in steps[:-1]:
        gather_z(Q, [far_z])
        gather_z(O, [far_z])
    gather_own_x(U)
    gather_own_z(U)
    gather_own_z(D)
    gather_z(Q, steps[-1:])
    gather_z(O, steps[-1:])
    gather_own_x(D)
    gather_own_c(O)
    gather_x(Q)
    gather_own_c(U)
    gather_own_c(D)
    gather_c(Q)
    spread_wait(0)
    gather_z(U, steps[:1])

    trip[...] = wide(
        full[0], wq[...].reshape(groups * width, 2 * half), ((1,), (1,))
    ).astype(jnp.bfloat16)

    gather_x(O)
    gather_z(D, steps[:1])

    scale = 1.0 / math.sqrt(width // 2)
    masks = head_masks(per, width)

    def part_of(ref, part, hp):
        return ref[:, pl.ds(pl.multiple_of((part * pairs + hp) * width, width), width)]

    def attend_pair(hp):
        query, key, value = (part_of(trip, part, hp) for part in range(3))
        rows = [None, None]
        for head in range(2):
            query_m, value_m = query * masks[head], value * masks[head]
            for b in range(2):
                n = (b + 1) * block
                scores = wide(query_m[b * block : n], key[:n], ((1,), (1,))) * scale
                scores = jnp.where(causal(block, n, b * block), scores, masked_score)
                highest = jnp.max(scores, axis=1, keepdims=True)
                raised = jnp.exp(scores - highest)
                total = jnp.sum(raised, axis=1, keepdims=True)
                lse[hp * 2 + head, b * block : n] = highest + jnp.log(total)
                probs = (raised * (1.0 / total)).astype(jnp.bfloat16)
                got = wide(probs, value_m[:n], ((1,), (0,)))
                rows[b] = got if rows[b] is None else rows[b] + got
        for b in range(2):
            mixed[b * block : (b + 1) * block, pl.ds(pl.multiple_of(hp * width, width), width)] = (
                rows[b].astype(jnp.bfloat16)
            )

    def attn_weight():
        return wo[...].reshape(pairs * width, 2 * half)

    for hp in range(pairs):
        attend_pair(hp)
        if hp == pairs - 2:
            gather_z(U, steps[1:2])
    gather_c(O)
    tmp[...] = wide(mixed[...], attn_weight(), ((1,), (0,)))
    for h in range(2):
        collect_start(0, h)
    gather_z(D, steps[1:2])
    gather_z(U, steps[2:])
    gather_z(D, steps[2:])
    for h in range(2):
        middle[parts[h]] = block_ref[parts[h]] + collect_wait(0, h)
        local_stats(middle[parts[h]], 1, h)
        swap_stats(1, h)
        finish_norm(
            middle[parts[h]], 1, h, gain_two, shift_two, normal_two, 1, spread_s.at[2]
        )
        spread_start(2, h)
        gather_x((U, D)[h])
    gather_c(U)
    gather_c(D)
    spread_wait(1)
    spread_wait(2)

    def tile(i):
        return pl.ds(pl.multiple_of(i * HIDDEN_TILE, HIDDEN_TILE), HIDDEN_TILE)

    @pl.loop(0, tiles)
    def _(i):
        pre = wide(full[2], wu[tile(i)], ((1,), (1,)))
        grad = wide(full[1], wd[tile(i)], ((1,), (1,)))
        smooth, slope = smooth_pair(pre)
        act[:, tile(i)] = smooth.astype(jnp.bfloat16)
        gpre[:, tile(i)] = (grad * slope).astype(jnp.bfloat16)

    tmp[...] = wide(gpre[...], wu[...], ((1,), (0,)))
    for h in range(2):
        collect_start(1, h)

    @pl.loop(0, tiles)
    def _(i):
        product(D, i, act[:, tile(i)], full[1])

    @pl.loop(0, tiles // 2)
    def _(i):
        product(U, i, gpre[:, tile(i)], full[2])

    reduce_x(D)

    @pl.loop(tiles // 2, tiles)
    def _(i):
        product(U, i, gpre[:, tile(i)], full[2])

    ns[0] = jnp.zeros((8, half), jnp.float32)
    for h in range(2):
        rows = parts[h]
        grad_two, normal = collect_wait(1, h), normal_two[rows]
        back_stats(grad_two, normal, gain_two, 2, h)
        swap_stats(2, h)
        ns[0, 2:3] += jnp.sum(grad_two * normal, axis=0, keepdims=True)
        ns[0, 3:4] += jnp.sum(grad_two, axis=0, keepdims=True)
        grad = up_ref[rows] + finish_back(grad_two, normal, inverse[1, rows], gain_two, 2, h)
        mgrad[rows] = grad
        spread_s[3, rows] = grad.astype(jnp.bfloat16)
        spread_start(3, h)
        if h == 0:
            reduce_z(D, steps[:1])
    reduce_x(U)
    reduce_z(D, steps[1:2])
    tmp[...] = wide(act[...], wd[...], ((1,), (0,)))
    for h in range(2):
        collect_start(2, h)
    reduce_z(D, steps[-1:])
    spread_wait(3)

    gmix[...] = wide(full[3], attn_weight(), ((1,), (1,))).astype(jnp.bfloat16)
    product(O, 0, mixed[...], full[3])

    def attend_back_pair(hp):
        query, key, value = (part_of(trip, part, hp) for part in range(3))
        upper = gmix[:, pl.ds(pl.multiple_of(hp * width, width), width)]
        grad_query = [None, None]
        grad_key = [None, None]
        grad_value = [None, None]

        def add(total, spot, term):
            total[spot] = term if total[spot] is None else total[spot] + term

        for head in range(2):
            query_m, key_m = query * masks[head], key * masks[head]
            upper_m = upper * masks[head]
            for b in range(2):
                n = (b + 1) * block
                here = slice(b * block, n)
                scores = wide(query_m[here], key[:n], ((1,), (1,))) * scale
                scores = jnp.where(causal(block, n, b * block), scores, masked_score)
                probs = jnp.exp(scores - lse[hp * 2 + head, b * block : n])
                rounded = probs.astype(jnp.bfloat16)
                grad_probs = wide(upper_m[here], value[:n], ((1,), (1,)))
                delta = jnp.sum(probs * grad_probs, axis=1, keepdims=True)
                grad_scores = (probs * (grad_probs - delta) * scale).astype(jnp.bfloat16)
                add(grad_query, b, wide(grad_scores, key_m[:n], ((1,), (0,))))
                for spot in range(b + 1):
                    cols = slice(spot * block, (spot + 1) * block)
                    add(grad_key, spot, wide(grad_scores[:, cols], query_m[here], ((0,), (0,))))
                    add(grad_value, spot, wide(rounded[:, cols], upper_m[here], ((0,), (0,))))
        for part, pieces in enumerate((grad_query, grad_key, grad_value)):
            for b in range(2):
                gtrip[
                    b * block : (b + 1) * block,
                    pl.ds(pl.multiple_of((part * pairs + hp) * width, width), width),
                ] = pieces[b].astype(jnp.bfloat16)

    for hp in range(pairs):
        attend_back_pair(hp)
        if hp == 0:
            reduce_z(D, [0])
        reduce_z(U, steps[hp - 1 : hp] if 0 < hp < nz - 1 else [])

    reduce_x(O)

    @pl.loop(0, 3)
    def _(i):
        product(
            Q,
            i,
            gtrip[:, pl.ds(pl.multiple_of(i * pairs * width, pairs * width), pairs * width)],
            full[0],
        )

    reduce_z(U, steps[pairs - 1 :])
    tmp[...] = wide(gtrip[...], wq[...].reshape(groups * width, 2 * half), ((1,), (0,)))
    for h in range(2):
        collect_start(3, h)
    reduce_x(Q)
    reduce_z(U, [0])
    for h in range(2):
        middle[parts[h]] = middle[parts[h]] + collect_wait(2, h)
    to_hbm(middle, out_ref, 4)
    reduce_z(O, steps + [0])
    reduce_z(Q, steps[:-1])
    for h in range(2):
        rows = parts[h]
        grad_one, normal = collect_wait(3, h), normal_one[rows]
        tmp[rows, 0:half] = grad_one
        ns[0, 0:1] += jnp.sum(grad_one * normal, axis=0, keepdims=True)
        ns[0, 1:2] += jnp.sum(grad_one, axis=0, keepdims=True)
        back_stats(grad_one, normal, gain_one, 3, h)
        swap_stats(3, h)
    pending.append(push(ns.at[0], nr.at[0], NS, NS, far(c)))
    reduce_z(Q, steps[-1:])
    arrived(nr.at[0], NS)
    ns[1] = ns[0] + nr[0]
    pending.append(push(ns.at[1], nr.at[1], NS + 1, NS + 1, x_peer))
    for h in range(2):
        rows = parts[h]
        mgrad[rows] += finish_back(
            tmp[rows, 0:half], normal_one[rows], inverse[0, rows], gain_one, 3, h
        )
    to_hbm(mgrad, back_ref, 5)
    arrived(nr.at[1], NS + 1)
    ns[2] = ns[1] + nr[1]
    for step in range(1, nz):
        pending.append(
            push(ns.at[2], nr.at[2 + z], NS + 2 + step, NS + 2 + z, at_z((z + step) % nz))
        )
    nr[2 + z] = ns[2]
    reduce_z(Q, [0])
    for p in (D, U, O, Q):
        reduce_end(p)
    for step in range(1, nz):
        zz = (z + step) % nz
        arrived(nr.at[2 + zz], NS + 2 + zz)
    total = nr[2]
    for zz in range(1, nz):
        total = total + nr[2 + zz]
    total_norm[...] = total * factor
    to_hbm(total_norm, norm_sum_ref, 6)

    for copy in pending:
        copy.wait_send()
    for flag, copy in guarded:

        @pl.when(flag)
        def _():
            copy.wait_send()

    for copy in writes:
        copy.wait()


def adam_values(weight, grad, first, second, decay):
    first_moment = beta_one * first + (1.0 - beta_one) * grad
    second_moment = beta_two * second + (1.0 - beta_two) * grad * grad
    step_size = (
        first_moment
        / (1.0 - beta_one**STEP)
        / (jnp.sqrt(second_moment / (1.0 - beta_two**STEP)) + adam_eps)
    )
    return weight - learn_rate * (step_size + decay * weight), first_moment, second_moment


def adam_kernel(*refs):
    ins, outs = refs[:17], refs[17:34]
    held, made, in_sem, out_sem = refs[34:51], refs[51:66], refs[66], refs[67]
    reads = [pltpu.make_async_copy(ins[i], held[i], in_sem.at[i]) for i in range(17)]
    order = (3, 4, 1, 2, 0)
    for i in order:
        for k in (i, 5 + i, 10 + i):
            reads[k].start()
    for k in (15, 16):
        reads[k].start()
    writes = []

    def write(src, dst, k):
        copy = pltpu.make_async_copy(src, outs[dst], out_sem.at[k])
        copy.start()
        writes.append(copy)

    for i in order:
        for k in (i, 5 + i, 10 + i):
            reads[k].wait()
        weight, moments = held[5 + i], held[10 + i]
        grad = held[i][...]
        if i == 0:
            grad = grad[0 : weight.shape[0]]
        grad = grad.reshape(weight.shape)
        made[i][...] = grad
        write(made[i], 2 + i, i)
        new, first, second = adam_values(
            weight[...], grad, moments[0], moments[1], decay_rate if i else 0.0
        )
        made[5 + i][...] = new
        write(made[5 + i], 7 + i, 5 + i)
        made[10 + i][0] = first
        made[10 + i][1] = second
        write(made[10 + i], 12 + i, 10 + i)
    for k in (15, 16):
        reads[k].wait()
        write(held[k], k - 15, k)
    for copy in writes:
        copy.wait()


def on_device_fused(
    block_in,
    upstream,
    norm_params,
    w_qkv,
    w_attn,
    w_up,
    w_down,
    mom_norm,
    mom_qkv,
    mom_attn,
    mom_up,
    mom_down,
):
    low = LOW
    ndp = lax.axis_size("dp")
    nz = ndp // low
    tokens, half = block_in.shape
    pairs = w_qkv.shape[1] // 2
    per = w_qkv.shape[2]
    groups = 3 * pairs
    width = 2 * per * ndp
    hidden_rows = w_up.shape[0]
    hidden = hidden_rows * ndp
    tiles = hidden // HIDDEN_TILE
    token_count = tokens * ndp * lax.axis_size("row")
    bf, f32 = jnp.bfloat16, jnp.float32

    def both(kind_of):
        return [kind_of(p) for p in range(4)]

    def piece(p):
        return ((groups, pairs)[p], 2 * per, half) if p < 2 else (hidden_rows, half)

    def whole(p, cols):
        return ((groups, pairs)[p], ndp, 2 * per, cols) if p < 2 else (hidden, cols)

    scratch = (
        both(lambda p: pltpu.VMEM(piece(p), bf))
        + both(lambda p: pltpu.VMEM(whole(p, 2 * half), bf))
        + [
            pltpu.VMEM((4, tokens, 128), f32),
            pltpu.VMEM((4, tokens, 128), f32),
            pltpu.VMEM((4, tokens, half), bf),
            pltpu.VMEM((4, tokens, 2 * half), bf),
            pltpu.VMEM((4, 2, tokens, half), bf),
            pltpu.VMEM((4, 2, tokens, half), bf),
            pltpu.VMEM((2, tokens, half), f32),
            pltpu.VMEM((tokens, 2 * half), f32),
            pltpu.VMEM((tokens, 3 * pairs * width), bf),
            pltpu.VMEM((tokens, pairs * width), bf),
            pltpu.VMEM((2 * pairs, tokens, 1), f32),
            pltpu.VMEM((tokens, hidden), bf),
            pltpu.VMEM((tokens, hidden), bf),
            pltpu.VMEM((tokens, half), f32),
            pltpu.VMEM((tokens, half), f32),
            pltpu.VMEM((tokens, half), f32),
            pltpu.VMEM((2, tokens, 1), f32),
            pltpu.VMEM((tokens, pairs * width), bf),
            pltpu.VMEM((tokens, 3 * pairs * width), bf),
            pltpu.VMEM((tokens, half), f32),
        ]
        + both(lambda p: pltpu.VMEM(whole(p, half), f32))
        + both(lambda p: pltpu.VMEM(whole(p, half), bf))
        + both(lambda p: pltpu.VMEM(whole(p, half), bf))
        + both(lambda p: pltpu.VMEM((nz,) + piece(p), bf))
        + both(lambda p: pltpu.VMEM((nz,) + piece(p), bf))
        + both(lambda p: pltpu.VMEM(piece(p), f32))
        + [
            pltpu.VMEM((8, half), f32),
            pltpu.VMEM((3, 8, half), f32),
            pltpu.VMEM((2 + nz, 8, half), f32),
            pltpu.SemaphoreType.DMA((50 + 21 * nz,)),
            pltpu.SemaphoreType.DMA((50 + 21 * nz,)),
            pltpu.SemaphoreType.DMA((19,)),
        ]
    )
    vmem = pl.BlockSpec(memory_space=pltpu.VMEM)
    hbm = pl.BlockSpec(memory_space=pltpu.HBM)
    outs = (
        jax.ShapeDtypeStruct(block_in.shape, f32),
        jax.ShapeDtypeStruct(block_in.shape, f32),
        *both(lambda p: jax.ShapeDtypeStruct(piece(p), f32)),
        jax.ShapeDtypeStruct((8, half), f32),
    )
    block_out, input_grad, *totals = pl.pallas_call(
        functools.partial(step_kernel, nz, low, 1.0 / math.sqrt(token_count)),
        out_shape=outs,
        in_specs=[vmem] * 7,
        out_specs=[hbm] * len(outs),
        scratch_shapes=scratch,
        compiler_params=pltpu.CompilerParams(
            collective_id=0, has_side_effects=True, vmem_limit_bytes=VMEM_BYTES
        ),
    )(block_in, upstream, norm_params, w_qkv, w_attn, w_up, w_down)
    params = (norm_params, w_qkv, w_attn, w_up, w_down)
    moments = (mom_norm, mom_qkv, mom_attn, mom_up, mom_down)
    norm_total = totals.pop()
    operands = (norm_total, *totals, *params, *moments, block_out, input_grad)
    shapes = [
        jax.ShapeDtypeStruct(item.shape, f32)
        for item in (block_out, input_grad) + params * 2 + moments
    ]
    return pl.pallas_call(
        adam_kernel,
        out_shape=shapes,
        in_specs=[hbm] * len(operands),
        out_specs=[hbm] * len(shapes),
        scratch_shapes=[pltpu.VMEM(item.shape, f32) for item in operands]
        + [pltpu.VMEM(item.shape, f32) for item in shapes[2:]]
        + [pltpu.SemaphoreType.DMA((17,)), pltpu.SemaphoreType.DMA((17,))],
        compiler_params=pltpu.CompilerParams(vmem_limit_bytes=VMEM_BYTES),
    )(*operands)


def fits(block_in, w_qkv, w_up, ndp, nrow, ncol):
    return (
        nrow == 2
        and ncol == 2
        and ndp == 4 * LOW
        and block_in.shape[0] == SEQ
        and w_qkv.shape[1] % 2 == 0
        and w_qkv.shape[2] == 8
        and (w_up.shape[0] * ndp) % HIDDEN_TILE == 0
        and w_up.shape[0] % 16 == 0
    )


def run_step(*args):
    sizes = [lax.axis_size(name) for name in ("dp", "row", "col")]
    if fits(args[0], args[3], args[5], *sizes):
        return on_device_fused(*args)
    return on_device(*args)


def solution(mesh):
    in_specs = (
        P(("dp", "row"), "col"),
        P(("dp", "row"), "col"),
        P(None, "col"),
        P(None, "row", "dp", "col"),
        P("row", "dp", "col"),
        P(("dp", "row"), "col"),
        P(("dp", "row"), "col"),
        P(None, None, "col"),
        P(None, None, "row", "dp", "col"),
        P(None, "row", "dp", "col"),
        P(None, ("dp", "row"), "col"),
        P(None, ("dp", "row"), "col"),
    )
    out_specs = (
        P(("dp", "row"), "col"),
        P(("dp", "row"), "col"),
        P(None, "col"),
        P(None, "row", "dp", "col"),
        P("row", "dp", "col"),
        P(("dp", "row"), "col"),
        P(("dp", "row"), "col"),
        P(None, "col"),
        P(None, "row", "dp", "col"),
        P("row", "dp", "col"),
        P(("dp", "row"), "col"),
        P(("dp", "row"), "col"),
        P(None, None, "col"),
        P(None, None, "row", "dp", "col"),
        P(None, "row", "dp", "col"),
        P(None, ("dp", "row"), "col"),
        P(None, ("dp", "row"), "col"),
    )
    return jax.shard_map(
        run_step, mesh=mesh, in_specs=in_specs, out_specs=out_specs, check_vma=False
    )
```

```python
import functools
import math

import jax
import jax.numpy as jnp
from jax import lax
from jax.experimental import pallas as pl
from jax.experimental.pallas import tpu as pltpu
from jax.sharding import PartitionSpec as P

SEQ = 512
STEP = 4
LOW = 2


norm_eps = 1e-05
adam_eps = 1e-08
beta_one = 0.9
beta_two = 0.95
learn_rate = 0.02
decay_rate = 0.1
gelu_coef = math.sqrt(2.0 / math.pi)
cubic_coef = 0.044715
masked_score = -1e30

group = ("row", "col")
swap_pair = [(0, 1), (1, 0)]
spread_first = [(1, 2), (2, 1)]
spread_second = [(0, 2), (3, 1), (1, 0), (2, 3)]
collect_second = [(dst, src) for src, dst in spread_second]


def smooth_pair(values):
    squared = values * values
    bent = jnp.tanh(gelu_coef * (values + cubic_coef * squared * values))
    smooth = 0.5 * values * (1.0 + bent)
    slope = 0.5 * (1.0 + bent) + 0.5 * values * (1.0 - bent * bent) * gelu_coef * (
        1.0 + 3.0 * cubic_coef * squared
    )
    return (smooth, slope)


def wide(left, right, dims):
    return lax.dot_general(left, right, (dims, ((), ())), preferred_element_type=jnp.float32)


def normalize(rows_in, gain_row, shift_row):
    count = rows_in.shape[1]
    mean_here = jnp.mean(rows_in, axis=1, keepdims=True)
    offset = rows_in - mean_here
    square_here = jnp.sum(offset * offset, axis=1, keepdims=True)
    there = lax.ppermute(jnp.concatenate([mean_here, square_here], axis=1), "col", swap_pair)
    gap = mean_here - there[:, :1]
    spread = (square_here + there[:, 1:] + gap * gap * (0.5 * count)) / (2.0 * count)
    inverse = lax.rsqrt(spread + norm_eps)
    normal = (rows_in - (mean_here - 0.5 * gap)) * inverse
    return (normal, inverse, (normal * gain_row + shift_row).astype(jnp.bfloat16))


def norm_back(grad_normed, normal, inverse, gain_row):
    count = 2.0 * grad_normed.shape[1]
    scaled = grad_normed * gain_row
    here = jnp.concatenate(
        [
            jnp.sum(scaled, axis=1, keepdims=True),
            jnp.sum(scaled * normal, axis=1, keepdims=True),
        ],
        axis=1,
    )
    total = (here + lax.ppermute(here, "col", swap_pair)) / count
    return inverse * (scaled - total[:, :1] - normal * total[:, 1:])


def pick(flag, one, other):
    return jnp.where(flag, one, other), jnp.where(flag, other, one)


def spread_rows(block):
    row, col = lax.axis_index("row"), lax.axis_index("col")
    first = lax.ppermute(block, group, spread_first)
    second = lax.ppermute(block, group, spread_second)
    first = jnp.where(row == col, block, first)
    low, high = pick(row == 0, first, second)
    return low, high


def collect_rows(low, high):
    row, col = lax.axis_index("row"), lax.axis_index("col")
    first, second = pick(row == 0, low, high)
    first_in = lax.ppermute(first.astype(jnp.bfloat16), group, spread_first)
    second_in = lax.ppermute(second.astype(jnp.bfloat16), group, collect_second)
    return jnp.where(row == col, first, first_in.astype(jnp.float32)) + second_in.astype(
        jnp.float32
    )


def out_project(rows, weight):
    half = weight.shape[1] // 2
    return collect_rows(
        wide(rows, weight[:, :half], ((1,), (0,))), wide(rows, weight[:, half:], ((1,), (0,)))
    )


def small_ring():
    size = lax.axis_size("dp")
    return size % LOW == 0 and size <= 8


def high_steps(sign):
    size = lax.axis_size("dp")
    high = size // LOW
    return [
        [(i, ((i // LOW + sign * step) % high) * LOW + i % LOW) for i in range(size)]
        for step in range(1, high)
    ]


def low_step():
    return [(i, i ^ 1) for i in range(lax.axis_size("dp"))]


def gather_weight(shard, axis):
    shard = shard.astype(jnp.bfloat16)
    if small_ring():
        near = jnp.concatenate(
            [shard] + [lax.ppermute(shard, "dp", perm) for perm in high_steps(1)], axis=axis
        )
        block = jnp.concatenate([near, lax.ppermute(near, "dp", low_step())], axis=axis)
    else:
        block = lax.all_gather(shard, "dp", axis=axis, tiled=True)
    there = lax.ppermute(block, "col", swap_pair)
    low, high = pick(lax.axis_index("col") == 0, block, there)
    return jnp.concatenate([low, high], axis=-1)


def reduce_weight(make, axis):
    away = make(False).astype(jnp.bfloat16)
    total = make(True) + lax.ppermute(away, "col", swap_pair).astype(jnp.float32)
    if not small_ring():
        return lax.psum_scatter(total, "dp", scatter_dimension=axis, tiled=True)
    near, far = jnp.split(total, 2, axis=axis)
    near = near + lax.ppermute(far.astype(jnp.bfloat16), "dp", low_step()).astype(jnp.float32)
    own, *rest = jnp.split(near, lax.axis_size("dp") // LOW, axis=axis)
    for piece, perm in zip(rest, high_steps(-1)):
        own = own + lax.ppermute(piece.astype(jnp.bfloat16), "dp", perm).astype(jnp.float32)
    return own


def sum_everywhere(terms):
    if not small_ring():
        return lax.psum(terms, ("dp", "row"))
    terms = terms + lax.ppermute(terms, "row", swap_pair)
    terms = terms + lax.ppermute(terms, "dp", low_step())
    moved = [lax.ppermute(terms, "dp", perm) for perm in high_steps(1)]
    for piece in moved:
        terms = terms + piece
    return terms


def head_scores(triples_ref, heads, size, head):
    width = heads * size
    query = triples_ref[:, head * size : (head + 1) * size]
    key = triples_ref[:, width + head * size : width + (head + 1) * size]
    value = triples_ref[:, 2 * width + head * size : 2 * width + (head + 1) * size]
    scores = wide(query, key, ((1,), (1,))) * (1.0 / math.sqrt(size))
    length = scores.shape[0]
    allowed = lax.broadcasted_iota(jnp.int32, (length, length), 0) >= lax.broadcasted_iota(
        jnp.int32, (length, length), 1
    )
    return query, key, value, jnp.where(allowed, scores, masked_score)


def attend_kernel(heads, size, triples_ref, mixed_ref, total_ref):
    for head in range(heads):
        _, _, value, scores = head_scores(triples_ref, heads, size, head)
        highest = jnp.max(scores, axis=1, keepdims=True)
        log_total = highest + jnp.log(jnp.sum(jnp.exp(scores - highest), axis=1, keepdims=True))
        probs = jnp.exp(scores - log_total).astype(jnp.bfloat16)
        mixed_ref[:, head * size : (head + 1) * size] = wide(probs, value, ((1,), (0,))).astype(
            jnp.bfloat16
        )
        total_ref[:, head : head + 1] = log_total


def attend_back_kernel(heads, size, triples_ref, grad_ref, total_ref, out_ref):
    width = heads * size
    scale = 1.0 / math.sqrt(size)
    for head in range(heads):
        query, key, value, scores = head_scores(triples_ref, heads, size, head)
        grad_mixed = grad_ref[:, head * size : (head + 1) * size]
        probs = jnp.exp(scores - total_ref[:, head : head + 1])
        grad_values = wide(probs.astype(jnp.bfloat16), grad_mixed, ((0,), (0,)))
        grad_probs = wide(grad_mixed, value, ((1,), (1,)))
        delta = jnp.sum(probs * grad_probs, axis=1, keepdims=True)
        grad_scores = (probs * (grad_probs - delta) * scale).astype(jnp.bfloat16)
        for part, piece in enumerate(
            (
                wide(grad_scores, key, ((1,), (0,))),
                wide(grad_scores, query, ((0,), (0,))),
                grad_values,
            )
        ):
            start = part * width + head * size
            out_ref[:, start : start + size] = piece.astype(jnp.bfloat16)


def by_sequence(kernel, operands, outs):
    rows = operands[0].shape[0]

    def spec(shape):
        return pl.BlockSpec((SEQ, shape[1]), lambda step: (step, 0))

    return pl.pallas_call(
        kernel,
        grid=(rows // SEQ,),
        in_specs=[spec(item.shape) for item in operands],
        out_specs=[spec(item.shape) for item in outs],
        out_shape=outs,
        compiler_params=pltpu.CompilerParams(vmem_limit_bytes=40 * 1024 * 1024),
        cost_estimate=pl.CostEstimate(
            flops=rows * SEQ * 2048, bytes_accessed=rows * 8192, transcendentals=rows * SEQ * 6
        ),
    )(*operands)


def adam_step(weight, grad, moments, decay):
    first_moment = beta_one * moments[0] + (1.0 - beta_one) * grad
    second_moment = beta_two * moments[1] + (1.0 - beta_two) * grad * grad
    step_size = (
        first_moment
        / (1.0 - beta_one**STEP)
        / (jnp.sqrt(second_moment / (1.0 - beta_two**STEP)) + adam_eps)
    )
    return (
        weight - learn_rate * (step_size + decay * weight),
        jnp.stack([first_moment, second_moment]),
    )


def on_device(
    block_in,
    upstream,
    norm_params,
    w_qkv,
    w_attn,
    w_up,
    w_down,
    mom_norm,
    mom_qkv,
    mom_attn,
    mom_up,
    mom_down,
):
    heads = w_qkv.shape[1]
    size = w_qkv.shape[2] * lax.axis_size("dp")
    width = heads * size
    at_low = lax.axis_index("col") == 0

    normal_one, inverse_one, normed_one = normalize(block_in, norm_params[0], norm_params[1])
    qkv_mat = gather_weight(w_qkv, 2).reshape(3 * width, -1)
    one_low, one_high = spread_rows(normed_one)
    attn_mat = gather_weight(w_attn, 1).reshape(width, -1)
    up_mat = gather_weight(w_up, 0)
    up_low, up_high = spread_rows(upstream.astype(jnp.bfloat16))
    down_mat = gather_weight(w_down, 0)

    triples = wide(
        jnp.concatenate([one_low, one_high], axis=1), qkv_mat, ((1,), (1,))
    ).astype(jnp.bfloat16)
    mixed, log_total = by_sequence(
        functools.partial(attend_kernel, heads, size),
        (triples,),
        (
            jax.ShapeDtypeStruct((triples.shape[0], width), jnp.bfloat16),
            jax.ShapeDtypeStruct((triples.shape[0], heads), jnp.float32),
        ),
    )
    middle = block_in + out_project(mixed, attn_mat)
    normal_two, inverse_two, normed_two = normalize(middle, norm_params[2], norm_params[3])
    two_low, two_high = spread_rows(normed_two)
    grad_hidden = wide(jnp.concatenate([up_low, up_high], axis=1), down_mat, ((1,), (1,)))
    hidden_pre = wide(jnp.concatenate([two_low, two_high], axis=1), up_mat, ((1,), (1,)))
    activated, slope = smooth_pair(hidden_pre)
    activated = activated.astype(jnp.bfloat16)
    grad_pre = (grad_hidden * slope).astype(jnp.bfloat16)
    grad_normed_two = out_project(grad_pre, up_mat)
    block_out = middle + out_project(activated, down_mat)

    def products(left, low, high):
        own, away = pick(at_low, low, high)
        return lambda mine: wide(left, own if mine else away, ((0,), (0,)))

    grad_down = reduce_weight(products(activated, up_low, up_high), 0)
    grad_up = reduce_weight(products(grad_pre, two_low, two_high), 0)
    middle_grad = upstream + norm_back(grad_normed_two, normal_two, inverse_two, norm_params[2])
    mid_low, mid_high = spread_rows(middle_grad.astype(jnp.bfloat16))
    grad_mixed = wide(
        jnp.concatenate([mid_low, mid_high], axis=1), attn_mat, ((1,), (1,))
    ).astype(jnp.bfloat16)

    def by_head(make, parts):
        return lambda mine: make(mine).reshape(*parts, heads, size, -1)

    grad_attn = reduce_weight(by_head(products(mixed, mid_low, mid_high), ()), 1)
    (grad_triples,) = by_sequence(
        functools.partial(attend_back_kernel, heads, size),
        (triples, grad_mixed, log_total),
        (jax.ShapeDtypeStruct(triples.shape, jnp.bfloat16),),
    )
    grad_qkv = reduce_weight(by_head(products(grad_triples, one_low, one_high), (3,)), 2)
    grad_normed_one = out_project(grad_triples, qkv_mat)
    input_grad = middle_grad + norm_back(grad_normed_one, normal_one, inverse_one, norm_params[0])
    norm_terms = jnp.stack(
        [
            jnp.sum(grad_normed_one * normal_one, axis=0),
            jnp.sum(grad_normed_one, axis=0),
            jnp.sum(grad_normed_two * normal_two, axis=0),
            jnp.sum(grad_normed_two, axis=0),
        ]
    )
    grad_norm = sum_everywhere(norm_terms)
    token_count = block_in.shape[0] * lax.axis_size("dp") * lax.axis_size("row")
    factor = 1.0 / math.sqrt(token_count)
    grad_norm = grad_norm * factor
    grad_qkv = grad_qkv * factor
    grad_attn = grad_attn * factor
    grad_up = grad_up * factor
    grad_down = grad_down * factor
    new_norm, new_mom_norm = adam_step(norm_params, grad_norm, mom_norm, 0.0)
    new_qkv, new_mom_qkv = adam_step(w_qkv, grad_qkv, mom_qkv, decay_rate)
    new_attn, new_mom_attn = adam_step(w_attn, grad_attn, mom_attn, decay_rate)
    new_up, new_mom_up = adam_step(w_up, grad_up, mom_up, decay_rate)
    new_down, new_mom_down = adam_step(w_down, grad_down, mom_down, decay_rate)
    return (
        block_out,
        input_grad,
        grad_norm,
        grad_qkv,
        grad_attn,
        grad_up,
        grad_down,
        new_norm,
        new_qkv,
        new_attn,
        new_up,
        new_down,
        new_mom_norm,
        new_mom_qkv,
        new_mom_attn,
        new_mom_up,
        new_mom_down,
    )


MESH = pl.DeviceIdType.MESH
VMEM_BYTES = 67043328
HIDDEN_TILE = 256


def causal(rows, cols, first):
    return (
        lax.broadcasted_iota(jnp.int32, (rows, cols), 0) + first
        >= lax.broadcasted_iota(jnp.int32, (rows, cols), 1)
    )


def head_masks(per, width):
    lane = lax.broadcasted_iota(jnp.int32, (1, width), 1)
    return [
        jnp.where((lane // per) % 2 == part, 1.0, 0.0).astype(jnp.bfloat16) for part in range(2)
    ]


def row_stats(first, second, width=128):
    lane = lax.broadcasted_iota(jnp.int32, (first.shape[0], width), 1)
    return jnp.where(lane == 0, first, second)


def step_kernel(
    nz,
    low,
    factor,
    block_hbm,
    up_hbm,
    norm_hbm,
    wqkv_hbm,
    wattn_hbm,
    wup_hbm,
    wdown_hbm,
    out_ref,
    back_ref,
    sum_q_ref,
    sum_o_ref,
    sum_u_ref,
    sum_d_ref,
    norm_sum_ref,
    block_ref,
    up_ref,
    norm_ref,
    wqkv_ref,
    wattn_ref,
    wup_ref,
    wdown_ref,
    shard_q,
    shard_o,
    shard_u,
    shard_d,
    wq,
    wo,
    wu,
    wd,
    stat_s,
    stat_r,
    spread_s,
    full,
    col_s,
    col_r,
    keep,
    tmp,
    trip,
    mixed,
    lse,
    act,
    gpre,
    middle,
    normal_one,
    normal_two,
    inverse,
    gmix,
    gtrip,
    mgrad,
    gq,
    go,
    gu,
    gd,
    gsq,
    gso,
    gsu,
    gsd,
    grq,
    gro,
    gru,
    grd,
    xrq,
    xro,
    xru,
    xrd,
    zrq,
    zro,
    zru,
    zrd,
    total_q,
    total_o,
    total_u,
    total_d,
    total_norm,
    ns,
    nr,
    send,
    recv,
    local,
):
    dp, r, c = lax.axis_index("dp"), lax.axis_index("row"), lax.axis_index("col")
    z, x = dp // low, dp % low
    same = r == c
    tokens, half = block_ref.shape
    per = wqkv_ref.shape[2]
    pairs = wqkv_ref.shape[1] // 2
    width = 2 * per * nz * low
    ndp = nz * low
    hidden_rows = wup_ref.shape[0]
    hidden = hidden_rows * ndp
    tiles = hidden // HIDDEN_TILE
    groups = 3 * pairs
    Q, O, U, D = range(4)

    STAT, SPR, COL, GZ = 0, 8, 24, 40
    GX = GZ + 4 * nz
    GC = GX + 4 * nz
    RC = GC + 4
    RX = RC + 4
    RZ = RX + 4 * nz
    NS = RZ + 4 * nz
    GD = NS + 3 + nz

    def at_z(zz):
        return {"dp": zz * low + x}

    x_peer = {"dp": z * low + 1 - x}
    diagonal = {"dp": z * low + 1 - x, "row": 1 - r}
    partner = {"col": 1 - c}

    def far(other):
        return {"row": 1 - r, "col": other}

    def feat(f):
        return pl.ds(pl.multiple_of(f * half, half), half)

    mine, other = feat(c), feat(1 - c)
    pending = []
    writes = []
    guarded = []

    def describe(src, dst, s, q, where):
        return pltpu.make_async_remote_copy(
            src_ref=src,
            dst_ref=dst,
            send_sem=send.at[s],
            recv_sem=recv.at[q],
            device_id=where,
            device_id_type=MESH,
        )

    def push(src, dst, s, q, where):
        copy = describe(src, dst, s, q, where)
        copy.start()
        return copy

    def arrived(dst, q):
        describe(dst, dst, q, q, partner).wait_recv()

    weights = (wq, wo, wu, wd)

    def slot(p, owner, f):
        if p < 2:
            return weights[p].at[:, owner, :, feat(f)]
        rows = pl.ds(pl.multiple_of(owner * hidden_rows, hidden_rows), hidden_rows)
        return weights[p].at[rows, feat(f)]

    shards = (shard_q, shard_o, shard_u, shard_d)

    block = tokens // 2
    parts = [slice(h * block, (h + 1) * block) for h in range(2)]

    def local_stats(rows_in, k, h):
        mean_here = jnp.mean(rows_in, axis=1, keepdims=True)
        offset = rows_in - mean_here
        square_here = jnp.sum(offset * offset, axis=1, keepdims=True)
        stat_s[k, parts[h]] = row_stats(mean_here, square_here)

    def swap_stats(k, h):
        spot = STAT + 2 * k + h
        pending.append(
            push(stat_s.at[k, parts[h]], stat_r.at[k, parts[h]], spot, spot, partner)
        )

    def finish_norm(rows_in, k, h, gain, shift, normal_ref, inverse_index, out):
        rows = parts[h]
        arrived(stat_r.at[k, rows], STAT + 2 * k + h)
        here, there = stat_s[k, rows], stat_r[k, rows]
        mean_here, square_here = here[:, 0:1], here[:, 1:2]
        gap = mean_here - there[:, 0:1]
        spread = (square_here + there[:, 1:2] + gap * gap * (0.5 * half)) / (2.0 * half)
        inv = lax.rsqrt(spread + norm_eps)
        normal = (rows_in - (mean_here - 0.5 * gap)) * inv
        normal_ref[rows] = normal
        inverse[inverse_index, rows] = inv
        out[rows] = (normal * gain + shift).astype(jnp.bfloat16)

    def back_stats(grad, normal, gain, k, h):
        scaled = grad * gain
        stat_s[k, parts[h]] = row_stats(
            jnp.sum(scaled, axis=1, keepdims=True),
            jnp.sum(scaled * normal, axis=1, keepdims=True),
        )

    def finish_back(grad, normal, inv, gain, k, h):
        rows = parts[h]
        arrived(stat_r.at[k, rows], STAT + 2 * k + h)
        total = (stat_s[k, rows] + stat_r[k, rows]) / (2.0 * half)
        return inv * (grad * gain - total[:, 0:1] - normal * total[:, 1:2])

    def spread_spot(k, f, h):
        return SPR + (2 * k + f) * 2 + h

    def spread_start(k, h):
        rows = parts[h]
        src = spread_s.at[k, rows]
        dst = full.at[k, rows, mine]
        pending.append(push(src, dst, spread_spot(k, 0, h), spread_spot(k, c, h), far(r)))

        @pl.when(same)
        def _():
            pltpu.make_async_copy(src, dst, local.at[4 + 2 * k + h]).start()

        @pl.when(jnp.logical_not(same))
        def _():
            push(src, dst, spread_spot(k, 1, h), spread_spot(k, c, h), partner)

    def spread_wait(k, some=(0, 1)):
        for h in some:
            rows = parts[h]
            src = spread_s.at[k, rows]
            dst = full.at[k, rows, mine]
            arrived(full.at[k, rows, other], spread_spot(k, 1 - c, h))

            @pl.when(same)
            def _():
                pltpu.make_async_copy(src, dst, local.at[4 + 2 * k + h]).wait()

            @pl.when(jnp.logical_not(same))
            def _():
                arrived(dst, spread_spot(k, c, h))
                describe(
                    src, dst, spread_spot(k, 1, h), spread_spot(k, c, h), partner
                ).wait_send()

    def collect_spot(k, f, h):
        return COL + (2 * k + f) * 2 + h

    def collect_start(k, h):
        rows = parts[h]
        col_s[k, 0, rows] = tmp[rows, other].astype(jnp.bfloat16)
        col_s[k, 1, rows] = tmp[rows, mine].astype(jnp.bfloat16)

        @pl.when(same)
        def _():
            keep[k % 2, rows] = tmp[rows, mine]
            spot = collect_spot(k, 0, h)
            push(col_s.at[k, 0, rows], col_r.at[k, 0, rows], spot, spot, partner)

        @pl.when(jnp.logical_not(same))
        def _():
            for f, where in enumerate((far(1 - c), far(c))):
                push(
                    col_s.at[k, f, rows],
                    col_r.at[k, 1, rows],
                    collect_spot(k, f, h),
                    collect_spot(k, 1, h),
                    where,
                )

    def collect_wait(k, h):
        rows = parts[h]
        arrived(col_r.at[k, 1, rows], collect_spot(k, 1, h))

        def sent(f):
            spot = collect_spot(k, f, h)
            describe(
                col_s.at[k, f, rows], col_r.at[k, f, rows], spot, spot, partner
            ).wait_send()

        @pl.when(same)
        def _():
            sent(0)

        @pl.when(jnp.logical_not(same))
        def _():
            arrived(col_r.at[k, 0, rows], collect_spot(k, 0, h))
            keep[k % 2, rows] = col_r[k, 0, rows].astype(jnp.float32)
            sent(0)
            sent(1)

        return keep[k % 2, rows] + col_r[k, 1, rows].astype(jnp.float32)

    def relay(p, zz, up, src):
        dst = slot(p, zz * low + x, c)
        spot = (GZ if up else GD) + p * nz + zz
        to = at_z((z + 1) % nz) if up else at_z((z + nz - 1) % nz)
        return describe(dst if src is None else src, dst, spot, GZ + p * nz + zz, to)

    def guard(flag, copy):
        @pl.when(flag)
        def _():
            copy.start()

        guarded.append((flag, copy))

    def gather_own_z(p):
        guard(z < nz - 1, relay(p, z, True, shards[p]))
        guard(z > 0, relay(p, z, False, shards[p]))

    def x_copy(p, zz, src):
        dst = slot(p, zz * low + x, c)
        spot = GX + p * nz + zz
        return describe(dst if src is None else src, dst, spot, spot, x_peer)

    def gather_own_x(p):
        x_copy(p, z, shards[p]).start()
        for step in range(nz):
            pending.append(x_copy(p, (z + step) % nz, None))

    def band(p, cols):
        return weights[p].at[:, :, :, cols] if p < 2 else weights[p].at[:, cols]

    def to_partner(p, owner):
        push(slot(p, owner, c), slot(p, owner, c), GC + p, GC + p, partner)

    def gather_own_c(p):
        pltpu.make_async_copy(shards[p], slot(p, dp, c), local.at[p]).start()
        push(shards[p], slot(p, dp, c), GC + p, GC + p, partner)
        pending.append(describe(band(p, mine), band(p, mine), GC + p, GC + p, partner))

    steps = list(range(1, nz))
    def by_distance(far_z, serve):
        below, above = (z + nz - far_z) % nz, (z + far_z) % nz

        @pl.when(z >= far_z)
        def _():
            serve(below, True)

        @pl.when(z + far_z < nz)
        def _():
            serve(above, False)

    def gather_z(p, some):
        def serve(zz, up):
            owner = zz * low + x
            arrived(slot(p, owner, c), GZ + p * nz + zz)
            x_copy(p, zz, None).start()

            @pl.when((z < nz - 1) if up else (z > 0))
            def _():
                relay(p, zz, up, None).start()

            to_partner(p, owner)

        for far_z in some:
            by_distance(far_z, serve)
            for zz, up, flag in (
                ((z + nz - far_z) % nz, True, jnp.logical_and(z >= far_z, z < nz - 1)),
                ((z + far_z) % nz, False, jnp.logical_and(z + far_z < nz, z > 0)),
            ):
                guarded.append((flag, relay(p, zz, up, None)))

    def gather_x(p):
        def serve(zz, up):
            owner = zz * low + 1 - x
            arrived(slot(p, owner, c), GX + p * nz + zz)
            to_partner(p, owner)

        serve(z, True)
        for far_z in steps:
            by_distance(far_z, serve)

    def gather_c(p):
        pltpu.make_async_copy(shards[p], slot(p, dp, c), local.at[p]).wait()
        arrived(band(p, other), GC + p)

    sums = (gq, go, gu, gd)
    away = (gsq, gso, gsu, gsd)
    near = (grq, gro, gru, grd)
    from_x = (xrq, xro, xru, xrd)
    from_z = (zrq, zro, zru, zrd)
    totals = (total_q, total_o, total_u, total_d)
    results = (sum_q_ref, sum_o_ref, sum_u_ref, sum_d_ref)

    def index(p, owner):
        if p < 2:
            return (slice(None), owner)
        return (pl.ds(pl.multiple_of(owner * hidden_rows, hidden_rows), hidden_rows),)

    def rows_of(p, i):
        if p < 2:
            return pl.ds(i * pairs, pairs)
        return pl.ds(pl.multiple_of(i * HIDDEN_TILE, HIDDEN_TILE), HIDDEN_TILE)

    def swap_chunk(p, i):
        rows = rows_of(p, i)
        return describe(
            away[p].at[rows], near[p].at[rows], RC + p, RC + p, partner
        )

    def product(p, i, left, right):
        tmp_rows = left.shape[1]
        tmp[0:tmp_rows] = wide(left, right, ((0,), (0,)))
        rows = rows_of(p, i)
        own, gone = tmp[0:tmp_rows, mine], tmp[0:tmp_rows, other].astype(jnp.bfloat16)
        if p < 2:
            own = own.reshape(pairs, ndp, 2 * per, half)
            gone = gone.reshape(pairs, ndp, 2 * per, half)
        sums[p][rows] = own
        away[p][rows] = gone
        swap_chunk(p, i).start()

    inner, upper = z * (nz - 1 - z) // 2, z // 2

    def target(step):
        if step == 0:
            return z
        place = (1 - inner) * (nz - step) + inner * (2, 0, 3)[step - 1]
        return place + upper * (nz - 1 - 2 * place)

    def reduce_x(p):
        describe(away[p], near[p], RC + p, RC + p, partner).wait()
        for step in steps + [0]:
            zz = target(step)
            at = index(p, zz * low + 1 - x)
            total = sums[p][at] + near[p][at].astype(jnp.float32)
            away[p][at] = total.astype(jnp.bfloat16)
            pending.append(
                push(
                    away[p].at[at],
                    from_x[p].at[zz],
                    RX + p * nz + step,
                    RX + p * nz + zz,
                    x_peer,
                )
            )

    def reduce_z(p, some):
        for step in some:
            zz = target(step)
            at = index(p, zz * low + x)
            arrived(from_x[p].at[zz], RX + p * nz + zz)
            if step == nz - 1:

                @pl.when(inner == 1)
                def _():
                    arrived(from_z[p].at[z], RZ + p * nz + z)
                    sums[p][at] = sums[p][at] + from_z[p][z].astype(jnp.float32)

            total = (
                sums[p][at] + near[p][at].astype(jnp.float32) + from_x[p][zz].astype(jnp.float32)
            )
            if step == 0:
                sums[p][at] = total
                continue
            away[p][at] = total.astype(jnp.bfloat16)
            to, spot = zz, z
            if step == 1:
                to = inner * zz + (1 - inner) * (1 + upper)
                spot = inner * z + (1 - inner) * (1 + upper)
            pending.append(
                push(
                    away[p].at[at],
                    from_z[p].at[spot],
                    RZ + p * nz + step,
                    RZ + p * nz + spot,
                    at_z(to),
                )
            )

    def reduce_end(p):
        totals[p][...] = sums[p][index(p, dp)]
        for step in range(1, nz):
            zz = (z + step) % nz

            @pl.when((zz - z) * (zz - z) < (nz - 1) * (nz - 1))
            def _():
                arrived(from_z[p].at[zz], RZ + p * nz + zz)
                totals[p][...] = totals[p][...] + from_z[p][zz].astype(jnp.float32)

        totals[p][...] = totals[p][...] * factor
        to_hbm(totals[p], results[p], p)

    def to_hbm(src, dst, i):
        copy = pltpu.make_async_copy(src, dst, local.at[12 + i])
        copy.start()
        writes.append(copy)

    sources = (block_hbm, up_hbm, norm_hbm, wqkv_hbm, wattn_hbm, wup_hbm, wdown_hbm)
    held = (block_ref, up_ref, norm_ref, wqkv_ref, wattn_ref, wup_ref, wdown_ref)
    loads = [
        pltpu.make_async_copy(src, dst, local.at[19 + i])
        for i, (src, dst) in enumerate(zip(sources, held))
    ]
    barrier = pltpu.get_barrier_semaphore()
    peers = [at_z((z + step) % nz) for step in range(1, nz)] + [
        x_peer,
        partner,
        far(c),
        far(1 - c),
        diagonal,
    ]
    for peer in peers:
        pl.semaphore_signal(barrier, inc=1, device_id=peer, device_id_type=MESH)
    for i in (3, 4, 0, 2, 5, 6, 1):
        loads[i].start()
    for i in (3, 4):
        loads[i].wait()
    shard_q[...] = wqkv_ref[...].reshape(groups, 2 * per, half).astype(jnp.bfloat16)
    shard_o[...] = wattn_ref[...].reshape(pairs, 2 * per, half).astype(jnp.bfloat16)
    loads[0].wait()
    for h in range(2):
        local_stats(block_ref[parts[h]], 0, h)
    for i in (2, 5, 6, 1):
        loads[i].wait()
    shard_u[...] = wup_ref[...].astype(jnp.bfloat16)
    shard_d[...] = wdown_ref[...].astype(jnp.bfloat16)
    gain_one, shift_one = norm_ref[0:1], norm_ref[1:2]
    gain_two, shift_two = norm_ref[2:3], norm_ref[3:4]
    pl.semaphore_wait(barrier, len(peers))

    gather_own_z(Q)
    gather_own_x(Q)
    for h in range(2):
        swap_stats(0, h)
    gather_own_c(Q)
    gather_own_z(O)
    gather_own_x(O)
    for h in range(2):
        finish_norm(
            block_ref[parts[h]], 0, h, gain_one, shift_one, normal_one, 0, spread_s.at[0]
        )
        spread_start(0, h)
    spread_s[1] = up_ref[...].astype(jnp.bfloat16)
    for h in range(2):
        spread_start(1, h)
    for far_z in steps[:-1]:
        gather_z(Q, [far_z])
        gather_z(O, [far_z])
    gather_own_x(U)
    gather_own_z(U)
    gather_z(Q, steps[-1:])
    gather_z(O, steps[-1:])
    gather_own_x(D)
    gather_own_c(O)
    gather_own_z(D)
    gather_x(Q)
    gather_own_c(U)
    gather_own_c(D)
    gather_c(Q)
    spread_wait(0)
    gather_z(U, steps[:1])

    trip[...] = wide(
        full[0], wq[...].reshape(groups * width, 2 * half), ((1,), (1,))
    ).astype(jnp.bfloat16)

    gather_x(O)
    gather_z(D, steps[:1])

    scale = 1.0 / math.sqrt(width // 2)
    masks = head_masks(per, width)

    def part_of(ref, part, hp):
        return ref[:, pl.ds(pl.multiple_of((part * pairs + hp) * width, width), width)]

    def attend_pair(hp):
        query, key, value = (part_of(trip, part, hp) for part in range(3))
        rows = [None, None]
        for head in range(2):
            query_m, value_m = query * masks[head], value * masks[head]
            for b in range(2):
                n = (b + 1) * block
                scores = wide(query_m[b * block : n], key[:n], ((1,), (1,))) * scale
                scores = jnp.where(causal(block, n, b * block), scores, masked_score)
                highest = jnp.max(scores, axis=1, keepdims=True)
                raised = jnp.exp(scores - highest)
                total = jnp.sum(raised, axis=1, keepdims=True)
                lse[hp * 2 + head, b * block : n] = highest + jnp.log(total)
                probs = (raised * (1.0 / total)).astype(jnp.bfloat16)
                got = wide(probs, value_m[:n], ((1,), (0,)))
                rows[b] = got if rows[b] is None else rows[b] + got
        for b in range(2):
            mixed[b * block : (b + 1) * block, pl.ds(pl.multiple_of(hp * width, width), width)] = (
                rows[b].astype(jnp.bfloat16)
            )

    def attn_weight():
        return wo[...].reshape(pairs * width, 2 * half)

    for hp in range(pairs):
        attend_pair(hp)
        if hp == pairs - 2:
            gather_z(U, steps[1:2])
    gather_c(O)
    tmp[...] = wide(mixed[...], attn_weight(), ((1,), (0,)))
    for h in range(2):
        collect_start(0, h)
    gather_z(D, steps[1:2])
    gather_z(U, steps[2:])
    gather_z(D, steps[2:])
    for h in range(2):
        middle[parts[h]] = block_ref[parts[h]] + collect_wait(0, h)
        local_stats(middle[parts[h]], 1, h)
        swap_stats(1, h)
        finish_norm(
            middle[parts[h]], 1, h, gain_two, shift_two, normal_two, 1, spread_s.at[2]
        )
        spread_start(2, h)
        gather_x((U, D)[h])
    gather_c(U)
    gather_c(D)
    spread_wait(1)

    def tile(i):
        return pl.ds(pl.multiple_of(i * HIDDEN_TILE, HIDDEN_TILE), HIDDEN_TILE)

    def hidden_rows_of(h):
        rows = parts[h]

        @pl.loop(0, tiles)
        def _(i):
            pre = wide(full[2, rows], wu[tile(i)], ((1,), (1,)))
            grad = wide(full[1, rows], wd[tile(i)], ((1,), (1,)))
            smooth, slope = smooth_pair(pre)
            act[rows, tile(i)] = smooth.astype(jnp.bfloat16)
            gpre[rows, tile(i)] = (grad * slope).astype(jnp.bfloat16)

    spread_wait(2, (0,))
    hidden_rows_of(0)
    spread_wait(2, (1,))
    hidden_rows_of(1)

    tmp[...] = wide(gpre[...], wu[...], ((1,), (0,)))
    for h in range(2):
        collect_start(1, h)

    @pl.loop(0, tiles)
    def _(i):
        product(D, i, act[:, tile(i)], full[1])

    @pl.loop(0, tiles // 2)
    def _(i):
        product(U, i, gpre[:, tile(i)], full[2])

    reduce_x(D)

    @pl.loop(tiles // 2, tiles)
    def _(i):
        product(U, i, gpre[:, tile(i)], full[2])

    ns[0] = jnp.zeros((8, half), jnp.float32)
    for h in range(2):
        rows = parts[h]
        grad_two, normal = collect_wait(1, h), normal_two[rows]
        back_stats(grad_two, normal, gain_two, 2, h)
        swap_stats(2, h)
        ns[0, 2:3] += jnp.sum(grad_two * normal, axis=0, keepdims=True)
        ns[0, 3:4] += jnp.sum(grad_two, axis=0, keepdims=True)
        grad = up_ref[rows] + finish_back(grad_two, normal, inverse[1, rows], gain_two, 2, h)
        mgrad[rows] = grad
        spread_s[3, rows] = grad.astype(jnp.bfloat16)
        spread_start(3, h)
        if h == 0:
            reduce_z(D, steps[:1])
    reduce_x(U)
    reduce_z(D, steps[1:2])
    tmp[...] = wide(act[...], wd[...], ((1,), (0,)))
    for h in range(2):
        collect_start(2, h)
    reduce_z(D, steps[-1:])
    spread_wait(3)

    gmix[...] = wide(full[3], attn_weight(), ((1,), (1,))).astype(jnp.bfloat16)
    product(O, 0, mixed[...], full[3])

    def attend_back_pair(hp):
        query, key, value = (part_of(trip, part, hp) for part in range(3))
        upper = gmix[:, pl.ds(pl.multiple_of(hp * width, width), width)]
        grad_query = [None, None]
        grad_key = [None, None]
        grad_value = [None, None]

        def add(total, spot, term):
            total[spot] = term if total[spot] is None else total[spot] + term

        for head in range(2):
            query_m, key_m = query * masks[head], key * masks[head]
            upper_m = upper * masks[head]
            for b in range(2):
                n = (b + 1) * block
                here = slice(b * block, n)
                scores = wide(query_m[here], key[:n], ((1,), (1,))) * scale
                scores = jnp.where(causal(block, n, b * block), scores, masked_score)
                probs = jnp.exp(scores - lse[hp * 2 + head, b * block : n])
                rounded = probs.astype(jnp.bfloat16)
                grad_probs = wide(upper_m[here], value[:n], ((1,), (1,)))
                delta = jnp.sum(probs * grad_probs, axis=1, keepdims=True)
                grad_scores = (probs * (grad_probs - delta) * scale).astype(jnp.bfloat16)
                add(grad_query, b, wide(grad_scores, key_m[:n], ((1,), (0,))))
                for spot in range(b + 1):
                    cols = slice(spot * block, (spot + 1) * block)
                    add(grad_key, spot, wide(grad_scores[:, cols], query_m[here], ((0,), (0,))))
                    add(grad_value, spot, wide(rounded[:, cols], upper_m[here], ((0,), (0,))))
        for part, pieces in enumerate((grad_query, grad_key, grad_value)):
            for b in range(2):
                gtrip[
                    b * block : (b + 1) * block,
                    pl.ds(pl.multiple_of((part * pairs + hp) * width, width), width),
                ] = pieces[b].astype(jnp.bfloat16)

    for hp in range(pairs):
        attend_back_pair(hp)
        if hp == 0:
            reduce_z(D, [0])
        reduce_z(U, steps[hp - 1 : hp] if 0 < hp < nz - 1 else [])

    reduce_x(O)

    @pl.loop(0, 3)
    def _(i):
        product(
            Q,
            i,
            gtrip[:, pl.ds(pl.multiple_of(i * pairs * width, pairs * width), pairs * width)],
            full[0],
        )

    reduce_z(U, steps[pairs - 1 :])
    tmp[...] = wide(gtrip[...], wq[...].reshape(groups * width, 2 * half), ((1,), (0,)))
    for h in range(2):
        collect_start(3, h)
    reduce_x(Q)
    reduce_z(U, [0])
    for h in range(2):
        middle[parts[h]] = middle[parts[h]] + collect_wait(2, h)
    to_hbm(middle, out_ref, 4)
    reduce_z(O, steps + [0])
    reduce_z(Q, steps[:-1])
    for h in range(2):
        rows = parts[h]
        grad_one, normal = collect_wait(3, h), normal_one[rows]
        tmp[rows, 0:half] = grad_one
        ns[0, 0:1] += jnp.sum(grad_one * normal, axis=0, keepdims=True)
        ns[0, 1:2] += jnp.sum(grad_one, axis=0, keepdims=True)
        back_stats(grad_one, normal, gain_one, 3, h)
        swap_stats(3, h)
    for i, peer in enumerate((far(c), x_peer, diagonal)):
        pending.append(push(ns.at[0], nr.at[2 * x + r], NS + i, NS + i, peer))
    nr[2 * x + r] = ns[0]
    reduce_z(Q, steps[-1:])
    for i, from_slot in enumerate((2 * x + 1 - r, 2 - 2 * x + r, 3 - 2 * x - r)):
        arrived(nr.at[from_slot], NS + i)
    ns[1] = (nr[0] + nr[1]) + (nr[2] + nr[3])
    for step in range(1, nz):
        pending.append(
            push(ns.at[1], nr.at[4 + z], NS + 3 + step, NS + 3 + z, at_z((z + step) % nz))
        )
    nr[4 + z] = ns[1]
    for h in range(2):
        rows = parts[h]
        mgrad[rows] += finish_back(
            tmp[rows, 0:half], normal_one[rows], inverse[0, rows], gain_one, 3, h
        )
    to_hbm(mgrad, back_ref, 5)
    reduce_z(Q, [0])
    for p in (D, U, O, Q):
        reduce_end(p)
    for step in range(1, nz):
        zz = (z + step) % nz
        arrived(nr.at[4 + zz], NS + 3 + zz)
    total = nr[4]
    for zz in range(1, nz):
        total = total + nr[4 + zz]
    total_norm[...] = total * factor
    to_hbm(total_norm, norm_sum_ref, 6)

    for copy in pending:
        copy.wait_send()
    for flag, copy in guarded:

        @pl.when(flag)
        def _():
            copy.wait_send()

    for copy in writes:
        copy.wait()


def adam_values(weight, grad, first, second, decay):
    first_moment = beta_one * first + (1.0 - beta_one) * grad
    second_moment = beta_two * second + (1.0 - beta_two) * grad * grad
    step_size = (
        first_moment
        / (1.0 - beta_one**STEP)
        / (jnp.sqrt(second_moment / (1.0 - beta_two**STEP)) + adam_eps)
    )
    return weight - learn_rate * (step_size + decay * weight), first_moment, second_moment


def adam_kernel(*refs):
    ins, outs = refs[:17], refs[17:34]
    held, made, in_sem, out_sem = refs[34:51], refs[51:66], refs[66], refs[67]
    reads = [pltpu.make_async_copy(ins[i], held[i], in_sem.at[i]) for i in range(17)]
    order = (3, 4, 1, 2, 0)
    for i in order:
        for k in (i, 5 + i, 10 + i):
            reads[k].start()
    for k in (15, 16):
        reads[k].start()
    writes = []

    def write(src, dst, k):
        copy = pltpu.make_async_copy(src, outs[dst], out_sem.at[k])
        copy.start()
        writes.append(copy)

    for i in order:
        for k in (i, 5 + i, 10 + i):
            reads[k].wait()
        weight, moments = held[5 + i], held[10 + i]
        grad = held[i][...]
        if i == 0:
            grad = grad[0 : weight.shape[0]]
        grad = grad.reshape(weight.shape)
        made[i][...] = grad
        write(made[i], 2 + i, i)
        new, first, second = adam_values(
            weight[...], grad, moments[0], moments[1], decay_rate if i else 0.0
        )
        made[5 + i][...] = new
        write(made[5 + i], 7 + i, 5 + i)
        made[10 + i][0] = first
        made[10 + i][1] = second
        write(made[10 + i], 12 + i, 10 + i)
    for k in (15, 16):
        reads[k].wait()
        write(held[k], k - 15, k)
    for copy in writes:
        copy.wait()


def on_device_fused(
    block_in,
    upstream,
    norm_params,
    w_qkv,
    w_attn,
    w_up,
    w_down,
    mom_norm,
    mom_qkv,
    mom_attn,
    mom_up,
    mom_down,
):
    low = LOW
    ndp = lax.axis_size("dp")
    nz = ndp // low
    tokens, half = block_in.shape
    pairs = w_qkv.shape[1] // 2
    per = w_qkv.shape[2]
    groups = 3 * pairs
    width = 2 * per * ndp
    hidden_rows = w_up.shape[0]
    hidden = hidden_rows * ndp
    tiles = hidden // HIDDEN_TILE
    token_count = tokens * ndp * lax.axis_size("row")
    bf, f32 = jnp.bfloat16, jnp.float32

    def both(kind_of):
        return [kind_of(p) for p in range(4)]

    def piece(p):
        return ((groups, pairs)[p], 2 * per, half) if p < 2 else (hidden_rows, half)

    def whole(p, cols):
        return ((groups, pairs)[p], ndp, 2 * per, cols) if p < 2 else (hidden, cols)

    ins = (block_in, upstream, norm_params, w_qkv, w_attn, w_up, w_down)
    scratch = (
        [pltpu.VMEM(item.shape, f32) for item in ins]
        + both(lambda p: pltpu.VMEM(piece(p), bf))
        + both(lambda p: pltpu.VMEM(whole(p, 2 * half), bf))
        + [
            pltpu.VMEM((4, tokens, 128), f32),
            pltpu.VMEM((4, tokens, 128), f32),
            pltpu.VMEM((4, tokens, half), bf),
            pltpu.VMEM((4, tokens, 2 * half), bf),
            pltpu.VMEM((4, 2, tokens, half), bf),
            pltpu.VMEM((4, 2, tokens, half), bf),
            pltpu.VMEM((2, tokens, half), f32),
            pltpu.VMEM((tokens, 2 * half), f32),
            pltpu.VMEM((tokens, 3 * pairs * width), bf),
            pltpu.VMEM((tokens, pairs * width), bf),
            pltpu.VMEM((2 * pairs, tokens, 1), f32),
            pltpu.VMEM((tokens, hidden), bf),
            pltpu.VMEM((tokens, hidden), bf),
            pltpu.VMEM((tokens, half), f32),
            pltpu.VMEM((tokens, half), f32),
            pltpu.VMEM((tokens, half), f32),
            pltpu.VMEM((2, tokens, 1), f32),
            pltpu.VMEM((tokens, pairs * width), bf),
            pltpu.VMEM((tokens, 3 * pairs * width), bf),
            pltpu.VMEM((tokens, half), f32),
        ]
        + both(lambda p: pltpu.VMEM(whole(p, half), f32))
        + both(lambda p: pltpu.VMEM(whole(p, half), bf))
        + both(lambda p: pltpu.VMEM(whole(p, half), bf))
        + both(lambda p: pltpu.VMEM((nz,) + piece(p), bf))
        + both(lambda p: pltpu.VMEM((nz,) + piece(p), bf))
        + both(lambda p: pltpu.VMEM(piece(p), f32))
        + [
            pltpu.VMEM((8, half), f32),
            pltpu.VMEM((2, 8, half), f32),
            pltpu.VMEM((4 + nz, 8, half), f32),
            pltpu.SemaphoreType.DMA((51 + 21 * nz,)),
            pltpu.SemaphoreType.DMA((51 + 21 * nz,)),
            pltpu.SemaphoreType.DMA((26,)),
        ]
    )
    hbm = pl.BlockSpec(memory_space=pltpu.HBM)
    outs = (
        jax.ShapeDtypeStruct(block_in.shape, f32),
        jax.ShapeDtypeStruct(block_in.shape, f32),
        *both(lambda p: jax.ShapeDtypeStruct(piece(p), f32)),
        jax.ShapeDtypeStruct((8, half), f32),
    )
    block_out, input_grad, *totals = pl.pallas_call(
        functools.partial(step_kernel, nz, low, 1.0 / math.sqrt(token_count)),
        out_shape=outs,
        in_specs=[hbm] * 7,
        out_specs=[hbm] * len(outs),
        scratch_shapes=scratch,
        compiler_params=pltpu.CompilerParams(
            collective_id=0, has_side_effects=True, vmem_limit_bytes=VMEM_BYTES
        ),
    )(*ins)
    params = (norm_params, w_qkv, w_attn, w_up, w_down)
    moments = (mom_norm, mom_qkv, mom_attn, mom_up, mom_down)
    norm_total = totals.pop()
    operands = (norm_total, *totals, *params, *moments, block_out, input_grad)
    shapes = [
        jax.ShapeDtypeStruct(item.shape, f32)
        for item in (block_out, input_grad) + params * 2 + moments
    ]
    return pl.pallas_call(
        adam_kernel,
        out_shape=shapes,
        in_specs=[hbm] * len(operands),
        out_specs=[hbm] * len(shapes),
        scratch_shapes=[pltpu.VMEM(item.shape, f32) for item in operands]
        + [pltpu.VMEM(item.shape, f32) for item in shapes[2:]]
        + [pltpu.SemaphoreType.DMA((17,)), pltpu.SemaphoreType.DMA((17,))],
        compiler_params=pltpu.CompilerParams(vmem_limit_bytes=VMEM_BYTES),
    )(*operands)


def fits(block_in, w_qkv, w_up, ndp, nrow, ncol):
    return (
        nrow == 2
        and ncol == 2
        and ndp == 4 * LOW
        and block_in.shape[0] == SEQ
        and w_qkv.shape[1] % 2 == 0
        and w_qkv.shape[2] == 8
        and (w_up.shape[0] * ndp) % HIDDEN_TILE == 0
        and w_up.shape[0] % 16 == 0
    )


def run_step(*args):
    sizes = [lax.axis_size(name) for name in ("dp", "row", "col")]
    if fits(args[0], args[3], args[5], *sizes):
        return on_device_fused(*args)
    return on_device(*args)


def solution(mesh):
    in_specs = (
        P(("dp", "row"), "col"),
        P(("dp", "row"), "col"),
        P(None, "col"),
        P(None, "row", "dp", "col"),
        P("row", "dp", "col"),
        P(("dp", "row"), "col"),
        P(("dp", "row"), "col"),
        P(None, None, "col"),
        P(None, None, "row", "dp", "col"),
        P(None, "row", "dp", "col"),
        P(None, ("dp", "row"), "col"),
        P(None, ("dp", "row"), "col"),
    )
    out_specs = (
        P(("dp", "row"), "col"),
        P(("dp", "row"), "col"),
        P(None, "col"),
        P(None, "row", "dp", "col"),
        P("row", "dp", "col"),
        P(("dp", "row"), "col"),
        P(("dp", "row"), "col"),
        P(None, "col"),
        P(None, "row", "dp", "col"),
        P("row", "dp", "col"),
        P(("dp", "row"), "col"),
        P(("dp", "row"), "col"),
        P(None, None, "col"),
        P(None, None, "row", "dp", "col"),
        P(None, "row", "dp", "col"),
        P(None, ("dp", "row"), "col"),
        P(None, ("dp", "row"), "col"),
    )
    return jax.shard_map(
        run_step, mesh=mesh, in_specs=in_specs, out_specs=out_specs, check_vma=False
    )
```
